32 devices in a mesh: seq: 8 (over z, y), head: 4 (over x, core).
Axes of the slice: x: 2, y: 2, z: 4, core: 2. Of those that a mesh axis runs over, the one named last changes fastest.
Arguments:
- inputs: bfloat16 [2, 4096, 1024], P(None, ('seq', 'head')), may hold values from -6 to 6
- attn_gain: float32 [1024], replicated, may hold values from 0.5 to 1.5
- mixer_weights: bfloat16 [4, 1024, 1024], P(None, None, 'head'), may hold values from -0.1875 to 0.1875
- beta_weight: bfloat16 [1024, 8], P(None, 'head'), may hold values from -0.1875 to 0.1875
- filter_weights: bfloat16 [3, 4, 1024], P(None, None, 'head'), may hold values from -3 to 3
- out_gain: float32 [128], replicated, may hold values from 0.5 to 1.5
- dense_gain: float32 [1024], replicated, may hold values from 0.5 to 1.5
- dense_weights: bfloat16 [3, 1024, 2816], P(None, 'seq', 'head'), may hold values from -0.1875 to 0.1875
- seq_offsets: int32 [2, 3], replicated, may hold values from 0 to 3072, as said below
- seq_lengths: int32 [2, 3], replicated, may hold values from 961 to 2048, as said below
- out_grad: bfloat16 [2, 4096, 1024], P(None, ('seq', 'head')), may hold values from -6 to 6
Outputs:
- output: bfloat16 [2, 4096, 1024], P(None, ('seq', 'head'))
- input_grad: float32 [2, 4096, 1024], P(None, ('seq', 'head'))
- attn_gain_grad: float32 [1024], replicated
- mixer_weights_grad: float32 [4, 1024, 1024], P(None, None, 'head')
- beta_weight_grad: float32 [1024, 8], P(None, 'head')
- filter_weights_grad: float32 [3, 4, 1024], P(None, None, 'head')
- out_gain_grad: float32 [128], replicated
- dense_gain_grad: float32 [1024], replicated
- dense_weights_grad: float32 [3, 1024, 2816], P(None, 'seq', 'head')
The draws below stay inside these ranges and needn't reach their ends.
Inputs may be any that keep to these rules, and one draw needn't show every extreme that they name: seq_offsets[m] starts at 0, rises by 1024 or more from one slot to the next, holds multiples of 64, and the last slot ends at token 4096. `seq_lengths`: each sequence fills its slot from the slot's first token and leaves fewer than 64 padding tokens at the slot's end.
All inputs are finite; a program needn't handle non-finite values.
Results may differ from the reference program's by a relative error of at most 0.02.
Values may be sent and summed in bfloat16 or wider, within the bound.
A program may use at most 192 MiB of HBM per device.

```python
import jax
import jax.numpy as jnp
from jax import lax

D = 1024
HEADS = 8
HEAD_DIM = 128
FF = 2816
CONV = 4
STRETCH = 64
NSEQ = 3
MIN_LEN = 1024
MB = 2
TOKENS = 4096


def slot_starts(base_key):
    free_stretches = (TOKENS - NSEQ * MIN_LEN) // STRETCH
    cut_points = jax.random.randint(base_key, (MB, NSEQ - 1), 0, free_stretches + 1)
    cut_points = jnp.sort(cut_points, axis=1)
    cut_points = cut_points.at[0].set(free_stretches)
    slot_index = jnp.arange(1, NSEQ, dtype=jnp.int32)
    later_starts = cut_points * STRETCH + slot_index[None, :] * MIN_LEN
    return jnp.concatenate([jnp.zeros((MB, 1), jnp.int32), later_starts.astype(jnp.int32)], axis=1)


def draw_seq_offsets(key, part):
    return slot_starts(jax.random.fold_in(key, 11))


def draw_seq_lengths(key, part):
    starts_all = slot_starts(jax.random.fold_in(key, 11))
    ends_all = jnp.concatenate([starts_all[:, 1:], jnp.full((MB, 1), TOKENS, jnp.int32)], axis=1)
    padding = jax.random.randint(jax.random.fold_in(key, 12), (MB, NSEQ), 0, STRETCH)
    padding = padding.at[0, 0].set(0).at[0, 1].set(STRETCH - 1)
    return (ends_all - starts_all - padding).astype(jnp.int32)


def levels(key, extent, cuts, smallest, largest):
    level, own = 1.0, jax.random.fold_in(key, 6)
    for dim, shards_of in cuts:
        steps = jnp.exp(jax.random.uniform(jax.random.fold_in(own, dim), (shards_of,), jnp.float32, smallest / len(cuts), largest / len(cuts)))
        level = level * jnp.repeat(steps, extent[dim] // shards_of).reshape([-1 if axis == dim else 1 for axis in range(len(extent))])
    return level


def centred(stream_key, extent, scale, reach, pieces=(), held_as=jnp.bfloat16):
    values = jax.random.normal(stream_key, extent, jnp.float32) * scale
    if len(pieces) > 0:
        values = levels(stream_key, extent, pieces, -0.22, 0.18) * values
    return jnp.clip(values, min=-reach, max=reach).astype(held_as)


def setup_inputs(seed: int = 0) -> dict:
    key_of = jax.random.split(jax.random.key(seed), 12)
    inputs = centred(key_of[0], (MB, TOKENS, D), 1.0, 6.0, ((1, 32),))
    attn_gain = jnp.clip(1.0 + 0.1 * jax.random.normal(key_of[1], (D,), jnp.float32), 0.5, 1.5)
    mixer_weights = centred(key_of[2], (4, D, D), D ** -0.5, 0.1875, ((2, 4),))
    beta_weight = centred(key_of[3], (D, HEADS), D ** -0.5, 0.1875, ((1, 4),))
    filter_weights = centred(key_of[4], (3, CONV, D), CONV ** -0.5, 3.0, ((2, 4),))
    out_gain = jnp.clip(1.0 + 0.1 * jax.random.normal(key_of[5], (HEAD_DIM,), jnp.float32), 0.5, 1.5)
    dense_gain = jnp.clip(1.0 + 0.1 * jax.random.normal(key_of[6], (D,), jnp.float32), 0.5, 1.5)
    dense_weights = centred(key_of[7], (3, D, FF), D ** -0.5, 0.1875, ((1, 8), (2, 4)))
    seq_offsets = draw_seq_offsets(jax.random.fold_in(key_of[11], 71), 0)
    seq_lengths = draw_seq_lengths(jax.random.fold_in(key_of[11], 71), 0)
    out_grad = centred(key_of[10], (MB, TOKENS, D), 1.0, 6.0, ((1, 32),))
    return {"inputs": inputs, "attn_gain": attn_gain, "mixer_weights": mixer_weights, "beta_weight": beta_weight, "filter_weights": filter_weights, "out_gain": out_gain, "dense_gain": dense_gain, "dense_weights": dense_weights, "seq_offsets": seq_offsets, "seq_lengths": seq_lengths, "out_grad": out_grad}


norm_eps = 1e-06
highest_precision = lax.Precision.HIGHEST

@jax.custom_vjp
def low(v):
    return lax.optimization_barrier(v.astype(jnp.bfloat16)).astype(jnp.float32)

@jax.custom_vjp
def low_back(v):
    return v

def low_keep(v):
    return (low(v), None)

def low_pass(kept, grad):
    return (grad,)

def back_keep(v):
    return (v, None)

def back_low(kept, grad):
    return (low(grad),)
low.defvjp(low_keep, low_pass)
low_back.defvjp(back_keep, back_low)

def matmul(left_side, right_side):
    return jnp.dot(left_side, right_side, precision=highest_precision)

def rms_scale(values, gain_vec):
    return values * lax.rsqrt(lax.optimization_barrier(jnp.mean(values * values, axis=-1, keepdims=True)) + norm_eps) * gain_vec

def unit_rows(values):
    return values * lax.rsqrt(lax.optimization_barrier(jnp.sum(values * values, axis=-1, keepdims=True)) + norm_eps)

def solve_one(system_one, right_one):
    return jax.scipy.linalg.solve_triangular(system_one, right_one, lower=True, unit_diagonal=True)

def stretch_solve(key_row_matrix, values, rate_rows):
    inner_prod = jnp.einsum('...ck,...dk->...cd', key_row_matrix, key_row_matrix, precision=highest_precision)
    lower_part = jnp.tril(rate_rows[..., :, None] * inner_prod, -1)
    system = lower_part + jnp.eye(key_row_matrix.shape[-2], dtype=key_row_matrix.dtype)
    right_side = rate_rows[..., :, None] * jnp.concatenate([key_row_matrix, values], axis=-1)
    flat_system = system.reshape((-1,) + system.shape[-2:])
    flat_right = right_side.reshape((-1,) + right_side.shape[-2:])
    solved = jax.vmap(solve_one)(flat_system, flat_right).reshape(right_side.shape)
    key_width = key_row_matrix.shape[-1]
    return (solved[..., :key_width], solved[..., key_width:])

def stretch_step(state_matrix, inputs):
    query_rows, key_row_matrix, values, rate_rows, keep_flag = inputs
    write_rows, update_rows = stretch_solve(key_row_matrix, values, rate_rows)
    state_matrix = state_matrix * keep_flag
    fresh_value_rows = update_rows - jnp.einsum('bdw,bws->bds', write_rows, state_matrix, precision=highest_precision)
    score_matrix = jnp.tril(jnp.einsum('hck,hdk->hcd', query_rows, key_row_matrix, precision=highest_precision))
    output_rows = jnp.einsum('bdw,bws->bds', query_rows, state_matrix, precision=highest_precision) + jnp.einsum('tbg,tgx->tbx', score_matrix, fresh_value_rows, precision=highest_precision)
    state_matrix = state_matrix + jnp.einsum('bua,buq->baq', key_row_matrix, fresh_value_rows, precision=highest_precision)
    return (state_matrix, output_rows)

def short_filter(values, filter_taps, offset_rel):
    summed = jnp.zeros_like(values)
    for lag_step in range(CONV):
        moved = jnp.pad(values, ((lag_step, 0), (0, 0)))[:TOKENS]
        summed = summed + filter_taps[lag_step] * moved * (offset_rel >= lag_step).astype(jnp.float32)[:, None]
    return summed

def heads_first(array_in):
    blocks = TOKENS // STRETCH
    return array_in.reshape(blocks, STRETCH, HEADS, HEAD_DIM).transpose(0, 2, 1, 3)

def block_forward(inputs_now, weights, offsets_now, lengths_now):
    attn_gain, mixer_weights, beta_weight, filter_weights, out_gain, dense_gain, dense_weights = weights
    positions = jnp.arange(TOKENS, dtype=jnp.int32)
    seq_index = lax.optimization_barrier(jnp.sum((offsets_now[None, :] <= positions[:, None]).astype(jnp.int32), axis=1)) - 1
    starts_now = jnp.take(offsets_now, seq_index)
    offset_rel = positions - starts_now
    valid_rows = (offset_rel < jnp.take(lengths_now, seq_index)).astype(jnp.float32)
    normed = low(rms_scale(inputs_now, attn_gain))
    projected = [low_back(low(matmul(normed, mixer_weights[member]))) for member in range(3)]
    rates_raw = matmul(normed, beta_weight)
    active = [jax.nn.silu(short_filter(projected[member], filter_weights[member], offset_rel)) for member in range(3)]
    query_rows = unit_rows(active[0].reshape(TOKENS, HEADS, HEAD_DIM))
    key_row_matrix = unit_rows(active[1].reshape(TOKENS, HEADS, HEAD_DIM))
    values = active[2].reshape(TOKENS, HEADS, HEAD_DIM)
    rate_rows = jax.nn.sigmoid(rates_raw) * valid_rows[:, None]
    blocks = TOKENS // STRETCH
    rate_blocks = rate_rows.reshape(blocks, STRETCH, HEADS).transpose(0, 2, 1)
    keep_flags = (offset_rel[::STRETCH] != 0).astype(jnp.float32)
    zero_state = jnp.zeros((HEADS, HEAD_DIM, HEAD_DIM), jnp.float32)
    mixed = lax.scan(jax.checkpoint(stretch_step), zero_state, (heads_first(query_rows), heads_first(key_row_matrix), heads_first(values), rate_blocks, keep_flags))[1]
    mixed = mixed.transpose(0, 2, 1, 3).reshape(TOKENS, HEADS, HEAD_DIM)
    head_out = low(rms_scale(mixed, out_gain)).reshape(TOKENS, D)
    resid = inputs_now + low_back(matmul(head_out, mixer_weights[3].T))
    dense_in = low(rms_scale(resid, dense_gain))
    gate_vals = low_back(matmul(dense_in, dense_weights[0]))
    up_vals = low_back(matmul(dense_in, dense_weights[1]))
    hidden = low(jax.nn.silu(gate_vals) * up_vals)
    return resid + matmul(hidden, dense_weights[2].T)

def reference(inputs, attn_gain, mixer_weights, beta_weight, filter_weights, out_gain, dense_gain, dense_weights, seq_offsets, seq_lengths, out_grad):
    params = tuple((member.astype(jnp.float32) for member in (attn_gain, mixer_weights, beta_weight, filter_weights, out_gain, dense_gain, dense_weights)))
    results = []
    input_grads = []
    totals = None
    for micro_batch in range(MB):
        offsets_now = seq_offsets[micro_batch]
        lengths_now = seq_lengths[micro_batch]

        def forward(inputs_now, weights):
            return block_forward(inputs_now, weights, offsets_now, lengths_now)
        result, pullback = jax.vjp(forward, inputs[micro_batch].astype(jnp.float32), params)
        grads = pullback(out_grad[micro_batch].astype(jnp.float32))
        results.append(result.astype(jnp.bfloat16))
        input_grads.append(grads[0])
        if totals is None:
            totals = grads[1]
        else:
            totals = jax.tree.map(jnp.add, totals, grads[1])
    return (jnp.stack(results), jnp.stack(input_grads), totals[0], totals[1], totals[2], totals[3], totals[4], totals[5], totals[6])
```

```python
import functools

import jax
import jax.numpy as jnp
from jax import lax
from jax.experimental import pallas as pl
from jax.experimental.pallas import tpu as pltpu
from jax.sharding import PartitionSpec as P

HEAD_DIM = 128
CONV = 4
CHUNK = 128
HALO = 16
RIM = 8
EPS = 1e-06
F32 = jnp.float32
BF16 = jnp.bfloat16
VMEM_LIMIT = 56 * 1024 * 1024


def mm(a, b, ca=1, cb=0):
    return lax.dot_general(
        a.astype(BF16), b.astype(BF16), (((ca,), (cb,)), ((), ())), preferred_element_type=F32
    )


def split(a):
    high = a.astype(BF16)
    return high, (a - high.astype(F32)).astype(BF16)


def mm3(a, b, ca=1, cb=0):
    ah, al = split(a)
    bh, bl = split(b)
    return mm(ah, bh, ca, cb) + (mm(ah, bl, ca, cb) + mm(al, bh, ca, cb))


def sigmoid(v):
    return 1.0 / (1.0 + jnp.exp(-v))


def row_info(off_ref, len_ref, m, base, rows):
    t = base + lax.broadcasted_iota(jnp.int32, (rows, 1), 0)
    start = jnp.zeros_like(t)
    length = jnp.zeros_like(t)
    for i in range(off_ref.shape[1]):
        inside = t >= off_ref[m, i]
        start = jnp.where(inside, off_ref[m, i], start)
        length = jnp.where(inside, len_ref[m, i], length)
    rel = t - start
    return rel, (rel < length).astype(F32)


def chunk_masks(rel):
    n = rel.shape[0]
    i = lax.broadcasted_iota(jnp.int32, (n, n), 0)
    j = lax.broadcasted_iota(jnp.int32, (n, n), 1)
    same = rel >= i - j
    strict = jnp.logical_and(same, i > j)
    incl = jnp.logical_and(same, i >= j)
    col = lax.broadcasted_iota(jnp.int32, (n, 1), 0)
    sees = (rel > col).astype(F32)
    last = rel[n - 1 : n, :]
    stays = ((n - 1 - col) <= last).astype(F32)
    keep = (last > n - 1).astype(F32)
    return strict, incl, sees, stays, keep


def unit_lower_inverse(a_list):
    n = a_list[0].shape[0]
    i = lax.broadcasted_iota(jnp.int32, (n, n), 0)
    j = lax.broadcasted_iota(jnp.int32, (n, n), 1)
    eye = (i == j).astype(F32)
    size = 1
    inv_list = [eye for _ in a_list]
    while size < n:
        pair = jnp.logical_and(i // size == j // size + 1, (i // size) % 2 == 1)
        below = [jnp.where(pair, a, 0.0) for a in a_list]
        if size == 1:
            inv_list = [eye - b for b in below]
        else:
            half = [mm3(b, inv) for b, inv in zip(below, inv_list)]
            inv_list = [inv - mm3(inv, h) for inv, h in zip(inv_list, half)]
        size *= 2
    return inv_list


def lagged(ext, lag, rows):
    moved = pltpu.roll(ext, lag, 0) if lag else ext
    return moved[HALO : HALO + rows]


def lag_masks(rel):
    return [None] + [(rel >= lag).astype(F32) for lag in range(1, CONV)]


def filtered(ext, taps, masks, rows):
    total = None
    for lag in range(CONV):
        term = taps[lag : lag + 1, :] * lagged(ext, lag, rows)
        if masks[lag] is not None:
            term = term * masks[lag]
        total = term if total is None else total + term
    return total


def mix_fwd_body(
    off_ref, len_ref, base_ref, x_ref, w_ref, beta_ref, taps_ref,
    pq_ref, pk_ref, pv_ref, rate_ref, ps_ref, oloc_ref, phi_ref, psi_ref, m_ref, inv_ref, wr_ref, up_ref, ts_ref,
):
    mb = pl.program_id(0)
    head = pl.program_id(1)
    rows = x_ref.shape[1] - HALO
    rel, valid = row_info(off_ref, len_ref, mb, base_ref[0], rows)
    x = x_ref[0]
    masks = lag_masks(rel)
    acts = []
    for member, out in enumerate((pq_ref, pk_ref, pv_ref)):
        proj = mm(x, w_ref[member]).astype(BF16)
        out[0] = proj
        filt = filtered(proj.astype(F32), taps_ref[member], masks, rows)
        acts.append(filt * sigmoid(filt))
    query, key, value = acts
    query = query * lax.rsqrt(jnp.sum(query * query, axis=-1, keepdims=True) + EPS)
    key = key * lax.rsqrt(jnp.sum(key * key, axis=-1, keepdims=True) + EPS)
    raw_all = mm(x, beta_ref[...])[HALO:]
    lane = lax.broadcasted_iota(jnp.int32, raw_all.shape, 1)
    raw = jnp.sum(jnp.where(lane == head, raw_all, 0.0), axis=-1, keepdims=True)
    rate_ref[0, 0] = raw
    rate = sigmoid(raw) * valid
    spans = [slice(c * CHUNK, (c + 1) * CHUNK) for c in range(rows // CHUNK)]
    all_masks = [chunk_masks(rel[s]) for s in spans]
    systems, scores = [], []
    for s, (strict, incl, _, _, _) in zip(spans, all_masks):
        both = mm(jnp.concatenate([query[s], key[s]], axis=0), key[s], 1, 1)
        scores.append(jnp.where(incl, both[:CHUNK], 0.0))
        systems.append(jnp.where(strict, rate[s] * both[CHUNK:], 0.0))
    inverses = unit_lower_inverse(systems)
    i = lax.broadcasted_iota(jnp.int32, (HEAD_DIM, HEAD_DIM), 0)
    j = lax.broadcasted_iota(jnp.int32, (HEAD_DIM, HEAD_DIM), 1)
    eye = (i == j).astype(F32)
    phis, psis, ps, olocs = [], [], [], []
    for s, masks_c, inv, score in zip(spans, all_masks, inverses, scores):
        _, _, sees, stays, keep = masks_c
        right = rate[s] * jnp.concatenate([sees * key[s], value[s]], axis=1)
        solved = mm(inv, right)
        write, update = solved[:, :HEAD_DIM], solved[:, HEAD_DIM:]
        moved = mm(stays * key[s], solved, 0, 0)
        phi = keep * eye - moved[:, :HEAD_DIM]
        psi = moved[:, HEAD_DIM:]
        scored = mm(score, solved)
        p = sees * query[s] - scored[:, :HEAD_DIM]
        m_ref[0, 0, s] = score.astype(BF16)
        inv_ref[0, 0, s] = inv.astype(BF16)
        wr_ref[0, 0, s] = write.astype(BF16)
        up_ref[0, 0, s] = update
        ps_ref[0, 0, s] = p.astype(BF16)
        oloc_ref[0, 0, s] = scored[:, HEAD_DIM:]
        phi_ref[0, 0, s] = phi
        psi_ref[0, 0, s] = psi
        phis.append(phi)
        psis.append(psi)
    trans, state = phis[0], psis[0]
    for phi, psi in zip(phis[1:], psis[1:]):
        both = mm3(phi, jnp.concatenate([trans, state], axis=1))
        trans = both[:, :HEAD_DIM]
        state = both[:, HEAD_DIM:] + psi
    ts_ref[0, 0, 0] = trans.astype(BF16)
    ts_ref[1, 0, 0] = state.astype(BF16)


def smem_spec():
    return pl.BlockSpec(memory_space=pltpu.SMEM)


def params(count):
    return pltpu.CompilerParams(
        dimension_semantics=("arbitrary",) * count, vmem_limit_bytes=VMEM_LIMIT
    )


def mix_fwd(offsets, lengths, base, x_ext, mixer_weights, beta_weight, taps):
    count, ext_rows, width = x_ext.shape
    rows = ext_rows - HALO
    heads = beta_weight.shape[1]
    per_head = pl.BlockSpec((1, 1, rows, HEAD_DIM), lambda m, h: (m, h, 0, 0))
    proj_spec = pl.BlockSpec((1, ext_rows, HEAD_DIM), lambda m, h: (m, 0, h))
    proj_shape = jax.ShapeDtypeStruct((count, ext_rows, heads * HEAD_DIM), BF16)

    def big(kind):
        return jax.ShapeDtypeStruct((count, heads, rows, HEAD_DIM), kind)

    return pl.pallas_call(
        mix_fwd_body,
        grid=(count, heads),
        in_specs=[
            smem_spec(), smem_spec(), smem_spec(),
            pl.BlockSpec((1, ext_rows, width), lambda m, h: (m, 0, 0)),
            pl.BlockSpec((3, width, HEAD_DIM), lambda m, h: (0, 0, h)),
            pl.BlockSpec(beta_weight.shape, lambda m, h: (0, 0)),
            pl.BlockSpec((3, CONV, HEAD_DIM), lambda m, h: (0, 0, h)),
        ],
        out_specs=[proj_spec] * 3
        + [pl.BlockSpec((1, 1, rows, 1), lambda m, h: (m, h, 0, 0))]
        + [per_head] * 8
        + [pl.BlockSpec((2, 1, 1, HEAD_DIM, HEAD_DIM), lambda m, h: (0, m, h, 0, 0))],
        out_shape=[proj_shape] * 3
        + [jax.ShapeDtypeStruct((count, heads, rows, 1), F32)]
        + [big(BF16), big(F32), big(F32), big(F32), big(BF16), big(BF16), big(BF16), big(F32)]
        + [jax.ShapeDtypeStruct((2, count, heads, HEAD_DIM, HEAD_DIM), BF16)],
        compiler_params=params(2),
        name="mix_fwd",
    )(offsets, lengths, base, x_ext, mixer_weights, beta_weight, taps)


def mix_out_body(state_ref, ps_ref, oloc_ref, phi_ref, psi_ref, gain_ref, w_ref, start_ref, mixed_ref, head_ref, part_ref):
    heads = ps_ref.shape[1]
    rows = ps_ref.shape[2]
    gain = gain_ref[...]
    states = [state_ref[0, h] for h in range(heads)]
    for c in range(rows // CHUNK):
        s = slice(c * CHUNK, (c + 1) * CHUNK)
        for h in range(heads):
            state = states[h]
            start_ref[0, h, s] = state.astype(BF16)
            mixed = oloc_ref[0, h, s] + mm(ps_ref[0, h, s], state)
            mixed_ref[0, h, s] = mixed
            normed = mixed * lax.rsqrt(jnp.mean(mixed * mixed, axis=-1, keepdims=True) + EPS) * gain
            head_ref[0, s, h * HEAD_DIM : (h + 1) * HEAD_DIM] = normed.astype(BF16)
            states[h] = mm3(phi_ref[0, h, s], state) + psi_ref[0, h, s]
    part_ref[0] = mm(head_ref[0], w_ref[0], 1, 1).astype(BF16)


def mix_out(state_in, ps, oloc, phi, psi, out_gain, mixer_weights):
    count, heads, rows, _ = ps.shape
    width = mixer_weights.shape[1]
    head_width = mixer_weights.shape[2]
    per_mb = pl.BlockSpec((1, heads, rows, HEAD_DIM), lambda m: (m, 0, 0, 0))
    return pl.pallas_call(
        mix_out_body,
        grid=(count,),
        in_specs=[
            pl.BlockSpec((1, heads, HEAD_DIM, HEAD_DIM), lambda m: (m, 0, 0, 0)),
            per_mb, per_mb, per_mb, per_mb,
            pl.BlockSpec((1, HEAD_DIM), lambda m: (0, 0)),
            pl.BlockSpec((1, width, head_width), lambda m: (3, 0, 0)),
        ],
        out_specs=[
            per_mb, per_mb,
            pl.BlockSpec((1, rows, head_width), lambda m: (m, 0, 0)),
            pl.BlockSpec((1, rows, width), lambda m: (m, 0, 0)),
        ],
        out_shape=[
            jax.ShapeDtypeStruct(ps.shape, BF16),
            jax.ShapeDtypeStruct(ps.shape, F32),
            jax.ShapeDtypeStruct((count, rows, head_width), BF16),
            jax.ShapeDtypeStruct((count, rows, width), BF16),
        ],
        compiler_params=params(1),
        name="mix_out",
    )(state_in, ps, oloc, phi, psi, out_gain, mixer_weights)


def dense_body(x_ref, g_ref, w_ref, down_ref, gin_ref, grad_ref, acc_ref):
    step = pl.program_id(0)
    x = x_ref[...]
    g = g_ref[...]
    gate = mm(x, w_ref[0])
    up = mm(x, w_ref[1])
    grad_hidden = mm(g, w_ref[2])
    sg = sigmoid(gate)
    silu = gate * sg
    hidden = (silu * up).astype(BF16)
    grad_gate = (grad_hidden * up * (sg * (1.0 + gate * (1.0 - sg)))).astype(BF16)
    grad_up = (grad_hidden * silu).astype(BF16)
    down_ref[...] = mm(hidden, w_ref[2], 1, 1).astype(BF16)
    gin_ref[...] = (mm(grad_gate, w_ref[0], 1, 1) + mm(grad_up, w_ref[1], 1, 1)).astype(BF16)

    @pl.when(step == 0)
    def _():
        acc_ref[0] = mm(x, grad_gate, 0, 0)
        acc_ref[1] = mm(x, grad_up, 0, 0)
        acc_ref[2] = mm(g, hidden, 0, 0)

    @pl.when(step > 0)
    def _():
        acc_ref[0] += mm(x, grad_gate, 0, 0)
        acc_ref[1] += mm(x, grad_up, 0, 0)
        acc_ref[2] += mm(g, hidden, 0, 0)

    @pl.when(step == pl.num_programs(0) - 1)
    def _():
        grad_ref[...] = acc_ref[...].astype(BF16)


def dense(dense_in, grad_top, weights):
    rows, width = dense_in.shape
    hidden = weights.shape[2]
    tile = 256
    row_spec = pl.BlockSpec((tile, width), lambda i: (i, 0))
    whole = pl.BlockSpec((3, width, hidden), lambda i: (0, 0, 0), pipeline_mode=pl.Buffered(1))
    return pl.pallas_call(
        dense_body,
        grid=(rows // tile,),
        in_specs=[row_spec, row_spec, whole],
        out_specs=[row_spec, row_spec, whole],
        out_shape=[
            jax.ShapeDtypeStruct((rows, width), BF16),
            jax.ShapeDtypeStruct((rows, width), BF16),
            jax.ShapeDtypeStruct((3, width, hidden), BF16),
        ],
        scratch_shapes=[pltpu.VMEM((3, width, hidden), F32)],
        compiler_params=params(1),
        name="dense",
    )(dense_in, grad_top, weights)


def mix_back_body(grad_ref, w_ref, mixed_ref, gain_ref, ps_ref, phi_ref, dout_ref, gain_grad_ref, dstate_ref):
    heads = ps_ref.shape[1]
    rows = ps_ref.shape[2]
    gain = gain_ref[...]
    grad_head = mm(grad_ref[0], w_ref[0])
    gain_grad = jnp.zeros((1, HEAD_DIM), F32)
    douts = []
    for h in range(heads):
        e = grad_head[:, h * HEAD_DIM : (h + 1) * HEAD_DIM]
        v = mixed_ref[0, h]
        r = lax.rsqrt(jnp.mean(v * v, axis=-1, keepdims=True) + EPS)
        weighted = e * gain
        dout = r * weighted - v * (r * r * r * jnp.mean(weighted * v, axis=-1, keepdims=True))
        gain_grad += jnp.sum(e * v * r, axis=0, keepdims=True)
        dout = dout.astype(BF16)
        dout_ref[0, h] = dout
        douts.append(dout)
    states = [None] * heads
    for c in reversed(range(rows // CHUNK)):
        s = slice(c * CHUNK, (c + 1) * CHUNK)
        for h in range(heads):
            new = mm(ps_ref[0, h, s], douts[h][s], 0, 0)
            if states[h] is not None:
                new += mm3(phi_ref[0, h, s], states[h], 0, 0)
            states[h] = new
    for h in range(heads):
        dstate_ref[0, h] = states[h].astype(BF16)

    @pl.when(pl.program_id(0) == 0)
    def _():
        gain_grad_ref[...] = gain_grad

    @pl.when(pl.program_id(0) > 0)
    def _():
        gain_grad_ref[...] += gain_grad


def mix_back(grad_attn, mixer_weights, mixed, out_gain, ps, phi):
    count, heads, rows, _ = ps.shape
    width = mixer_weights.shape[1]
    head_width = mixer_weights.shape[2]
    per_mb = pl.BlockSpec((1, heads, rows, HEAD_DIM), lambda m: (m, 0, 0, 0))
    return pl.pallas_call(
        mix_back_body,
        grid=(count,),
        in_specs=[
            pl.BlockSpec((1, rows, width), lambda m: (m, 0, 0)),
            pl.BlockSpec((1, width, head_width), lambda m: (3, 0, 0)),
            per_mb,
            pl.BlockSpec((1, HEAD_DIM), lambda m: (0, 0)),
            per_mb, per_mb,
        ],
        out_specs=[
            per_mb,
            pl.BlockSpec((1, HEAD_DIM), lambda m: (0, 0)),
            pl.BlockSpec((1, heads, HEAD_DIM, HEAD_DIM), lambda m: (m, 0, 0, 0)),
        ],
        out_shape=[
            jax.ShapeDtypeStruct(ps.shape, BF16),
            jax.ShapeDtypeStruct((1, HEAD_DIM), F32),
            jax.ShapeDtypeStruct((count, heads, HEAD_DIM, HEAD_DIM), BF16),
        ],
        compiler_params=params(1),
        name="mix_back",
    )(grad_attn, mixer_weights, mixed, out_gain, ps, phi)


def mix_grad_body(
    off_ref, len_ref, base_ref, pq_ref, pk_ref, pv_ref, rate_ref, taps_ref, dend_ref, dout_ref, start_ref, ps_ref, phi_ref,
    m_ref, inv_ref, wr_ref, up_ref,
    gq_ref, gk_ref, gv_ref, tail_ref, rim_ref, grate_ref, gtaps_ref,
):
    mb = pl.program_id(1)
    rows = rate_ref.shape[2]
    rel, valid = row_info(off_ref, len_ref, mb, base_ref[0], rows)
    masks = lag_masks(rel)
    projs, filts, sigs, acts = [], [], [], []
    for member, ref in enumerate((pq_ref, pk_ref, pv_ref)):
        proj = ref[0].astype(F32)
        filt = filtered(proj, taps_ref[member], masks, rows)
        sg = sigmoid(filt)
        projs.append(proj)
        filts.append(filt)
        sigs.append(sg)
        acts.append(filt * sg)
    rq = lax.rsqrt(jnp.sum(acts[0] * acts[0], axis=-1, keepdims=True) + EPS)
    rk = lax.rsqrt(jnp.sum(acts[1] * acts[1], axis=-1, keepdims=True) + EPS)
    query = acts[0] * rq
    key = acts[1] * rk
    value = acts[2]
    sig_rate = sigmoid(rate_ref[0, 0])
    rate = sig_rate * valid
    dstate = dend_ref[0, 0]
    spans = [slice(c * CHUNK, (c + 1) * CHUNK) for c in range(rows // CHUNK)]
    dstates = [None] * len(spans)
    for c in reversed(range(len(spans))):
        s = spans[c]
        dstates[c] = dstate
        if c:
            dstate = mm3(phi_ref[0, 0, s], dstate, 0, 0) + mm(ps_ref[0, 0, s], dout_ref[0, 0, s], 0, 0)
    dqs, dks, dvs, drates = [], [], [], []
    for c, s in enumerate(spans):
        strict, incl, sees, stays, _ = chunk_masks(rel[s])
        q, k, v, b = query[s], key[s], value[s], rate[s]
        dout = dout_ref[0, 0, s]
        start = start_ref[0, 0, s]
        fresh = up_ref[0, 0, s] - mm(wr_ref[0, 0, s], start)
        dfresh = mm(m_ref[0, 0, s], dout, 0, 0) + mm(stays * k, dstates[c])
        e = mm(inv_ref[0, 0, s], dfresh, 0, 0)
        left = jnp.concatenate([dout, e.astype(BF16)], axis=0)
        right = jnp.concatenate([fresh.astype(BF16), start], axis=0)
        outer = mm(left, right, 1, 1)
        dscore = jnp.where(incl, outer[:CHUNK, :CHUNK], 0.0)
        dsystem = jnp.where(strict, -outer[CHUNK:, :CHUNK], 0.0)
        grads = jnp.concatenate([dscore, dsystem], axis=0).astype(BF16)
        byk = mm(grads, k)
        z = byk[CHUNK:] - sees * outer[CHUNK:, CHUNK:]
        dqs.append(sees * outer[:CHUNK, CHUNK:] + byk[:CHUNK])
        dk = mm(grads, jnp.concatenate([q, b * k], axis=0), 0, 0)
        dks.append(dk + stays * mm(fresh, dstates[c], 1, 1) + b * z)
        dvs.append(b * e)
        drates.append(jnp.sum(e * v + k * z, axis=-1, keepdims=True))
    dq = jnp.concatenate(dqs, axis=0)
    dk = jnp.concatenate(dks, axis=0)
    dv = jnp.concatenate(dvs, axis=0)
    drate = jnp.concatenate(drates, axis=0)
    grate_ref[0, 0] = drate * valid * sig_rate * (1.0 - sig_rate)
    dacts = [
        rq * dq - acts[0] * (rq * rq * rq * jnp.sum(dq * acts[0], axis=-1, keepdims=True)),
        rk * dk - acts[1] * (rk * rk * rk * jnp.sum(dk * acts[1], axis=-1, keepdims=True)),
        dv,
    ]
    for member, out in enumerate((gq_ref, gk_ref, gv_ref)):
        sg = sigs[member]
        dfilt = dacts[member] * (sg * (1.0 + filts[member] * (1.0 - sg)))
        taps = taps_ref[member]
        total = None
        pieces = []
        for lag in range(CONV):
            masked = dfilt if lag == 0 else dfilt * masks[lag]
            pieces.append(jnp.sum(masked * lagged(projs[member], lag, rows), axis=0, keepdims=True))
            scaled = masked * taps[lag : lag + 1, :]
            ext = jnp.concatenate([jnp.zeros((RIM, HEAD_DIM), F32), scaled], axis=0)
            if lag:
                ext = pltpu.roll(ext, rows + RIM - lag, 0)
            total = ext if total is None else total + ext
        here = total[RIM:]
        out[0] = here.astype(BF16)
        tail_ref[0, member] = here[rows - RIM :]
        rim_ref[0, member] = total[:RIM]
        gt = jnp.concatenate(pieces, axis=0)

        @pl.when(mb == 0)
        def _(gt=gt, member=member):
            gtaps_ref[member] = gt

        @pl.when(mb > 0)
        def _(gt=gt, member=member):
            gtaps_ref[member] += gt


def mix_grad(offsets, lengths, base, proj3, rates, taps, dend, dout, start, ps, phi, m, inv, wr, up):
    count, heads, rows, _ = ps.shape
    ext_rows = rows + HALO
    per_head = pl.BlockSpec((1, 1, rows, HEAD_DIM), lambda h, m: (m, h, 0, 0))
    proj_spec = pl.BlockSpec((1, ext_rows, HEAD_DIM), lambda h, m: (m, 0, h))
    out_spec = pl.BlockSpec((1, rows, HEAD_DIM), lambda h, m: (m, 0, h))
    rate_spec = pl.BlockSpec((1, 1, rows, 1), lambda h, m: (m, h, 0, 0))
    taps_spec = pl.BlockSpec((3, CONV, HEAD_DIM), lambda h, m: (0, 0, h))
    small = pl.BlockSpec((1, 3, RIM, HEAD_DIM), lambda h, m: (m, 0, 0, h))
    small_shape = jax.ShapeDtypeStruct((count, 3, RIM, heads * HEAD_DIM), F32)
    return pl.pallas_call(
        mix_grad_body,
        grid=(heads, count),
        in_specs=[
            smem_spec(), smem_spec(), smem_spec(),
            proj_spec, proj_spec, proj_spec, rate_spec, taps_spec,
            pl.BlockSpec((1, 1, HEAD_DIM, HEAD_DIM), lambda h, m: (m, h, 0, 0)),
        ]
        + [per_head] * 8,
        out_specs=[out_spec] * 3 + [small, small, rate_spec, taps_spec],
        out_shape=[jax.ShapeDtypeStruct((count, rows, heads * HEAD_DIM), BF16)] * 3
        + [
            small_shape, small_shape,
            jax.ShapeDtypeStruct(rates.shape, F32),
            jax.ShapeDtypeStruct(taps.shape, F32),
        ],
        compiler_params=params(2),
        name="mix_grad",
    )(offsets, lengths, base, *proj3, rates, taps, dend, dout, start, ps, phi, m, inv, wr, up)


def proj_back_body(
    gq_ref, gk_ref, gv_ref, tail_ref, rim_ref, grate_ref, x_ref, w_ref, beta_ref, gattn_ref, head_ref,
    gx_ref, gw_ref, gbeta_ref, acc_ref,
):
    step = pl.program_id(0)
    rows = gq_ref.shape[1]
    heads = grate_ref.shape[1]
    lane = lax.broadcasted_iota(jnp.int32, (rows, heads), 1)
    grate = jnp.zeros((rows, heads), F32)
    for h in range(heads):
        grate = jnp.where(lane == h, grate_ref[0, h], grate)
    x = x_ref[0, HALO:, :]
    total = mm(grate, beta_ref[...], 1, 1)
    adds = []
    for member, ref in enumerate((gq_ref, gk_ref, gv_ref)):
        last = (tail_ref[0, member] + rim_ref[0, member]).astype(BF16)
        g = jnp.concatenate([ref[0, : rows - RIM], last], axis=0)
        total += mm(g, w_ref[member], 1, 1)
        adds.append(mm(x, g, 0, 0))
    adds.append(mm(gattn_ref[0], head_ref[0], 0, 0))
    gx_ref[0] = total.astype(BF16)
    gb = mm(x, grate, 0, 0)

    @pl.when(step == 0)
    def _():
        for member in range(4):
            acc_ref[member] = adds[member]
        gbeta_ref[...] = gb

    @pl.when(step > 0)
    def _():
        for member in range(4):
            acc_ref[member] += adds[member]
        gbeta_ref[...] += gb

    @pl.when(step == pl.num_programs(0) - 1)
    def _():
        gw_ref[...] = acc_ref[...].astype(BF16)


def proj_back(g3, tail, rim, grate, x_ext, mixer_weights, beta_weight, grad_attn, head_out):
    count, rows, head_width = g3[0].shape
    ext_rows, width = x_ext.shape[1:]
    heads = beta_weight.shape[1]
    g_spec = pl.BlockSpec((1, rows, head_width), lambda m: (m, 0, 0))
    small = pl.BlockSpec((1, 3, RIM, head_width), lambda m: (m, 0, 0, 0))
    row_spec = pl.BlockSpec((1, rows, width), lambda m: (m, 0, 0))
    return pl.pallas_call(
        proj_back_body,
        grid=(count,),
        in_specs=[
            g_spec, g_spec, g_spec, small, small,
            pl.BlockSpec((1, heads, rows, 1), lambda m: (m, 0, 0, 0)),
            pl.BlockSpec((1, ext_rows, width), lambda m: (m, 0, 0)),
            pl.BlockSpec((3, width, head_width), lambda m: (0, 0, 0)),
            pl.BlockSpec((width, heads), lambda m: (0, 0)),
            row_spec, g_spec,
        ],
        out_specs=[
            row_spec,
            pl.BlockSpec((4, width, head_width), lambda m: (0, 0, 0)),
            pl.BlockSpec((width, heads), lambda m: (0, 0)),
        ],
        out_shape=[
            jax.ShapeDtypeStruct((count, rows, width), BF16),
            jax.ShapeDtypeStruct((4, width, head_width), BF16),
            jax.ShapeDtypeStruct((width, heads), F32),
        ],
        scratch_shapes=[pltpu.VMEM((4, width, head_width), F32)],
        compiler_params=params(1),
        name="proj_back",
    )(*g3, tail, rim, grate, x_ext, mixer_weights, beta_weight, grad_attn, head_out)


def shifted(block, axis, distance):
    count = lax.axis_size(axis)
    return lax.ppermute(block, axis, [(i, (i + distance) % count) for i in range(count)])


def compose(pair, axis, backward):
    count = lax.axis_size(axis)
    place = lax.axis_index(axis)
    gathered = lax.all_gather(pair, axis)
    laps = count - 1 - place if backward else place

    def one(lap, state):
        source = count - 1 - lap if backward else lap
        block = lax.dynamic_index_in_dim(gathered, source, 0, False)
        return (
            jnp.einsum("mhij,mhjk->mhik", block[0], state.astype(BF16), preferred_element_type=F32)
            + block[1]
        )

    return lax.fori_loop(0, laps, one, jnp.zeros(pair.shape[1:], F32))


def rms(values, gain):
    return values * lax.rsqrt(jnp.mean(values * values, axis=-1, keepdims=True) + EPS) * gain


def rms_back(grad, values, gain):
    inv = lax.rsqrt(jnp.mean(values * values, axis=-1, keepdims=True) + EPS)
    weighted = grad * gain
    grad_in = inv * weighted - values * inv**3 * jnp.mean(weighted * values, axis=-1, keepdims=True)
    return grad_in, jnp.sum(grad * values * inv, axis=(0, 1))


def per_device(
    inputs, attn_gain, mixer_weights, beta_weight, filter_weights, out_gain, dense_gain, dense_weights,
    seq_offsets, seq_lengths, out_grad,
):
    count, local_rows, width = inputs.shape
    rows = local_rows * lax.axis_size("head")
    base = (lax.axis_index("seq") * rows).astype(jnp.int32).reshape(1)
    taps = filter_weights.astype(F32)
    gain_row = out_gain.reshape(1, HEAD_DIM)
    dense_full = lax.all_gather(dense_weights, "seq", axis=1, tiled=True)
    grad_top = lax.all_gather(out_grad, "head", axis=1, tiled=True)

    resid_in = inputs.astype(F32)
    normed_local = rms(resid_in, attn_gain).astype(BF16)
    gathered = lax.all_gather(normed_local, "head", axis=1, tiled=True)
    halo = shifted(gathered[:, rows - HALO :, :], "seq", 1)
    x_ext = jnp.concatenate([halo, gathered], axis=1)
    pq, pk, pv, rates, ps, oloc, phi, psi, score, inv, wr, up, pair = mix_fwd(
        seq_offsets, seq_lengths, base, x_ext, mixer_weights, beta_weight, taps
    )
    state_in = compose(pair, "seq", False)
    start, mixed, head_out, attn_part = mix_out(state_in, ps, oloc, phi, psi, gain_row, mixer_weights)
    attn = lax.psum_scatter(attn_part, "head", scatter_dimension=1, tiled=True).astype(F32)
    resid_mid = resid_in + attn
    dense_in = lax.all_gather(rms(resid_mid, dense_gain).astype(BF16), "head", axis=1, tiled=True)
    down_part, gin_part, dense_part = dense(
        dense_in.reshape(-1, width), grad_top.reshape(-1, width), dense_full
    )
    gin = lax.psum_scatter(
        gin_part.reshape(count, rows, width), "head", scatter_dimension=1, tiled=True
    ).astype(F32)
    down = lax.psum_scatter(
        down_part.reshape(count, rows, width), "head", scatter_dimension=1, tiled=True
    ).astype(F32)
    dense_total = lax.psum_scatter(dense_part, "seq", scatter_dimension=1, tiled=True).astype(F32)
    output = (resid_mid + down).astype(BF16)
    grad_norm, dense_gain_part = rms_back(gin, resid_mid, dense_gain)
    grad_mid = out_grad.astype(F32) + grad_norm
    grad_attn = lax.all_gather(grad_mid.astype(BF16), "head", axis=1, tiled=True)
    dout, out_gain_part, dstate = mix_back(grad_attn, mixer_weights, mixed, gain_row, ps, phi)
    dpair = jnp.stack([jnp.swapaxes(pair[0], 2, 3), dstate])
    dend = compose(dpair, "seq", True)
    gq, gk, gv, tail, rim, grate, filter_part = mix_grad(
        seq_offsets, seq_lengths, base, (pq, pk, pv), rates, taps, dend, dout, start, ps, phi, score, inv, wr, up
    )
    rim_next = shifted(rim, "seq", -1)
    last_shard = lax.axis_index("seq") == lax.axis_size("seq") - 1
    rim_next = jnp.where(last_shard, 0.0, rim_next)
    gx_part, mixer_part, beta_part = proj_back(
        (gq, gk, gv), tail, rim_next, grate, x_ext, mixer_weights, beta_weight, grad_attn, head_out
    )
    gx = lax.psum_scatter(gx_part, "head", scatter_dimension=1, tiled=True).astype(F32)
    grad_in_norm, attn_gain_part = rms_back(gx, resid_in, attn_gain)
    input_grad = grad_mid + grad_in_norm
    mixer_total = lax.psum(mixer_part.astype(F32), "seq")
    beta_total, filter_total = lax.psum((beta_part, filter_part), "seq")
    attn_gain_total, out_gain_total, dense_gain_total = lax.psum(
        (attn_gain_part, out_gain_part.reshape(HEAD_DIM), dense_gain_part), ("seq", "head")
    )
    return (
        output, input_grad, attn_gain_total, mixer_total, beta_total, filter_total, out_gain_total,
        dense_gain_total, dense_total,
    )


def solution(mesh):
    rows = P(None, ("seq", "head"), None)
    return jax.shard_map(
        per_device,
        mesh=mesh,
        in_specs=(
            rows, P(), P(None, None, "head"), P(None, "head"), P(None, None, "head"), P(), P(),
            P(None, "seq", "head"), P(), P(), rows,
        ),
        out_specs=(
            rows, rows, P(), P(None, None, "head"), P(None, "head"), P(None, None, "head"), P(), P(),
            P(None, "seq", "head"),
        ),
        check_vma=False,
    )
```

```python
import functools

import jax
import jax.numpy as jnp
from jax import lax
from jax.experimental import pallas as pl
from jax.experimental.pallas import tpu as pltpu
from jax.sharding import PartitionSpec as P

HEAD_DIM = 128
CONV = 4
CHUNK = 128
HALO = 16
RIM = 8
EPS = 1e-06
F32 = jnp.float32
BF16 = jnp.bfloat16
VMEM_LIMIT = 56 * 1024 * 1024


def mm(a, b, ca=1, cb=0):
    return lax.dot_general(
        a.astype(BF16), b.astype(BF16), (((ca,), (cb,)), ((), ())), preferred_element_type=F32
    )


def split(a):
    high = a.astype(BF16)
    return high, (a - high.astype(F32)).astype(BF16)


def mm3(a, b, ca=1, cb=0):
    ah, al = split(a)
    bh, bl = split(b)
    return mm(ah, bh, ca, cb) + (mm(ah, bl, ca, cb) + mm(al, bh, ca, cb))


def sigmoid(v):
    return 1.0 / (1.0 + jnp.exp(-v))


def row_info(off_ref, len_ref, m, base, rows):
    t = base + lax.broadcasted_iota(jnp.int32, (rows, 1), 0)
    start = jnp.zeros_like(t)
    length = jnp.zeros_like(t)
    for i in range(off_ref.shape[1]):
        inside = t >= off_ref[m, i]
        start = jnp.where(inside, off_ref[m, i], start)
        length = jnp.where(inside, len_ref[m, i], length)
    rel = t - start
    return rel, (rel < length).astype(F32)


def chunk_masks(rel):
    n = rel.shape[0]
    i = lax.broadcasted_iota(jnp.int32, (n, n), 0)
    j = lax.broadcasted_iota(jnp.int32, (n, n), 1)
    same = rel >= i - j
    strict = jnp.logical_and(same, i > j)
    incl = jnp.logical_and(same, i >= j)
    col = lax.broadcasted_iota(jnp.int32, (n, 1), 0)
    sees = (rel > col).astype(F32)
    last = rel[n - 1 : n, :]
    stays = ((n - 1 - col) <= last).astype(F32)
    keep = (last > n - 1).astype(F32)
    return strict, incl, sees, stays, keep


def unit_lower_inverse(a_list):
    n = a_list[0].shape[0]
    i = lax.broadcasted_iota(jnp.int32, (n, n), 0)
    j = lax.broadcasted_iota(jnp.int32, (n, n), 1)
    eye = (i == j).astype(F32)
    size = 1
    inv_list = [eye for _ in a_list]
    while size < n:
        pair = jnp.logical_and(i // size == j // size + 1, (i // size) % 2 == 1)
        below = [jnp.where(pair, a, 0.0) for a in a_list]
        if size == 1:
            inv_list = [eye - b for b in below]
        else:
            half = [mm3(b, inv) for b, inv in zip(below, inv_list)]
            inv_list = [inv - mm3(inv, h) for inv, h in zip(inv_list, half)]
        size *= 2
    return inv_list


def lagged(ext, lag, rows):
    moved = pltpu.roll(ext, lag, 0) if lag else ext
    return moved[HALO : HALO + rows]


def lag_masks(rel):
    return [None] + [(rel >= lag).astype(F32) for lag in range(1, CONV)]


def filtered(ext, taps, masks, rows):
    total = None
    for lag in range(CONV):
        term = taps[lag : lag + 1, :] * lagged(ext, lag, rows)
        if masks[lag] is not None:
            term = term * masks[lag]
        total = term if total is None else total + term
    return total


def mix_fwd_body(
    off_ref, len_ref, base_ref, x_ref, w_ref, beta_ref, taps_ref,
    pq_ref, pk_ref, pv_ref, rate_ref, ps_ref, oloc_ref, phi_ref, psi_ref, m_ref, inv_ref, wr_ref, up_ref, trans_ref, state_ref,
):
    mb = pl.program_id(0)
    head = pl.program_id(1)
    rows = x_ref.shape[1] - HALO
    rel, valid = row_info(off_ref, len_ref, mb, base_ref[0], rows)
    x = x_ref[0]
    masks = lag_masks(rel)
    acts = []
    for member, out in enumerate((pq_ref, pk_ref, pv_ref)):
        proj = mm(x, w_ref[member]).astype(BF16)
        out[0] = proj
        filt = filtered(proj.astype(F32), taps_ref[member], masks, rows)
        acts.append(filt * sigmoid(filt))
    query, key, value = acts
    query = query * lax.rsqrt(jnp.sum(query * query, axis=-1, keepdims=True) + EPS)
    key = key * lax.rsqrt(jnp.sum(key * key, axis=-1, keepdims=True) + EPS)
    raw_all = mm(x, beta_ref[...])[HALO:]
    lane = lax.broadcasted_iota(jnp.int32, raw_all.shape, 1)
    raw = jnp.sum(jnp.where(lane == head, raw_all, 0.0), axis=-1, keepdims=True)
    rate_ref[0, 0] = raw
    rate = sigmoid(raw) * valid
    spans = [slice(c * CHUNK, (c + 1) * CHUNK) for c in range(rows // CHUNK)]
    all_masks = [chunk_masks(rel[s]) for s in spans]
    systems, scores = [], []
    for s, (strict, incl, _, _, _) in zip(spans, all_masks):
        both = mm(jnp.concatenate([query[s], key[s]], axis=0), key[s], 1, 1)
        scores.append(jnp.where(incl, both[:CHUNK], 0.0))
        systems.append(jnp.where(strict, rate[s] * both[CHUNK:], 0.0))
    inverses = unit_lower_inverse(systems)
    i = lax.broadcasted_iota(jnp.int32, (HEAD_DIM, HEAD_DIM), 0)
    j = lax.broadcasted_iota(jnp.int32, (HEAD_DIM, HEAD_DIM), 1)
    eye = (i == j).astype(F32)
    phis, psis, ps, olocs = [], [], [], []
    for s, masks_c, inv, score in zip(spans, all_masks, inverses, scores):
        _, _, sees, stays, keep = masks_c
        right = rate[s] * jnp.concatenate([sees * key[s], value[s]], axis=1)
        solved = mm(inv, right)
        write, update = solved[:, :HEAD_DIM], solved[:, HEAD_DIM:]
        moved = mm(stays * key[s], solved, 0, 0)
        phi = keep * eye - moved[:, :HEAD_DIM]
        psi = moved[:, HEAD_DIM:]
        scored = mm(score, solved)
        p = sees * query[s] - scored[:, :HEAD_DIM]
        m_ref[0, 0, s] = score.astype(BF16)
        inv_ref[0, 0, s] = inv.astype(BF16)
        wr_ref[0, 0, s] = write.astype(BF16)
        up_ref[0, 0, s] = update
        ps_ref[0, 0, s] = p.astype(BF16)
        oloc_ref[0, 0, s] = scored[:, HEAD_DIM:]
        phi_ref[0, 0, s] = phi
        psi_ref[0, 0, s] = psi
        phis.append(phi)
        psis.append(psi)
    trans, state = phis[0], psis[0]
    for phi, psi in zip(phis[1:], psis[1:]):
        both = mm3(phi, jnp.concatenate([trans, state], axis=1))
        trans = both[:, :HEAD_DIM]
        state = both[:, HEAD_DIM:] + psi
    trans_ref[0, 0] = trans.astype(BF16)
    state_ref[0, 0] = state.astype(BF16)


def smem_spec():
    return pl.BlockSpec(memory_space=pltpu.SMEM)


def params(count):
    return pltpu.CompilerParams(
        dimension_semantics=("arbitrary",) * count, vmem_limit_bytes=VMEM_LIMIT
    )


def mix_fwd(offsets, lengths, base, x_ext, mixer_weights, beta_weight, taps):
    count, ext_rows, width = x_ext.shape
    rows = ext_rows - HALO
    heads = beta_weight.shape[1]
    per_head = pl.BlockSpec((1, 1, rows, HEAD_DIM), lambda m, h: (m, h, 0, 0))
    proj_spec = pl.BlockSpec((1, ext_rows, HEAD_DIM), lambda m, h: (m, 0, h))
    proj_shape = jax.ShapeDtypeStruct((count, ext_rows, heads * HEAD_DIM), BF16)

    def big(kind):
        return jax.ShapeDtypeStruct((count, heads, rows, HEAD_DIM), kind)

    return pl.pallas_call(
        mix_fwd_body,
        grid=(count, heads),
        in_specs=[
            smem_spec(), smem_spec(), smem_spec(),
            pl.BlockSpec((1, ext_rows, width), lambda m, h: (m, 0, 0)),
            pl.BlockSpec((3, width, HEAD_DIM), lambda m, h: (0, 0, h)),
            pl.BlockSpec(beta_weight.shape, lambda m, h: (0, 0)),
            pl.BlockSpec((3, CONV, HEAD_DIM), lambda m, h: (0, 0, h)),
        ],
        out_specs=[proj_spec] * 3
        + [pl.BlockSpec((1, 1, rows, 1), lambda m, h: (m, h, 0, 0))]
        + [per_head] * 8
        + [pl.BlockSpec((1, 1, HEAD_DIM, HEAD_DIM), lambda m, h: (m, h, 0, 0))] * 2,
        out_shape=[proj_shape] * 3
        + [jax.ShapeDtypeStruct((count, heads, rows, 1), F32)]
        + [big(BF16), big(F32), big(F32), big(F32), big(BF16), big(BF16), big(BF16), big(F32)]
        + [jax.ShapeDtypeStruct((count, heads, HEAD_DIM, HEAD_DIM), BF16)] * 2,
        compiler_params=params(2),
        name="mix_fwd",
    )(offsets, lengths, base, x_ext, mixer_weights, beta_weight, taps)


def mix_out_body(state_ref, ps_ref, oloc_ref, phi_ref, psi_ref, gain_ref, w_ref, start_ref, mixed_ref, head_ref, part_ref):
    heads = ps_ref.shape[1]
    rows = ps_ref.shape[2]
    gain = gain_ref[...]
    states = [state_ref[0, h] for h in range(heads)]
    for c in range(rows // CHUNK):
        s = slice(c * CHUNK, (c + 1) * CHUNK)
        for h in range(heads):
            state = states[h]
            start_ref[0, h, s] = state.astype(BF16)
            mixed = oloc_ref[0, h, s] + mm(ps_ref[0, h, s], state)
            mixed_ref[0, h, s] = mixed
            normed = mixed * lax.rsqrt(jnp.mean(mixed * mixed, axis=-1, keepdims=True) + EPS) * gain
            head_ref[0, s, h * HEAD_DIM : (h + 1) * HEAD_DIM] = normed.astype(BF16)
            states[h] = mm3(phi_ref[0, h, s], state) + psi_ref[0, h, s]
    part_ref[0] = mm(head_ref[0], w_ref[0], 1, 1).astype(BF16)


def mix_out(state_in, ps, oloc, phi, psi, out_gain, mixer_weights):
    count, heads, rows, _ = ps.shape
    width = mixer_weights.shape[1]
    head_width = mixer_weights.shape[2]
    per_mb = pl.BlockSpec((1, heads, rows, HEAD_DIM), lambda m: (m, 0, 0, 0))
    return pl.pallas_call(
        mix_out_body,
        grid=(count,),
        in_specs=[
            pl.BlockSpec((1, heads, HEAD_DIM, HEAD_DIM), lambda m: (m, 0, 0, 0)),
            per_mb, per_mb, per_mb, per_mb,
            pl.BlockSpec((1, HEAD_DIM), lambda m: (0, 0)),
            pl.BlockSpec((1, width, head_width), lambda m: (3, 0, 0)),
        ],
        out_specs=[
            per_mb, per_mb,
            pl.BlockSpec((1, rows, head_width), lambda m: (m, 0, 0)),
            pl.BlockSpec((1, rows, width), lambda m: (m, 0, 0)),
        ],
        out_shape=[
            jax.ShapeDtypeStruct(ps.shape, BF16),
            jax.ShapeDtypeStruct(ps.shape, F32),
            jax.ShapeDtypeStruct((count, rows, head_width), BF16),
            jax.ShapeDtypeStruct((count, rows, width), BF16),
        ],
        compiler_params=params(1),
        name="mix_out",
    )(state_in, ps, oloc, phi, psi, out_gain, mixer_weights)


def dense_body(x_ref, g_ref, w_ref, down_ref, gin_ref, grad_ref, acc_ref):
    step = pl.program_id(0)
    x = x_ref[...]
    g = g_ref[...]
    gate = mm(x, w_ref[0])
    up = mm(x, w_ref[1])
    grad_hidden = mm(g, w_ref[2])
    sg = sigmoid(gate)
    silu = gate * sg
    hidden = (silu * up).astype(BF16)
    grad_gate = (grad_hidden * up * (sg * (1.0 + gate * (1.0 - sg)))).astype(BF16)
    grad_up = (grad_hidden * silu).astype(BF16)
    down_ref[...] = mm(hidden, w_ref[2], 1, 1).astype(BF16)
    gin_ref[...] = (mm(grad_gate, w_ref[0], 1, 1) + mm(grad_up, w_ref[1], 1, 1)).astype(BF16)

    @pl.when(step == 0)
    def _():
        acc_ref[0] = mm(x, grad_gate, 0, 0)
        acc_ref[1] = mm(x, grad_up, 0, 0)
        acc_ref[2] = mm(g, hidden, 0, 0)

    @pl.when(step > 0)
    def _():
        acc_ref[0] += mm(x, grad_gate, 0, 0)
        acc_ref[1] += mm(x, grad_up, 0, 0)
        acc_ref[2] += mm(g, hidden, 0, 0)

    @pl.when(step == pl.num_programs(0) - 1)
    def _():
        grad_ref[...] = acc_ref[...].astype(BF16)


def dense(dense_in, grad_top, weights):
    rows, width = dense_in.shape
    hidden = weights.shape[2]
    tile = 256
    row_spec = pl.BlockSpec((tile, width), lambda i: (i, 0))
    whole = pl.BlockSpec((3, width, hidden), lambda i: (0, 0, 0), pipeline_mode=pl.Buffered(1))
    return pl.pallas_call(
        dense_body,
        grid=(rows // tile,),
        in_specs=[row_spec, row_spec, whole],
        out_specs=[row_spec, row_spec, whole],
        out_shape=[
            jax.ShapeDtypeStruct((rows, width), BF16),
            jax.ShapeDtypeStruct((rows, width), BF16),
            jax.ShapeDtypeStruct((3, width, hidden), BF16),
        ],
        scratch_shapes=[pltpu.VMEM((3, width, hidden), F32)],
        compiler_params=params(1),
        name="dense",
    )(dense_in, grad_top, weights)


def mix_back_body(grad_ref, w_ref, mixed_ref, gain_ref, ps_ref, phi_ref, dout_ref, gain_grad_ref, dstate_ref):
    heads = ps_ref.shape[1]
    rows = ps_ref.shape[2]
    gain = gain_ref[...]
    grad_head = mm(grad_ref[0], w_ref[0])
    gain_grad = jnp.zeros((1, HEAD_DIM), F32)
    douts = []
    for h in range(heads):
        e = grad_head[:, h * HEAD_DIM : (h + 1) * HEAD_DIM]
        v = mixed_ref[0, h]
        r = lax.rsqrt(jnp.mean(v * v, axis=-1, keepdims=True) + EPS)
        weighted = e * gain
        dout = r * weighted - v * (r * r * r * jnp.mean(weighted * v, axis=-1, keepdims=True))
        gain_grad += jnp.sum(e * v * r, axis=0, keepdims=True)
        dout = dout.astype(BF16)
        dout_ref[0, h] = dout
        douts.append(dout)
    states = [None] * heads
    for c in reversed(range(rows // CHUNK)):
        s = slice(c * CHUNK, (c + 1) * CHUNK)
        for h in range(heads):
            new = mm(ps_ref[0, h, s], douts[h][s], 0, 0)
            if states[h] is not None:
                new += mm3(phi_ref[0, h, s], states[h], 0, 0)
            states[h] = new
    for h in range(heads):
        dstate_ref[0, h] = states[h].astype(BF16)

    @pl.when(pl.program_id(0) == 0)
    def _():
        gain_grad_ref[...] = gain_grad

    @pl.when(pl.program_id(0) > 0)
    def _():
        gain_grad_ref[...] += gain_grad


def mix_back(grad_attn, mixer_weights, mixed, out_gain, ps, phi):
    count, heads, rows, _ = ps.shape
    width = mixer_weights.shape[1]
    head_width = mixer_weights.shape[2]
    per_mb = pl.BlockSpec((1, heads, rows, HEAD_DIM), lambda m: (m, 0, 0, 0))
    return pl.pallas_call(
        mix_back_body,
        grid=(count,),
        in_specs=[
            pl.BlockSpec((1, rows, width), lambda m: (m, 0, 0)),
            pl.BlockSpec((1, width, head_width), lambda m: (3, 0, 0)),
            per_mb,
            pl.BlockSpec((1, HEAD_DIM), lambda m: (0, 0)),
            per_mb, per_mb,
        ],
        out_specs=[
            per_mb,
            pl.BlockSpec((1, HEAD_DIM), lambda m: (0, 0)),
            pl.BlockSpec((1, heads, HEAD_DIM, HEAD_DIM), lambda m: (m, 0, 0, 0)),
        ],
        out_shape=[
            jax.ShapeDtypeStruct(ps.shape, BF16),
            jax.ShapeDtypeStruct((1, HEAD_DIM), F32),
            jax.ShapeDtypeStruct((count, heads, HEAD_DIM, HEAD_DIM), BF16),
        ],
        compiler_params=params(1),
        name="mix_back",
    )(grad_attn, mixer_weights, mixed, out_gain, ps, phi)


def mix_grad_body(
    off_ref, len_ref, base_ref, pq_ref, pk_ref, pv_ref, rate_ref, taps_ref, dend_ref, dout_ref, start_ref, ps_ref, phi_ref,
    m_ref, inv_ref, wr_ref, up_ref,
    gq_ref, gk_ref, gv_ref, tail_ref, rim_ref, grate_ref, gtaps_ref,
):
    mb = pl.program_id(1)
    rows = rate_ref.shape[2]
    rel, valid = row_info(off_ref, len_ref, mb, base_ref[0], rows)
    masks = lag_masks(rel)
    projs, filts, sigs, acts = [], [], [], []
    for member, ref in enumerate((pq_ref, pk_ref, pv_ref)):
        proj = ref[0].astype(F32)
        filt = filtered(proj, taps_ref[member], masks, rows)
        sg = sigmoid(filt)
        projs.append(proj)
        filts.append(filt)
        sigs.append(sg)
        acts.append(filt * sg)
    rq = lax.rsqrt(jnp.sum(acts[0] * acts[0], axis=-1, keepdims=True) + EPS)
    rk = lax.rsqrt(jnp.sum(acts[1] * acts[1], axis=-1, keepdims=True) + EPS)
    query = acts[0] * rq
    key = acts[1] * rk
    value = acts[2]
    sig_rate = sigmoid(rate_ref[0, 0])
    rate = sig_rate * valid
    dstate = dend_ref[0, 0]
    spans = [slice(c * CHUNK, (c + 1) * CHUNK) for c in range(rows // CHUNK)]
    dstates = [None] * len(spans)
    for c in reversed(range(len(spans))):
        s = spans[c]
        dstates[c] = dstate
        if c:
            dstate = mm3(phi_ref[0, 0, s], dstate, 0, 0) + mm(ps_ref[0, 0, s], dout_ref[0, 0, s], 0, 0)
    dqs, dks, dvs, drates = [], [], [], []
    for c, s in enumerate(spans):
        strict, incl, sees, stays, _ = chunk_masks(rel[s])
        q, k, v, b = query[s], key[s], value[s], rate[s]
        dout = dout_ref[0, 0, s]
        start = start_ref[0, 0, s]
        fresh = up_ref[0, 0, s] - mm(wr_ref[0, 0, s], start)
        dfresh = mm(m_ref[0, 0, s], dout, 0, 0) + mm(stays * k, dstates[c])
        e = mm(inv_ref[0, 0, s], dfresh, 0, 0)
        left = jnp.concatenate([dout, e.astype(BF16)], axis=0)
        right = jnp.concatenate([fresh.astype(BF16), start], axis=0)
        outer = mm(left, right, 1, 1)
        dscore = jnp.where(incl, outer[:CHUNK, :CHUNK], 0.0)
        dsystem = jnp.where(strict, -outer[CHUNK:, :CHUNK], 0.0)
        grads = jnp.concatenate([dscore, dsystem], axis=0).astype(BF16)
        byk = mm(grads, k)
        z = byk[CHUNK:] - sees * outer[CHUNK:, CHUNK:]
        dqs.append(sees * outer[:CHUNK, CHUNK:] + byk[:CHUNK])
        dk = mm(grads, jnp.concatenate([q, b * k], axis=0), 0, 0)
        dks.append(dk + stays * mm(fresh, dstates[c], 1, 1) + b * z)
        dvs.append(b * e)
        drates.append(jnp.sum(e * v + k * z, axis=-1, keepdims=True))
    dq = jnp.concatenate(dqs, axis=0)
    dk = jnp.concatenate(dks, axis=0)
    dv = jnp.concatenate(dvs, axis=0)
    drate = jnp.concatenate(drates, axis=0)
    grate_ref[0, 0] = drate * valid * sig_rate * (1.0 - sig_rate)
    dacts = [
        rq * dq - acts[0] * (rq * rq * rq * jnp.sum(dq * acts[0], axis=-1, keepdims=True)),
        rk * dk - acts[1] * (rk * rk * rk * jnp.sum(dk * acts[1], axis=-1, keepdims=True)),
        dv,
    ]
    for member, out in enumerate((gq_ref, gk_ref, gv_ref)):
        sg = sigs[member]
        dfilt = dacts[member] * (sg * (1.0 + filts[member] * (1.0 - sg)))
        taps = taps_ref[member]
        total = None
        pieces = []
        for lag in range(CONV):
            masked = dfilt if lag == 0 else dfilt * masks[lag]
            pieces.append(jnp.sum(masked * lagged(projs[member], lag, rows), axis=0, keepdims=True))
            scaled = masked * taps[lag : lag + 1, :]
            ext = jnp.concatenate([jnp.zeros((RIM, HEAD_DIM), F32), scaled], axis=0)
            if lag:
                ext = pltpu.roll(ext, rows + RIM - lag, 0)
            total = ext if total is None else total + ext
        here = total[RIM:]
        out[0] = here.astype(BF16)
        tail_ref[0, member] = here[rows - RIM :]
        rim_ref[0, member] = total[:RIM]
        gt = jnp.concatenate(pieces, axis=0)

        @pl.when(mb == 0)
        def _(gt=gt, member=member):
            gtaps_ref[member] = gt

        @pl.when(mb > 0)
        def _(gt=gt, member=member):
            gtaps_ref[member] += gt


def mix_grad(offsets, lengths, base, proj3, rates, taps, dend, dout, start, ps, phi, m, inv, wr, up):
    count, heads, rows, _ = ps.shape
    ext_rows = rows + HALO
    per_head = pl.BlockSpec((1, 1, rows, HEAD_DIM), lambda h, m: (m, h, 0, 0))
    proj_spec = pl.BlockSpec((1, ext_rows, HEAD_DIM), lambda h, m: (m, 0, h))
    out_spec = pl.BlockSpec((1, rows, HEAD_DIM), lambda h, m: (m, 0, h))
    rate_spec = pl.BlockSpec((1, 1, rows, 1), lambda h, m: (m, h, 0, 0))
    taps_spec = pl.BlockSpec((3, CONV, HEAD_DIM), lambda h, m: (0, 0, h))
    small = pl.BlockSpec((1, 3, RIM, HEAD_DIM), lambda h, m: (m, 0, 0, h))
    small_shape = jax.ShapeDtypeStruct((count, 3, RIM, heads * HEAD_DIM), F32)
    return pl.pallas_call(
        mix_grad_body,
        grid=(heads, count),
        in_specs=[
            smem_spec(), smem_spec(), smem_spec(),
            proj_spec, proj_spec, proj_spec, rate_spec, taps_spec,
            pl.BlockSpec((1, 1, HEAD_DIM, HEAD_DIM), lambda h, m: (m, h, 0, 0)),
        ]
        + [per_head] * 8,
        out_specs=[out_spec] * 3 + [small, small, rate_spec, taps_spec],
        out_shape=[jax.ShapeDtypeStruct((count, rows, heads * HEAD_DIM), BF16)] * 3
        + [
            small_shape, small_shape,
            jax.ShapeDtypeStruct(rates.shape, F32),
            jax.ShapeDtypeStruct(taps.shape, F32),
        ],
        compiler_params=params(2),
        name="mix_grad",
    )(offsets, lengths, base, *proj3, rates, taps, dend, dout, start, ps, phi, m, inv, wr, up)


def proj_back_body(
    gq_ref, gk_ref, gv_ref, tail_ref, rim_ref, grate_ref, x_ref, w_ref, beta_ref, gattn_ref, head_ref,
    gx_ref, gw_ref, gbeta_ref, acc_ref,
):
    step = pl.program_id(0)
    rows = gq_ref.shape[1]
    heads = grate_ref.shape[1]
    lane = lax.broadcasted_iota(jnp.int32, (rows, heads), 1)
    grate = jnp.zeros((rows, heads), F32)
    for h in range(heads):
        grate = jnp.where(lane == h, grate_ref[0, h], grate)
    x = x_ref[0, HALO:, :]
    total = mm(grate, beta_ref[...], 1, 1)
    adds = []
    for member, ref in enumerate((gq_ref, gk_ref, gv_ref)):
        last = (tail_ref[0, member] + rim_ref[0, member]).astype(BF16)
        g = jnp.concatenate([ref[0, : rows - RIM], last], axis=0)
        total += mm(g, w_ref[member], 1, 1)
        adds.append(mm(x, g, 0, 0))
    adds.append(mm(gattn_ref[0], head_ref[0], 0, 0))
    gx_ref[0] = total.astype(BF16)
    gb = mm(x, grate, 0, 0)

    @pl.when(step == 0)
    def _():
        for member in range(4):
            acc_ref[member] = adds[member]
        gbeta_ref[...] = gb

    @pl.when(step > 0)
    def _():
        for member in range(4):
            acc_ref[member] += adds[member]
        gbeta_ref[...] += gb

    @pl.when(step == pl.num_programs(0) - 1)
    def _():
        gw_ref[...] = acc_ref[...].astype(BF16)


def proj_back(g3, tail, rim, grate, x_ext, mixer_weights, beta_weight, grad_attn, head_out):
    count, rows, head_width = g3[0].shape
    ext_rows, width = x_ext.shape[1:]
    heads = beta_weight.shape[1]
    g_spec = pl.BlockSpec((1, rows, head_width), lambda m: (m, 0, 0))
    small = pl.BlockSpec((1, 3, RIM, head_width), lambda m: (m, 0, 0, 0))
    row_spec = pl.BlockSpec((1, rows, width), lambda m: (m, 0, 0))
    return pl.pallas_call(
        proj_back_body,
        grid=(count,),
        in_specs=[
            g_spec, g_spec, g_spec, small, small,
            pl.BlockSpec((1, heads, rows, 1), lambda m: (m, 0, 0, 0)),
            pl.BlockSpec((1, ext_rows, width), lambda m: (m, 0, 0)),
            pl.BlockSpec((3, width, head_width), lambda m: (0, 0, 0)),
            pl.BlockSpec((width, heads), lambda m: (0, 0)),
            row_spec, g_spec,
        ],
        out_specs=[
            row_spec,
            pl.BlockSpec((4, width, head_width), lambda m: (0, 0, 0)),
            pl.BlockSpec((width, heads), lambda m: (0, 0)),
        ],
        out_shape=[
            jax.ShapeDtypeStruct((count, rows, width), BF16),
            jax.ShapeDtypeStruct((4, width, head_width), BF16),
            jax.ShapeDtypeStruct((width, heads), F32),
        ],
        scratch_shapes=[pltpu.VMEM((4, width, head_width), F32)],
        compiler_params=params(1),
        name="proj_back",
    )(*g3, tail, rim, grate, x_ext, mixer_weights, beta_weight, grad_attn, head_out)


def shifted(block, axis, distance):
    count = lax.axis_size(axis)
    return lax.ppermute(block, axis, [(i, (i + distance) % count) for i in range(count)])


def rms(values, gain):
    return values * lax.rsqrt(jnp.mean(values * values, axis=-1, keepdims=True) + EPS) * gain


def rms_back(grad, values, gain):
    inv = lax.rsqrt(jnp.mean(values * values, axis=-1, keepdims=True) + EPS)
    weighted = grad * gain
    grad_in = inv * weighted - values * inv**3 * jnp.mean(weighted * values, axis=-1, keepdims=True)
    return grad_in, jnp.sum(grad * values * inv, axis=0, keepdims=True)

MESH = pl.DeviceIdType.MESH


def flip(index, bit):
    return index + bit * (1 - 2 * (index // bit % 2))


def remote(src, dst, send, recv, seq, head):
    return pltpu.make_async_remote_copy(
        src_ref=src, dst_ref=dst, send_sem=send, recv_sem=recv, device_id=(seq, head), device_id_type=MESH
    )


def greet(devices, expected):
    barrier = pltpu.get_barrier_semaphore()
    for seq, head in devices:
        pl.semaphore_signal(barrier, inc=1, device_id=(seq, head), device_id_type=MESH)
    pl.semaphore_wait(barrier, expected)


def pieces_of(count, rows, piece):
    return [(m, r) for m in range(count) for r in range(0, rows, piece)]


class HeadGather:
    def __init__(self, out_ref, local, first_row, send, recv, piece):
        self.out, self.local, self.first, self.piece = out_ref, local, first_row, piece
        self.send, self.recv = send, recv
        self.seq, self.head = lax.axis_index("seq"), lax.axis_index("head")
        self.far, self.near = flip(self.head, 2), flip(self.head, 1)
        self.copies = {}

    def rows(self, block, r):
        start = self.first + block * self.local + r
        return pl.ds(pl.multiple_of(start, 16), self.piece)

    def copy(self, kind, at, block, target):
        m, r = at
        n = self.local // self.piece
        ref = self.out.at[m, self.rows(block, r), :]
        c = remote(ref, ref, self.send.at[kind, m * n + r // self.piece], self.recv.at[kind, m * n + r // self.piece], self.seq, target)
        c.start()
        self.copies[kind, at] = c

    def own(self, at):
        self.copy(0, at, self.head, self.far)
        self.copy(1, at, self.head, self.near)

    def forward(self, at):
        self.copies[0, at].wait_recv()
        self.copy(2, at, self.far, self.near)

    def finish(self):
        for (kind, at), c in self.copies.items():
            c.wait_send()
            if kind:
                c.wait_recv()


class HeadScatter:
    def __init__(self, part_ref, local, near_ref, stage_ref, far_ref, send, recv, piece):
        self.part, self.local, self.piece = part_ref, local, piece
        self.nearby, self.stage, self.faraway = near_ref, stage_ref, far_ref
        self.send, self.recv = send, recv
        self.seq, self.head = lax.axis_index("seq"), lax.axis_index("head")
        self.far, self.near = flip(self.head, 2), flip(self.head, 1)
        self.copies = {}

    def index(self, at):
        return at[0] * (self.local // self.piece) + at[1] // self.piece

    def block(self, block, at):
        m, r = at
        return self.part.at[m, pl.ds(pl.multiple_of(block * self.local + r, 16), self.piece), :]

    def start(self, at):
        i = self.index(at)
        for kind, block in ((0, flip(self.near, 2)), (1, self.near)):
            c = remote(
                self.block(block, at), self.nearby.at[kind, i], self.send.at[kind, i], self.recv.at[kind, i], self.seq, self.near
            )
            c.start()
            self.copies[kind, at] = c

    def forward(self, at):
        i = self.index(at)
        self.copies[0, at].wait_recv()
        total = self.block(self.far, at)[...].astype(F32) + self.nearby[0, i].astype(F32)
        self.stage[i] = total.astype(BF16)
        c = remote(self.stage.at[i], self.faraway.at[i], self.send.at[2, i], self.recv.at[2, i], self.seq, self.far)
        c.start()
        self.copies[2, at] = c

    def total(self, at):
        i = self.index(at)
        self.copies[1, at].wait_recv()
        self.copies[2, at].wait_recv()
        near = self.block(self.head, at)[...].astype(F32) + self.nearby[1, i].astype(F32)
        return near + self.faraway[i].astype(F32)

    def finish(self):
        for c in self.copies.values():
            c.wait_send()


def scatter_scratch(count, local, width, piece):
    n = count * local // piece
    return [
        pltpu.VMEM((2, n, piece, width), BF16),
        pltpu.VMEM((n, piece, width), BF16),
        pltpu.VMEM((n, piece, width), BF16),
        pltpu.SemaphoreType.DMA((3, n)),
        pltpu.SemaphoreType.DMA((3, n)),
    ]


def gather_scratch(count, local, piece):
    n = count * local // piece
    return [pltpu.SemaphoreType.DMA((3, n)), pltpu.SemaphoreType.DMA((3, n))]


def vmem_specs(count):
    return [pl.BlockSpec(memory_space=pltpu.VMEM)] * count


def comm_params(collective):
    return pltpu.CompilerParams(
        collective_id=collective, has_side_effects=True, vmem_limit_bytes=VMEM_LIMIT
    )


PIECE = 64


def norm_gather_body(heads, shards, x_ref, gain_ref, out_ref, send, recv, halo_send, halo_recv):
    count, local, _ = x_ref.shape
    seq, head = lax.axis_index("seq"), lax.axis_index("head")
    after = lax.rem(seq + 1, shards)
    before = lax.rem(seq + shards - 1, shards)
    last = head == heads - 1
    gather = HeadGather(out_ref, local, HALO, send, recv, PIECE)
    for m, r in pieces_of(count, local, PIECE):
        x = x_ref[m, pl.ds(r, PIECE), :].astype(F32)
        out_ref[m, gather.rows(head, r), :] = rms(x, gain_ref[...]).astype(BF16)
    greet(
        [(seq, gather.far), (seq, gather.near), (before, heads - 1)],
        2 + heads * last.astype(jnp.int32),
    )
    for at in pieces_of(count, local, PIECE):
        gather.own(at)

    def halo(target):
        src = out_ref.at[:, pl.ds(heads * local, HALO), :]
        return remote(src, out_ref.at[:, pl.ds(0, HALO), :], halo_send.at[target], halo_recv, after, target)

    @pl.when(last)
    def _():
        for target in range(heads):
            halo(target).start()

    for at in pieces_of(count, local, PIECE):
        gather.forward(at)
    gather.finish()
    halo(0).wait_recv()

    @pl.when(last)
    def _():
        for target in range(heads):
            halo(target).wait_send()


def norm_gather(inputs, gain, heads, shards):
    count, local, width = inputs.shape
    return pl.pallas_call(
        functools.partial(norm_gather_body, heads, shards),
        in_specs=vmem_specs(2),
        out_specs=vmem_specs(1)[0],
        out_shape=jax.ShapeDtypeStruct((count, HALO + heads * local, width), BF16),
        scratch_shapes=gather_scratch(count, local, PIECE)
        + [pltpu.SemaphoreType.DMA((heads,)), pltpu.SemaphoreType.DMA],
        compiler_params=comm_params(0),
        name="norm_gather",
    )(inputs, gain)


def resid_gather_body(part_ref, x_ref, gain_ref, resid_ref, out_ref, near_ref, stage_ref, far_ref, ss, sr, gs, gr):
    count, local, _ = x_ref.shape
    scatter = HeadScatter(part_ref, local, near_ref, stage_ref, far_ref, ss, sr, PIECE)
    gather = HeadGather(out_ref, local, 0, gs, gr, PIECE)
    greet([(gather.seq, gather.far), (gather.seq, gather.near)], 2)
    order = pieces_of(count, local, PIECE)
    for at in order:
        scatter.start(at)
    for at in order:
        scatter.forward(at)
    for at in order:
        m, r = at
        resid = x_ref[m, pl.ds(r, PIECE), :].astype(F32) + scatter.total(at)
        resid_ref[m, pl.ds(r, PIECE), :] = resid
        out_ref[m, gather.rows(gather.head, r), :] = rms(resid, gain_ref[...]).astype(BF16)
        gather.own(at)
    for at in order:
        gather.forward(at)
    gather.finish()
    scatter.finish()


def resid_gather(part, inputs, gain):
    count, local, width = inputs.shape
    return pl.pallas_call(
        resid_gather_body,
        in_specs=vmem_specs(3),
        out_specs=vmem_specs(2),
        out_shape=[jax.ShapeDtypeStruct(inputs.shape, F32), jax.ShapeDtypeStruct(part.shape, BF16)],
        scratch_shapes=scatter_scratch(count, local, width, PIECE) + gather_scratch(count, local, PIECE),
        compiler_params=comm_params(1),
        name="resid_gather",
    )(part, inputs, gain)


def grad_gather_body(
    part_ref, resid_ref, top_ref, gain_ref, mid_ref, out_ref, gain_grad_ref, near_ref, stage_ref, far_ref, ss, sr, gs, gr
):
    count, local, width = resid_ref.shape
    scatter = HeadScatter(part_ref, local, near_ref, stage_ref, far_ref, ss, sr, PIECE)
    gather = HeadGather(out_ref, local, 0, gs, gr, PIECE)
    greet([(gather.seq, gather.far), (gather.seq, gather.near)], 2)
    order = pieces_of(count, local, PIECE)
    for at in order:
        scatter.start(at)
    for at in order:
        scatter.forward(at)
    gain_grad = jnp.zeros((1, width), F32)
    for at in order:
        m, r = at
        grad, gain_part = rms_back(scatter.total(at), resid_ref[m, pl.ds(r, PIECE), :], gain_ref[...])
        mid = top_ref[m, pl.ds(r, PIECE), :].astype(F32) + grad
        gain_grad += gain_part
        mid_ref[m, pl.ds(r, PIECE), :] = mid
        out_ref[m, gather.rows(gather.head, r), :] = mid.astype(BF16)
        gather.own(at)
    gain_grad_ref[...] = gain_grad
    for at in order:
        gather.forward(at)
    gather.finish()
    scatter.finish()


def grad_gather(part, resid, grad_top, gain):
    count, local, width = resid.shape
    return pl.pallas_call(
        grad_gather_body,
        in_specs=vmem_specs(4),
        out_specs=vmem_specs(3),
        out_shape=[
            jax.ShapeDtypeStruct(resid.shape, F32),
            jax.ShapeDtypeStruct(part.shape, BF16),
            jax.ShapeDtypeStruct((1, width), F32),
        ],
        scratch_shapes=scatter_scratch(count, local, width, PIECE) + gather_scratch(count, local, PIECE),
        compiler_params=comm_params(2),
        name="grad_gather",
    )(part, resid, grad_top, gain)


def last_scatter_body(part_ref, x_ref, mid_ref, gain_ref, out_ref, gain_grad_ref, near_ref, stage_ref, far_ref, ss, sr):
    count, local, width = x_ref.shape
    scatter = HeadScatter(part_ref, local, near_ref, stage_ref, far_ref, ss, sr, PIECE)
    greet([(scatter.seq, scatter.far), (scatter.seq, scatter.near)], 2)
    order = pieces_of(count, local, PIECE)
    for at in order:
        scatter.start(at)
    for at in order:
        scatter.forward(at)
    gain_grad = jnp.zeros((1, width), F32)
    for at in order:
        m, r = at
        here = pl.ds(r, PIECE)
        grad, gain_part = rms_back(scatter.total(at), x_ref[m, here, :].astype(F32), gain_ref[...])
        gain_grad += gain_part
        out_ref[m, here, :] = mid_ref[m, here, :] + grad
    gain_grad_ref[...] = gain_grad
    scatter.finish()


def last_scatter(part, inputs, mid, gain):
    count, local, width = inputs.shape
    return pl.pallas_call(
        last_scatter_body,
        in_specs=vmem_specs(4),
        out_specs=vmem_specs(2),
        out_shape=[jax.ShapeDtypeStruct(inputs.shape, F32), jax.ShapeDtypeStruct((1, width), F32)],
        scratch_shapes=scatter_scratch(count, local, width, PIECE),
        compiler_params=comm_params(3),
        name="last_scatter",
    )(part, inputs, mid, gain)


def compose_body(shards, backward, trans_ref, state_ref, out_ref, stage_ref, got_ref, tx_ref, t_ref, s_ref, send, recv):
    groups = trans_ref.shape[0]
    seq, head = lax.axis_index("seq"), lax.axis_index("head")
    place = shards - 1 - seq if backward else seq
    steps = [1 << k for k in range((shards - 1).bit_length())]

    def peer(distance):
        return lax.rem(seq + shards + distance, shards)

    sign = -1 if backward else 1
    greet([(peer(-sign * d), head) for d in steps], len(steps))

    def apply(trans, state):
        return mm(trans, state, 0, 0) if backward else mm(trans, state)

    def join(late, early):
        return mm(early, late) if backward else mm(late, early)

    for k, d in enumerate(steps):
        final = k == len(steps) - 1
        copies = []
        for part in range(1 if final else 2):
            if k == 0:
                src = state_ref if part == 0 else trans_ref
            else:
                src = stage_ref.at[k - 1, part]
            copies.append(
                remote(src, got_ref.at[k, part], send.at[k, part], recv.at[k, part], peer(sign * d), head)
            )
        for c in copies:
            c.start()
        for c in copies:
            c.wait_recv()
        here = (place >= d).astype(F32)

        @pl.loop(0, groups)
        def _(g, k=k, final=final, here=here):
            state = got_ref[k, 0, g].astype(F32) * here
            if k == 0:
                out_ref[g] = state
            else:
                out_ref[g] += apply(tx_ref[g], state)
            if not final:
                trans = got_ref[k, 1, g].astype(F32) * here
                if k == 0:
                    old_t, old_s = trans_ref[g].astype(F32), state_ref[g].astype(F32)
                    tx_ref[g] = trans.astype(BF16)
                else:
                    old_t, old_s = t_ref[g], s_ref[g]
                    tx_ref[g] = join(tx_ref[g], trans).astype(BF16)
                new_s = old_s + apply(old_t, state)
                new_t = join(old_t, trans)
                s_ref[g] = new_s
                t_ref[g] = new_t
                stage_ref[k, 0, g] = new_s.astype(BF16)
                stage_ref[k, 1, g] = new_t.astype(BF16)

        for c in copies:
            c.wait_send()


def compose(trans, state, shards, backward):
    count, heads = state.shape[:2]
    groups = count * heads
    flat = (groups, HEAD_DIM, HEAD_DIM)
    rounds = (shards - 1).bit_length()
    out = pl.pallas_call(
        functools.partial(compose_body, shards, backward),
        in_specs=vmem_specs(2),
        out_specs=vmem_specs(1)[0],
        out_shape=jax.ShapeDtypeStruct(flat, F32),
        scratch_shapes=[
            pltpu.VMEM((max(rounds - 1, 1), 2) + flat, BF16),
            pltpu.VMEM((rounds, 2) + flat, BF16),
            pltpu.VMEM(flat, BF16),
            pltpu.VMEM(flat, F32),
            pltpu.VMEM(flat, F32),
            pltpu.SemaphoreType.DMA((rounds, 2)),
            pltpu.SemaphoreType.DMA((rounds, 2)),
        ],
        compiler_params=comm_params(5 if backward else 4),
        name="compose_back" if backward else "compose",
    )(trans.reshape(flat), state.reshape(flat))
    return out.reshape(state.shape)


def per_device(
    inputs, attn_gain, mixer_weights, beta_weight, filter_weights, out_gain, dense_gain, dense_weights,
    seq_offsets, seq_lengths, out_grad,
):
    count, local_rows, width = inputs.shape
    heads, shards = lax.axis_size("head"), lax.axis_size("seq")
    rows = local_rows * heads
    base = (lax.axis_index("seq") * rows).astype(jnp.int32).reshape(1)
    taps = filter_weights.astype(F32)
    gain_row = out_gain.reshape(1, HEAD_DIM)
    attn_row = attn_gain.reshape(1, width)
    dense_row = dense_gain.reshape(1, width)
    dense_full = lax.all_gather(dense_weights, "seq", axis=1, tiled=True)
    grad_top = lax.all_gather(out_grad, "head", axis=1, tiled=True)

    x_ext = norm_gather(inputs, attn_row, heads, shards)
    pq, pk, pv, rates, ps, oloc, phi, psi, score, inv, wr, up, trans, state = mix_fwd(
        seq_offsets, seq_lengths, base, x_ext, mixer_weights, beta_weight, taps
    )
    state_in = compose(trans, state, shards, False)
    start, mixed, head_out, attn_part = mix_out(state_in, ps, oloc, phi, psi, gain_row, mixer_weights)
    resid_mid, dense_in = resid_gather(attn_part, inputs, dense_row)
    down_part, gin_part, dense_part = dense(
        dense_in.reshape(-1, width), grad_top.reshape(-1, width), dense_full
    )
    down = lax.psum_scatter(
        down_part.reshape(count, rows, width), "head", scatter_dimension=1, tiled=True
    ).astype(F32)
    dense_total = lax.psum_scatter(dense_part, "seq", scatter_dimension=1, tiled=True).astype(F32)
    output = (resid_mid + down).astype(BF16)
    grad_mid, grad_attn, dense_gain_part = grad_gather(
        gin_part.reshape(count, rows, width), resid_mid, out_grad, dense_row
    )
    dout, out_gain_part, dstate = mix_back(grad_attn, mixer_weights, mixed, gain_row, ps, phi)
    dend = compose(trans, dstate, shards, True)
    gq, gk, gv, tail, rim, grate, filter_part = mix_grad(
        seq_offsets, seq_lengths, base, (pq, pk, pv), rates, taps, dend, dout, start, ps, phi, score, inv, wr, up
    )
    rim_next = shifted(rim, "seq", -1)
    gx_part, mixer_part, beta_part = proj_back(
        (gq, gk, gv), tail, rim_next, grate, x_ext, mixer_weights, beta_weight, grad_attn, head_out
    )
    input_grad, attn_gain_part = last_scatter(gx_part, inputs, grad_mid, attn_row)
    mixer_total = lax.psum(mixer_part, "seq").astype(F32)
    beta_total, filter_total = lax.psum((beta_part, filter_part), "seq")
    attn_gain_total, out_gain_total, dense_gain_total = lax.psum(
        (attn_gain_part.reshape(width), out_gain_part.reshape(HEAD_DIM), dense_gain_part.reshape(width)), ("seq", "head")
    )
    return (
        output, input_grad, attn_gain_total, mixer_total, beta_total, filter_total, out_gain_total,
        dense_gain_total, dense_total,
    )


def solution(mesh):
    rows = P(None, ("seq", "head"), None)
    return jax.shard_map(
        per_device,
        mesh=mesh,
        in_specs=(
            rows, P(), P(None, None, "head"), P(None, "head"), P(None, None, "head"), P(), P(),
            P(None, "seq", "head"), P(), P(), rows,
        ),
        out_specs=(
            rows, rows, P(), P(None, None, "head"), P(None, "head"), P(None, None, "head"), P(), P(),
            P(None, "seq", "head"),
        ),
        check_vma=False,
    )
```

```python
import functools

import jax
import jax.numpy as jnp
from jax import lax
from jax.experimental import pallas as pl
from jax.experimental.pallas import tpu as pltpu
from jax.sharding import PartitionSpec as P

HEAD_DIM = 128
CONV = 4
CHUNK = 128
HALO = 16
RIM = 8
EPS = 1e-06
F32 = jnp.float32
BF16 = jnp.bfloat16
VMEM_LIMIT = 56 * 1024 * 1024


def mm(a, b, ca=1, cb=0):
    return lax.dot_general(
        a.astype(BF16), b.astype(BF16), (((ca,), (cb,)), ((), ())), preferred_element_type=F32
    )


def split(a):
    high = a.astype(BF16)
    return high, (a - high.astype(F32)).astype(BF16)


def mm3(a, b, ca=1, cb=0):
    ah, al = split(a)
    bh, bl = split(b)
    return mm(ah, bh, ca, cb) + (mm(ah, bl, ca, cb) + mm(al, bh, ca, cb))


def sigmoid(v):
    return 1.0 / (1.0 + jnp.exp(-v))


def row_info(off_ref, len_ref, m, base, rows):
    t = base + lax.broadcasted_iota(jnp.int32, (rows, 1), 0)
    start = jnp.zeros_like(t)
    length = jnp.zeros_like(t)
    for i in range(off_ref.shape[1]):
        inside = t >= off_ref[m, i]
        start = jnp.where(inside, off_ref[m, i], start)
        length = jnp.where(inside, len_ref[m, i], length)
    rel = t - start
    return rel, (rel < length).astype(F32)


def chunk_masks(rel):
    n = rel.shape[0]
    i = lax.broadcasted_iota(jnp.int32, (n, n), 0)
    j = lax.broadcasted_iota(jnp.int32, (n, n), 1)
    same = rel >= i - j
    strict = jnp.logical_and(same, i > j)
    incl = jnp.logical_and(same, i >= j)
    col = lax.broadcasted_iota(jnp.int32, (n, 1), 0)
    sees = (rel > col).astype(F32)
    last = rel[n - 1 : n, :]
    stays = ((n - 1 - col) <= last).astype(F32)
    keep = (last > n - 1).astype(F32)
    return strict, incl, sees, stays, keep


def unit_lower_inverse(a_list):
    n = a_list[0].shape[0]
    i = lax.broadcasted_iota(jnp.int32, (n, n), 0)
    j = lax.broadcasted_iota(jnp.int32, (n, n), 1)
    eye = (i == j).astype(F32)
    size = 1
    inv_list = [eye for _ in a_list]
    while size < n:
        pair = jnp.logical_and(i // size == j // size + 1, (i // size) % 2 == 1)
        below = [jnp.where(pair, a, 0.0) for a in a_list]
        if size == 1:
            inv_list = [eye - b for b in below]
        else:
            half = [mm3(b, inv) for b, inv in zip(below, inv_list)]
            inv_list = [inv - mm3(inv, h) for inv, h in zip(inv_list, half)]
        size *= 2
    return inv_list


def lagged(ext, lag, rows):
    moved = pltpu.roll(ext, lag, 0) if lag else ext
    return moved[HALO : HALO + rows]


def lag_masks(rel):
    return [None] + [(rel >= lag).astype(F32) for lag in range(1, CONV)]


def filtered(ext, taps, masks, rows):
    total = None
    for lag in range(CONV):
        term = taps[lag : lag + 1, :] * lagged(ext, lag, rows)
        if masks[lag] is not None:
            term = term * masks[lag]
        total = term if total is None else total + term
    return total


def mix_fwd_body(
    off_ref, len_ref, base_ref, x_ref, w_ref, beta_ref, taps_ref,
    pq_ref, pk_ref, pv_ref, rate_ref, ps_ref, oloc_ref, phi_ref, psi_ref, m_ref, inv_ref, wr_ref, up_ref, trans_ref, state_ref,
):
    mb = pl.program_id(0)
    head = pl.program_id(1)
    rows = x_ref.shape[1] - HALO
    rel, valid = row_info(off_ref, len_ref, mb, base_ref[0], rows)
    x = x_ref[0]
    masks = lag_masks(rel)
    acts = []
    for member, out in enumerate((pq_ref, pk_ref, pv_ref)):
        proj = mm(x, w_ref[member]).astype(BF16)
        out[0] = proj
        filt = filtered(proj.astype(F32), taps_ref[member].astype(F32), masks, rows)
        acts.append(filt * sigmoid(filt))
    query, key, value = acts
    query = query * lax.rsqrt(jnp.sum(query * query, axis=-1, keepdims=True) + EPS)
    key = key * lax.rsqrt(jnp.sum(key * key, axis=-1, keepdims=True) + EPS)
    raw_all = mm(x, beta_ref[...], 1, 1)[HALO:]
    lane = lax.broadcasted_iota(jnp.int32, raw_all.shape, 1)
    raw = jnp.sum(jnp.where(lane == head, raw_all, 0.0), axis=-1, keepdims=True)
    rate_ref[0, 0] = raw
    rate = sigmoid(raw) * valid
    spans = [slice(c * CHUNK, (c + 1) * CHUNK) for c in range(rows // CHUNK)]
    all_masks = [chunk_masks(rel[s]) for s in spans]
    systems, scores = [], []
    for s, (strict, incl, _, _, _) in zip(spans, all_masks):
        both = mm(jnp.concatenate([query[s], key[s]], axis=0), key[s], 1, 1)
        scores.append(jnp.where(incl, both[:CHUNK], 0.0))
        systems.append(jnp.where(strict, rate[s] * both[CHUNK:], 0.0))
    inverses = unit_lower_inverse(systems)
    i = lax.broadcasted_iota(jnp.int32, (HEAD_DIM, HEAD_DIM), 0)
    j = lax.broadcasted_iota(jnp.int32, (HEAD_DIM, HEAD_DIM), 1)
    eye = (i == j).astype(F32)
    phis, psis, ps, olocs = [], [], [], []
    for s, masks_c, inv, score in zip(spans, all_masks, inverses, scores):
        _, _, sees, stays, keep = masks_c
        right = rate[s] * jnp.concatenate([sees * key[s], value[s]], axis=1)
        solved = mm(inv, right)
        write, update = solved[:, :HEAD_DIM], solved[:, HEAD_DIM:]
        moved = mm(stays * key[s], solved, 0, 0)
        phi = keep * eye - moved[:, :HEAD_DIM]
        psi = moved[:, HEAD_DIM:]
        scored = mm(score, solved)
        p = sees * query[s] - scored[:, :HEAD_DIM]
        m_ref[0, 0, s] = score.astype(BF16)
        inv_ref[0, 0, s] = inv.astype(BF16)
        wr_ref[0, 0, s] = write.astype(BF16)
        up_ref[0, 0, s] = update
        ps_ref[0, 0, s] = p.astype(BF16)
        oloc_ref[0, 0, s] = scored[:, HEAD_DIM:]
        phi_ref[0, 0, s] = phi
        psi_ref[0, 0, s] = psi
        phis.append(phi)
        psis.append(psi)
    trans, state = phis[0], psis[0]
    for phi, psi in zip(phis[1:], psis[1:]):
        both = mm3(phi, jnp.concatenate([trans, state], axis=1))
        trans = both[:, :HEAD_DIM]
        state = both[:, HEAD_DIM:] + psi
    trans_ref[0, 0] = trans.astype(BF16)
    state_ref[0, 0] = state.astype(BF16)


def cost(us):
    return pl.CostEstimate(flops=0, bytes_accessed=int(us * 3.0e6), transcendentals=0)


def smem_spec():
    return pl.BlockSpec(memory_space=pltpu.SMEM)


def params(count):
    return pltpu.CompilerParams(
        dimension_semantics=("arbitrary",) * count, vmem_limit_bytes=VMEM_LIMIT
    )


def mix_fwd(offsets, lengths, base, x_ext, mixer_weights, beta_weight, taps):
    count, ext_rows, width = x_ext.shape
    rows = ext_rows - HALO
    heads = beta_weight.shape[0]
    per_head = pl.BlockSpec((1, 1, rows, HEAD_DIM), lambda m, h: (m, h, 0, 0))
    proj_spec = pl.BlockSpec((1, ext_rows, HEAD_DIM), lambda m, h: (m, 0, h))
    proj_shape = jax.ShapeDtypeStruct((count, ext_rows, heads * HEAD_DIM), BF16)

    def big(kind):
        return jax.ShapeDtypeStruct((count, heads, rows, HEAD_DIM), kind)

    return pl.pallas_call(
        mix_fwd_body,
        grid=(count, heads),
        in_specs=[
            smem_spec(), smem_spec(), smem_spec(),
            pl.BlockSpec((1, ext_rows, width), lambda m, h: (m, 0, 0)),
            pl.BlockSpec((3, width, HEAD_DIM), lambda m, h: (0, 0, h)),
            pl.BlockSpec(beta_weight.shape, lambda m, h: (0, 0)),
            pl.BlockSpec((3, CONV, HEAD_DIM), lambda m, h: (0, 0, h)),
        ],
        out_specs=[proj_spec] * 3
        + [pl.BlockSpec((1, 1, rows, 1), lambda m, h: (m, h, 0, 0))]
        + [per_head] * 8
        + [pl.BlockSpec((1, 1, HEAD_DIM, HEAD_DIM), lambda m, h: (m, h, 0, 0))] * 2,
        out_shape=[proj_shape] * 3
        + [jax.ShapeDtypeStruct((count, heads, rows, 1), F32)]
        + [big(BF16), big(F32), big(F32), big(F32), big(BF16), big(BF16), big(BF16), big(F32)]
        + [jax.ShapeDtypeStruct((count, heads, HEAD_DIM, HEAD_DIM), BF16)] * 2,
        compiler_params=params(2),
        cost_estimate=cost(23),
        name="mix_fwd",
    )(offsets, lengths, base, x_ext, mixer_weights, beta_weight, taps)


def mix_out_body(state_ref, ps_ref, oloc_ref, phi_ref, psi_ref, gain_ref, w_ref, start_ref, mixed_ref, head_ref, part_ref):
    heads = ps_ref.shape[1]
    rows = ps_ref.shape[2]
    gain = gain_ref[...]
    states = [state_ref[0, h] for h in range(heads)]
    for c in range(rows // CHUNK):
        s = slice(c * CHUNK, (c + 1) * CHUNK)
        for h in range(heads):
            state = states[h]
            start_ref[0, h, s] = state.astype(BF16)
            mixed = oloc_ref[0, h, s] + mm(ps_ref[0, h, s], state)
            mixed_ref[0, h, s] = mixed
            normed = mixed * lax.rsqrt(jnp.mean(mixed * mixed, axis=-1, keepdims=True) + EPS) * gain
            head_ref[0, s, h * HEAD_DIM : (h + 1) * HEAD_DIM] = normed.astype(BF16)
            states[h] = mm3(phi_ref[0, h, s], state) + psi_ref[0, h, s]
    part_ref[0] = mm(head_ref[0], w_ref[0], 1, 1).astype(BF16)


def mix_out(state_in, ps, oloc, phi, psi, out_gain, mixer_weights):
    count, heads, rows, _ = ps.shape
    width = mixer_weights.shape[1]
    head_width = mixer_weights.shape[2]
    per_mb = pl.BlockSpec((1, heads, rows, HEAD_DIM), lambda m: (m, 0, 0, 0))
    return pl.pallas_call(
        mix_out_body,
        grid=(count,),
        in_specs=[
            pl.BlockSpec((1, heads, HEAD_DIM, HEAD_DIM), lambda m: (m, 0, 0, 0)),
            per_mb, per_mb, per_mb, per_mb,
            pl.BlockSpec((1, HEAD_DIM), lambda m: (0, 0)),
            pl.BlockSpec((1, width, head_width), lambda m: (3, 0, 0)),
        ],
        out_specs=[
            per_mb, per_mb,
            pl.BlockSpec((1, rows, head_width), lambda m: (m, 0, 0)),
            pl.BlockSpec((1, rows, width), lambda m: (m, 0, 0)),
        ],
        out_shape=[
            jax.ShapeDtypeStruct(ps.shape, BF16),
            jax.ShapeDtypeStruct(ps.shape, F32),
            jax.ShapeDtypeStruct((count, rows, head_width), BF16),
            jax.ShapeDtypeStruct((count, rows, width), BF16),
        ],
        compiler_params=params(1),
        cost_estimate=cost(5),
        name="mix_out",
    )(state_in, ps, oloc, phi, psi, out_gain, mixer_weights)


def mix_back_body(grad_ref, w_ref, mixed_ref, gain_ref, ps_ref, phi_ref, dout_ref, gain_grad_ref, dstate_ref):
    heads = ps_ref.shape[1]
    rows = ps_ref.shape[2]
    gain = gain_ref[...]
    grad_head = mm(grad_ref[0], w_ref[0])
    gain_grad = jnp.zeros((1, HEAD_DIM), F32)
    douts = []
    for h in range(heads):
        e = grad_head[:, h * HEAD_DIM : (h + 1) * HEAD_DIM]
        v = mixed_ref[0, h]
        r = lax.rsqrt(jnp.mean(v * v, axis=-1, keepdims=True) + EPS)
        weighted = e * gain
        dout = r * weighted - v * (r * r * r * jnp.mean(weighted * v, axis=-1, keepdims=True))
        gain_grad += jnp.sum(e * v * r, axis=0, keepdims=True)
        dout = dout.astype(BF16)
        dout_ref[0, h] = dout
        douts.append(dout)
    states = [None] * heads
    for c in reversed(range(rows // CHUNK)):
        s = slice(c * CHUNK, (c + 1) * CHUNK)
        for h in range(heads):
            new = mm(ps_ref[0, h, s], douts[h][s], 0, 0)
            if states[h] is not None:
                new += mm3(phi_ref[0, h, s], states[h], 0, 0)
            states[h] = new
    for h in range(heads):
        dstate_ref[0, h] = states[h].astype(BF16)

    @pl.when(pl.program_id(0) == 0)
    def _():
        gain_grad_ref[...] = gain_grad

    @pl.when(pl.program_id(0) > 0)
    def _():
        gain_grad_ref[...] += gain_grad


def mix_back(grad_attn, mixer_weights, mixed, out_gain, ps, phi):
    count, heads, rows, _ = ps.shape
    width = mixer_weights.shape[1]
    head_width = mixer_weights.shape[2]
    per_mb = pl.BlockSpec((1, heads, rows, HEAD_DIM), lambda m: (m, 0, 0, 0))
    return pl.pallas_call(
        mix_back_body,
        grid=(count,),
        in_specs=[
            pl.BlockSpec((1, rows, width), lambda m: (m, 0, 0)),
            pl.BlockSpec((1, width, head_width), lambda m: (3, 0, 0)),
            per_mb,
            pl.BlockSpec((1, HEAD_DIM), lambda m: (0, 0)),
            per_mb, per_mb,
        ],
        out_specs=[
            per_mb,
            pl.BlockSpec((1, HEAD_DIM), lambda m: (0, 0)),
            pl.BlockSpec((1, heads, HEAD_DIM, HEAD_DIM), lambda m: (m, 0, 0, 0)),
        ],
        out_shape=[
            jax.ShapeDtypeStruct(ps.shape, BF16),
            jax.ShapeDtypeStruct((1, HEAD_DIM), F32),
            jax.ShapeDtypeStruct((count, heads, HEAD_DIM, HEAD_DIM), BF16),
        ],
        compiler_params=params(1),
        cost_estimate=cost(6),
        name="mix_back",
    )(grad_attn, mixer_weights, mixed, out_gain, ps, phi)


def mix_grad_body(
    off_ref, len_ref, base_ref, pq_ref, pk_ref, pv_ref, rate_ref, taps_ref, dend_ref, dout_ref, start_ref, ps_ref, phi_ref,
    m_ref, inv_ref, wr_ref, up_ref,
    gq_ref, gk_ref, gv_ref, tail_ref, rim_ref, grate_ref, gtaps_ref,
):
    mb = pl.program_id(1)
    rows = rate_ref.shape[2]
    rel, valid = row_info(off_ref, len_ref, mb, base_ref[0], rows)
    masks = lag_masks(rel)
    projs, filts, sigs, acts = [], [], [], []
    for member, ref in enumerate((pq_ref, pk_ref, pv_ref)):
        proj = ref[0].astype(F32)
        filt = filtered(proj, taps_ref[member].astype(F32), masks, rows)
        sg = sigmoid(filt)
        projs.append(proj)
        filts.append(filt)
        sigs.append(sg)
        acts.append(filt * sg)
    rq = lax.rsqrt(jnp.sum(acts[0] * acts[0], axis=-1, keepdims=True) + EPS)
    rk = lax.rsqrt(jnp.sum(acts[1] * acts[1], axis=-1, keepdims=True) + EPS)
    query = acts[0] * rq
    key = acts[1] * rk
    value = acts[2]
    sig_rate = sigmoid(rate_ref[0, 0])
    rate = sig_rate * valid
    dstate = dend_ref[0, 0]
    spans = [slice(c * CHUNK, (c + 1) * CHUNK) for c in range(rows // CHUNK)]
    dstates = [None] * len(spans)
    for c in reversed(range(len(spans))):
        s = spans[c]
        dstates[c] = dstate
        if c:
            dstate = mm3(phi_ref[0, 0, s], dstate, 0, 0) + mm(ps_ref[0, 0, s], dout_ref[0, 0, s], 0, 0)
    dqs, dks, dvs, drates = [], [], [], []
    for c, s in enumerate(spans):
        strict, incl, sees, stays, _ = chunk_masks(rel[s])
        q, k, v, b = query[s], key[s], value[s], rate[s]
        dout = dout_ref[0, 0, s]
        start = start_ref[0, 0, s]
        fresh = up_ref[0, 0, s] - mm(wr_ref[0, 0, s], start)
        dfresh = mm(m_ref[0, 0, s], dout, 0, 0) + mm(stays * k, dstates[c])
        e = mm(inv_ref[0, 0, s], dfresh, 0, 0)
        left = jnp.concatenate([dout, e.astype(BF16)], axis=0)
        right = jnp.concatenate([fresh.astype(BF16), start], axis=0)
        outer = mm(left, right, 1, 1)
        dscore = jnp.where(incl, outer[:CHUNK, :CHUNK], 0.0)
        dsystem = jnp.where(strict, -outer[CHUNK:, :CHUNK], 0.0)
        grads = jnp.concatenate([dscore, dsystem], axis=0).astype(BF16)
        byk = mm(grads, k)
        z = byk[CHUNK:] - sees * outer[CHUNK:, CHUNK:]
        dqs.append(sees * outer[:CHUNK, CHUNK:] + byk[:CHUNK])
        dk = mm(grads, jnp.concatenate([q, b * k], axis=0), 0, 0)
        dks.append(dk + stays * mm(fresh, dstates[c], 1, 1) + b * z)
        dvs.append(b * e)
        drates.append(jnp.sum(e * v + k * z, axis=-1, keepdims=True))
    dq = jnp.concatenate(dqs, axis=0)
    dk = jnp.concatenate(dks, axis=0)
    dv = jnp.concatenate(dvs, axis=0)
    drate = jnp.concatenate(drates, axis=0)
    grate_ref[0, 0] = drate * valid * sig_rate * (1.0 - sig_rate)
    dacts = [
        rq * dq - acts[0] * (rq * rq * rq * jnp.sum(dq * acts[0], axis=-1, keepdims=True)),
        rk * dk - acts[1] * (rk * rk * rk * jnp.sum(dk * acts[1], axis=-1, keepdims=True)),
        dv,
    ]
    for member, out in enumerate((gq_ref, gk_ref, gv_ref)):
        sg = sigs[member]
        dfilt = dacts[member] * (sg * (1.0 + filts[member] * (1.0 - sg)))
        taps = taps_ref[member].astype(F32)
        total = None
        pieces = []
        for lag in range(CONV):
            masked = dfilt if lag == 0 else dfilt * masks[lag]
            pieces.append(jnp.sum(masked * lagged(projs[member], lag, rows), axis=0, keepdims=True))
            scaled = masked * taps[lag : lag + 1, :]
            ext = jnp.concatenate([jnp.zeros((RIM, HEAD_DIM), F32), scaled], axis=0)
            if lag:
                ext = pltpu.roll(ext, rows + RIM - lag, 0)
            total = ext if total is None else total + ext
        here = total[RIM:]
        out[0] = here.astype(BF16)
        tail_ref[0, member] = here[rows - RIM :]
        rim_ref[0, member] = total[:RIM]
        gt = jnp.concatenate(pieces, axis=0)

        @pl.when(mb == 0)
        def _(gt=gt, member=member):
            gtaps_ref[member] = gt

        @pl.when(mb > 0)
        def _(gt=gt, member=member):
            gtaps_ref[member] += gt


def mix_grad(offsets, lengths, base, proj3, rates, taps, dend, dout, start, ps, phi, m, inv, wr, up):
    count, heads, rows, _ = ps.shape
    ext_rows = rows + HALO
    per_head = pl.BlockSpec((1, 1, rows, HEAD_DIM), lambda h, m: (m, h, 0, 0))
    proj_spec = pl.BlockSpec((1, ext_rows, HEAD_DIM), lambda h, m: (m, 0, h))
    out_spec = pl.BlockSpec((1, rows, HEAD_DIM), lambda h, m: (m, 0, h))
    rate_spec = pl.BlockSpec((1, 1, rows, 1), lambda h, m: (m, h, 0, 0))
    taps_spec = pl.BlockSpec((3, CONV, HEAD_DIM), lambda h, m: (0, 0, h))
    small = pl.BlockSpec((1, 3, RIM, HEAD_DIM), lambda h, m: (m, 0, 0, h))
    small_shape = jax.ShapeDtypeStruct((count, 3, RIM, heads * HEAD_DIM), F32)
    return pl.pallas_call(
        mix_grad_body,
        grid=(heads, count),
        in_specs=[
            smem_spec(), smem_spec(), smem_spec(),
            proj_spec, proj_spec, proj_spec, rate_spec, taps_spec,
            pl.BlockSpec((1, 1, HEAD_DIM, HEAD_DIM), lambda h, m: (m, h, 0, 0)),
        ]
        + [per_head] * 8,
        out_specs=[out_spec] * 3 + [small, small, rate_spec, taps_spec],
        out_shape=[jax.ShapeDtypeStruct((count, rows, heads * HEAD_DIM), BF16)] * 3
        + [
            small_shape, small_shape,
            jax.ShapeDtypeStruct(rates.shape, F32),
            jax.ShapeDtypeStruct(taps.shape, F32),
        ],
        compiler_params=params(2),
        cost_estimate=cost(17),
        name="mix_grad",
    )(offsets, lengths, base, *proj3, rates, taps, dend, dout, start, ps, phi, m, inv, wr, up)


def proj_back_body(
    gq_ref, gk_ref, gv_ref, tail_ref, rim_ref, grate_ref, x_ref, w_ref, beta_ref, gattn_ref, head_ref,
    gx_ref, gw_ref, gbeta_ref, acc_ref,
):
    step = pl.program_id(0)
    rows = gq_ref.shape[1]
    heads = grate_ref.shape[1]
    lane = lax.broadcasted_iota(jnp.int32, (rows, heads), 1)
    grate = jnp.zeros((rows, heads), F32)
    for h in range(heads):
        grate = jnp.where(lane == h, grate_ref[0, h], grate)
    x = x_ref[0, HALO:, :]
    total = mm(grate, beta_ref[...])
    adds = []
    for member, ref in enumerate((gq_ref, gk_ref, gv_ref)):
        last = (tail_ref[0, member] + rim_ref[0, member]).astype(BF16)
        g = jnp.concatenate([ref[0, : rows - RIM], last], axis=0)
        total += mm(g, w_ref[member], 1, 1)
        adds.append(mm(x, g, 0, 0))
    adds.append(mm(gattn_ref[0], head_ref[0], 0, 0))
    gx_ref[0] = total.astype(BF16)
    gb = mm(grate, x, 0, 0)

    @pl.when(step == 0)
    def _():
        for member in range(4):
            acc_ref[member] = adds[member]
        gbeta_ref[...] = gb

    @pl.when(step > 0)
    def _():
        for member in range(4):
            acc_ref[member] += adds[member]
        gbeta_ref[...] += gb

    @pl.when(step == pl.num_programs(0) - 1)
    def _():
        gw_ref[...] = acc_ref[...].astype(BF16)


def proj_back(g3, tail, rim, grate, x_ext, mixer_weights, beta_weight, grad_attn, head_out):
    count, rows, head_width = g3[0].shape
    ext_rows, width = x_ext.shape[1:]
    heads = beta_weight.shape[0]
    g_spec = pl.BlockSpec((1, rows, head_width), lambda m: (m, 0, 0))
    small = pl.BlockSpec((1, 3, RIM, head_width), lambda m: (m, 0, 0, 0))
    row_spec = pl.BlockSpec((1, rows, width), lambda m: (m, 0, 0))
    return pl.pallas_call(
        proj_back_body,
        grid=(count,),
        in_specs=[
            g_spec, g_spec, g_spec, small, small,
            pl.BlockSpec((1, heads, rows, 1), lambda m: (m, 0, 0, 0)),
            pl.BlockSpec((1, ext_rows, width), lambda m: (m, 0, 0)),
            pl.BlockSpec((3, width, head_width), lambda m: (0, 0, 0)),
            pl.BlockSpec((heads, width), lambda m: (0, 0)),
            row_spec, g_spec,
        ],
        out_specs=[
            row_spec,
            pl.BlockSpec((4, width, head_width), lambda m: (0, 0, 0)),
            pl.BlockSpec((heads, width), lambda m: (0, 0)),
        ],
        out_shape=[
            jax.ShapeDtypeStruct((count, rows, width), BF16),
            jax.ShapeDtypeStruct((4, width, head_width), BF16),
            jax.ShapeDtypeStruct((heads, width), F32),
        ],
        scratch_shapes=[pltpu.VMEM((4, width, head_width), F32)],
        compiler_params=params(1),
        cost_estimate=cost(11),
        name="proj_back",
    )(*g3, tail, rim, grate, x_ext, mixer_weights, beta_weight, grad_attn, head_out)


def shifted(block, axis, distance):
    count = lax.axis_size(axis)
    return lax.ppermute(block, axis, [(i, (i + distance) % count) for i in range(count)])


def rms(values, gain):
    return values * lax.rsqrt(jnp.mean(values * values, axis=-1, keepdims=True) + EPS) * gain


def rms_back(grad, values, gain):
    inv = lax.rsqrt(jnp.mean(values * values, axis=-1, keepdims=True) + EPS)
    weighted = grad * gain
    grad_in = inv * weighted - values * inv**3 * jnp.mean(weighted * values, axis=-1, keepdims=True)
    return grad_in, jnp.sum(grad * values * inv, axis=0, keepdims=True)

MESH = pl.DeviceIdType.MESH


def flip(index, bit):
    return index + bit * (1 - 2 * (index // bit % 2))


def remote(src, dst, send, recv, seq, head):
    return pltpu.make_async_remote_copy(
        src_ref=src, dst_ref=dst, send_sem=send, recv_sem=recv, device_id=(seq, head), device_id_type=MESH
    )


def greet(devices, expected):
    barrier = pltpu.get_barrier_semaphore()
    for seq, head in devices:
        pl.semaphore_signal(barrier, inc=1, device_id=(seq, head), device_id_type=MESH)
    pl.semaphore_wait(barrier, expected)


class Pieces:
    def __init__(self, count, local):
        self.local = local
        self.per = local // PIECE
        self.total = count * self.per
        self.seq, self.head = lax.axis_index("seq"), lax.axis_index("head")
        self.far, self.near = flip(self.head, 2), flip(self.head, 1)

    def mine(self, k):
        return k // self.per, pl.ds(pl.multiple_of(k % self.per * PIECE, PIECE), PIECE)

    def block(self, ref, k, owner, tiled, first=0):
        if tiled:
            return ref.at[k, pl.ds(pl.multiple_of(owner * PIECE, PIECE), PIECE), :]
        start = first + owner * self.local + k % self.per * PIECE
        return ref.at[k // self.per, pl.ds(pl.multiple_of(start, 16), PIECE), :]


class HeadGather:
    def __init__(self, pieces, out_ref, tiled, first, send, recv):
        self.pieces, self.out, self.tiled, self.first = pieces, out_ref, tiled, first
        self.send, self.recv = send, recv

    def place(self, k, owner):
        return self.pieces.block(self.out, k, owner, self.tiled, self.first)

    def copy(self, kind, k):
        p = self.pieces
        owner = p.far if kind == 2 else p.head
        target = p.near if kind else p.far
        ref = self.place(k, owner)
        return remote(ref, ref, self.send.at[kind, k], self.recv.at[kind, k], p.seq, target)

    def own(self, k):
        self.copy(0, k).start()
        self.copy(1, k).start()

    def forward(self, k):
        self.copy(0, k).wait_recv()
        self.copy(2, k).start()

    def arrived(self, k):
        self.copy(1, k).wait_recv()
        self.copy(2, k).wait_recv()

    def sent(self, k):
        for kind in range(3):
            self.copy(kind, k).wait_send()


class HeadScatter:
    def __init__(self, pieces, part_ref, tiled, near_ref, stage_ref, far_ref, send, recv):
        self.pieces, self.part, self.tiled = pieces, part_ref, tiled
        self.nearby, self.stage, self.faraway = near_ref, stage_ref, far_ref
        self.send, self.recv = send, recv

    def block(self, k, owner):
        return self.pieces.block(self.part, k, owner, self.tiled)

    def copy(self, kind, k):
        p = self.pieces
        if kind == 2:
            return remote(
                self.stage.at[k], self.faraway.at[k], self.send.at[2, k], self.recv.at[2, k], p.seq, p.far
            )
        owner = p.near if kind else flip(p.near, 2)
        return remote(
            self.block(k, owner), self.nearby.at[kind, k], self.send.at[kind, k], self.recv.at[kind, k], p.seq, p.near
        )

    def start(self, k):
        self.copy(0, k).start()
        self.copy(1, k).start()

    def forward(self, k):
        self.copy(0, k).wait_recv()
        total = self.block(k, self.pieces.far)[...].astype(F32) + self.nearby[0, k].astype(F32)
        self.stage[k] = total.astype(BF16)
        self.copy(2, k).start()

    def total(self, k):
        self.copy(1, k).wait_recv()
        self.copy(2, k).wait_recv()
        near = self.block(k, self.pieces.head)[...].astype(F32) + self.nearby[1, k].astype(F32)
        return near + self.faraway[k].astype(F32)

    def sent(self, k):
        for kind in range(3):
            self.copy(kind, k).wait_send()


def each(count, *steps):
    for step in steps:
        pl.loop(0, count)(step)


def scatter_scratch(count, local, width):
    n = count * local // PIECE
    return [
        pltpu.VMEM((2, n, PIECE, width), BF16),
        pltpu.VMEM((n, PIECE, width), BF16),
        pltpu.VMEM((n, PIECE, width), BF16),
        pltpu.SemaphoreType.DMA((3, n)),
        pltpu.SemaphoreType.DMA((3, n)),
    ]


def gather_scratch(count, local):
    n = count * local // PIECE
    return [pltpu.SemaphoreType.DMA((3, n)), pltpu.SemaphoreType.DMA((3, n))]


def vmem_specs(count):
    return [pl.BlockSpec(memory_space=pltpu.VMEM)] * count


def comm_params(collective):
    return pltpu.CompilerParams(
        collective_id=collective, has_side_effects=True, vmem_limit_bytes=VMEM_LIMIT
    )


PIECE = 64


def norm_gather_body(heads, shards, x_ref, gain_ref, out_ref, send, recv, halo_send, halo_recv):
    count, local, _ = x_ref.shape
    pieces = Pieces(count, local)
    seq, head = pieces.seq, pieces.head
    after = lax.rem(seq + 1, shards)
    before = lax.rem(seq + shards - 1, shards)
    last = head == heads - 1
    gather = HeadGather(pieces, out_ref, False, HALO, send, recv)
    for k in range(pieces.total):
        m, here = pieces.mine(k)
        x = x_ref[m, here, :].astype(F32)
        gather.place(k, head)[...] = rms(x, gain_ref[...]).astype(BF16)
    greet(
        [(seq, pieces.far), (seq, pieces.near), (before, heads - 1)],
        2 + heads * last.astype(jnp.int32),
    )
    each(pieces.total, gather.own)

    def halo(target):
        src = out_ref.at[:, pl.ds(heads * local, HALO), :]
        return remote(src, out_ref.at[:, pl.ds(0, HALO), :], halo_send.at[target], halo_recv, after, target)

    @pl.when(last)
    def _():
        for target in range(heads):
            halo(target).start()

    each(pieces.total, gather.forward, gather.arrived, gather.sent)
    halo(0).wait_recv()

    @pl.when(last)
    def _():
        for target in range(heads):
            halo(target).wait_send()


def norm_gather(inputs, gain, heads, shards):
    count, local, width = inputs.shape
    return pl.pallas_call(
        functools.partial(norm_gather_body, heads, shards),
        in_specs=vmem_specs(2),
        out_specs=vmem_specs(1)[0],
        out_shape=jax.ShapeDtypeStruct((count, HALO + heads * local, width), BF16),
        scratch_shapes=gather_scratch(count, local)
        + [pltpu.SemaphoreType.DMA((heads,)), pltpu.SemaphoreType.DMA],
        compiler_params=comm_params(0),
        cost_estimate=cost(15),
        name="norm_gather",
    )(inputs, gain)


def dense_block_body(
    part_ref, x_ref, top_ref, all_top_ref, gain_ref, w_ref,
    resid_ref, down_ref, grad_ref, mid_ref, out_ref, gain_grad_ref,
    wt_ref, wsem, acc_ref, gh_ref, in_ref, gin_ref, *scratch,
):
    count, local, width = x_ref.shape
    shards = w_ref.shape[0]
    cut = width // shards
    pieces = Pieces(count, local)
    first = HeadScatter(pieces, part_ref, False, *scratch[:5])
    spread = HeadGather(pieces, in_ref, True, 0, *scratch[5:7])
    second = HeadScatter(pieces, gin_ref, True, *scratch[7:12])
    back = HeadGather(pieces, out_ref, False, 0, *scratch[12:14])

    def weights(p):
        return pltpu.make_async_copy(w_ref.at[p], wt_ref.at[:, :, pl.ds(p * cut, cut)], wsem.at[p])

    for p in range(shards):
        weights(p).start()
    greet([(pieces.seq, pieces.far), (pieces.seq, pieces.near)], 2)
    n = pieces.total
    each(n, first.start, first.forward)
    for p in range(shards):
        weights(p).wait()
    gain_grad_ref[...] = jnp.zeros_like(gain_grad_ref)

    @pl.loop(0, n)
    def _(k):
        gh_ref[k] = mm(all_top_ref[k], wt_ref[2], 1, 1)
        m, here = pieces.mine(k)
        resid = x_ref[m, here, :].astype(F32) + first.total(k)
        resid_ref[m, here, :] = resid
        spread.place(k, pieces.head)[...] = rms(resid, gain_ref[...]).astype(BF16)
        spread.own(k)

    def turn_back(k):
        m, here = pieces.mine(k)
        grad, gain_part = rms_back(second.total(k), resid_ref[m, here, :], gain_ref[...])
        mid = top_ref[m, here, :].astype(F32) + grad
        gain_grad_ref[...] += gain_part
        mid_ref[m, here, :] = mid
        back.place(k, pieces.head)[...] = mid.astype(BF16)
        back.own(k)

    spread.forward(0)

    @pl.loop(0, n)
    def _(k):
        spread.arrived(k)
        x = in_ref[k]
        gate = mm(x, wt_ref[0], 1, 1)
        up = mm(x, wt_ref[1], 1, 1)
        grad_hidden = gh_ref[k]
        sg = sigmoid(gate)
        silu = gate * sg
        hidden = (silu * up).astype(BF16)
        grad_gate = (grad_hidden * up * (sg * (1.0 + gate * (1.0 - sg)))).astype(BF16)
        grad_up = (grad_hidden * silu).astype(BF16)
        gin_ref[k] = (mm(grad_gate, wt_ref[0]) + mm(grad_up, wt_ref[1])).astype(BF16)
        second.start(k)

        @pl.when(k + 1 < n)
        def _():
            spread.forward(k + 1)

        down_ref[k] = mm(hidden, wt_ref[2]).astype(BF16)
        second.forward(k)
        adds = (mm(grad_gate, x, 0, 0), mm(grad_up, x, 0, 0), mm(hidden, all_top_ref[k], 0, 0))

        @pl.when(k == 0)
        def _():
            for i, add in enumerate(adds):
                acc_ref[i] = add

        @pl.when(jnp.logical_and(k > 0, k + 1 < n))
        def _():
            for i, add in enumerate(adds):
                acc_ref[i] += add

        @pl.when(k + 1 == n)
        def _():
            for i, add in enumerate(adds):
                total = (acc_ref[i] + add).astype(BF16)
                for p in range(shards):
                    grad_ref[p, i] = total[:, p * cut : (p + 1) * cut]

        @pl.when(k > 0)
        def _():
            turn_back(k - 1)

        @pl.when(k > 1)
        def _():
            back.forward(k - 2)

    turn_back(n - 1)
    back.forward(n - 2)
    back.forward(n - 1)
    each(n, back.arrived, back.sent, second.sent, spread.sent, first.sent)


def dense_block(part, inputs, top, all_top, gain, weights):
    count, local, width = inputs.shape
    shards, _, hidden, cut = weights.shape
    n = count * local // PIECE
    tile = all_top.shape[1]
    rows = part.shape[1]
    return pl.pallas_call(
        dense_block_body,
        in_specs=vmem_specs(5) + [pl.BlockSpec(memory_space=pl.ANY)],
        out_specs=vmem_specs(6),
        out_shape=[
            jax.ShapeDtypeStruct(inputs.shape, F32),
            jax.ShapeDtypeStruct((n, tile, width), BF16),
            jax.ShapeDtypeStruct(weights.shape, BF16),
            jax.ShapeDtypeStruct(inputs.shape, F32),
            jax.ShapeDtypeStruct((count, rows, width), BF16),
            jax.ShapeDtypeStruct((1, width), F32),
        ],
        scratch_shapes=[
            pltpu.VMEM((3, hidden, width), BF16),
            pltpu.SemaphoreType.DMA((shards,)),
            pltpu.VMEM((3, hidden, width), F32),
            pltpu.VMEM((n, tile, hidden), F32),
            pltpu.VMEM((n, tile, width), BF16),
            pltpu.VMEM((n, tile, width), BF16),
        ]
        + (scatter_scratch(count, local, width) + gather_scratch(count, local)) * 2,
        compiler_params=comm_params(1),
        cost_estimate=cost(55),
        name="dense_block",
    )(part, inputs, top, all_top, gain, weights)


class SeqSum:
    def __init__(self, shards, part_ref, work_ref, got_ref, full_ref, send, recv):
        self.part, self.work, self.got, self.full = part_ref, work_ref, got_ref, full_ref
        self.send, self.recv = send, recv
        self.seq, self.head = lax.axis_index("seq"), lax.axis_index("head")
        self.bits = [1 << k for k in range((shards - 1).bit_length())]
        self.members, self.rows = part_ref.shape[0], part_ref.shape[1] // 2
        self.half = 128
        self.chunks = 2 * self.members * (part_ref.shape[2] // self.half)
        self.steps = 2 * len(self.bits)
        self.copies = {}
        self.kept, self.gone = [0], []
        size = self.rows
        for bit in self.bits:
            size //= 2
            mine = self.seq // bit % 2
            self.gone.append(self.kept[-1] + size * (1 - mine))
            self.kept.append(self.kept[-1] + size * mine)

    def view(self, ref, chunk, first, size):
        per = self.chunks // self.members
        first = pl.multiple_of(chunk % 2 * self.rows + first, 8)
        return ref.at[chunk // per, pl.ds(first, size), pl.ds(chunk % per // 2 * self.half, self.half)]

    def begin(self, chunk, step):
        size = self.rows >> (step + 1)
        src = self.view(self.part if step == 0 else self.work, chunk, self.gone[step], size)
        offset = self.rows - 2 * size
        dst = self.view(self.got, chunk, offset, size)
        c = remote(src, dst, self.send.at[step, chunk], self.recv.at[step, chunk], flip(self.seq, self.bits[step]), self.head)
        c.start()
        self.copies[step, chunk] = c

    def fold(self, chunk, step):
        size = self.rows >> (step + 1)
        self.copies[step, chunk].wait_recv()
        got = self.view(self.got, chunk, self.rows - 2 * size, size)
        kept = self.view(self.part if step == 0 else self.work, chunk, self.kept[step + 1], size)
        total = (kept[...].astype(F32) + got[...].astype(F32)).astype(BF16)
        last = step == len(self.bits) - 1
        self.view(self.full if last else self.work, chunk, self.kept[step + 1], size)[...] = total

    def spread(self, chunk, step):
        back = len(self.bits) - 1 - step
        size = self.rows >> (back + 1)
        ref = self.view(self.full, chunk, self.kept[back + 1], size)
        at = len(self.bits) + step
        c = remote(ref, ref, self.send.at[at, chunk], self.recv.at[at, chunk], flip(self.seq, self.bits[back]), self.head)
        c.start()
        self.copies[at, chunk] = c

    def stage(self, chunk, step):
        n = len(self.bits)
        if step > n:
            self.copies[step - 1, chunk].wait_recv()
        elif step > 0:
            self.fold(chunk, step - 1)
        if step < n:
            self.begin(chunk, step)
        elif step < 2 * n:
            self.spread(chunk, step - n)

    def tick(self, t):
        done = []
        for chunk in range(self.chunks):
            step, odd = divmod(t - chunk, 2)
            if not odd and 0 <= step <= self.steps:
                self.stage(chunk, step)
                if step == self.steps:
                    done.append(chunk)
        return done

    def ticks(self):
        return self.chunks + 2 * self.steps

    def finish(self):
        for c in self.copies.values():
            c.wait_send()


def finish_body(
    shards, gx_ref, down_ref, mixer_ref, beta_ref, taps_ref, attn_part_ref, dense_part_ref, out_part_ref,
    x_ref, mid_ref, resid_ref, gain_ref,
    in_grad_ref, output_ref, total_ref, rows_ref, filter_ref, *scratch,
):
    gx_scratch, down_scratch = scratch[:5], scratch[5:10]
    work_ref, got_ref, full_ref, ms, mr, row_got, row_now, tap_got, tap_now, rs, rr, gain_grad_ref = scratch[10:]
    count, local, width = x_ref.shape
    heads = beta_ref.shape[0]
    members = taps_ref.shape[0]
    pieces = Pieces(count, local)
    gx = HeadScatter(pieces, gx_ref, False, *gx_scratch)
    down = HeadScatter(pieces, down_ref, True, *down_scratch)
    total = SeqSum(shards, mixer_ref, work_ref, got_ref, full_ref, ms, mr)
    seq, head = pieces.seq, pieces.head

    row_now[0] = jnp.zeros(row_now.shape[1:], F32)
    tap_now[0] = jnp.zeros(tap_now.shape[1:], F32)
    row_now[0, 0:heads, :] = beta_ref[...]
    row_now[0, heads : heads + 1, :] = dense_part_ref[...]
    row_now[0, heads + 1 : heads + 2, 0:HEAD_DIM] = out_part_ref[...]
    for k in range(members):
        tap_now[0, 8 * k : 8 * k + CONV, :] = taps_ref[k]
    rounds = [(flip(seq, bit), head) for bit in total.bits] + [(seq, flip(head, 2)), (seq, flip(head, 1))]
    greet(rounds, len(rounds))
    small = {}

    def small_start(k):
        small[k] = [
            remote(row_now.at[k], row_got.at[k], rs.at[0, k], rr.at[0, k], *rounds[k]),
            remote(tap_now.at[k], tap_got.at[k], rs.at[1, k], rr.at[1, k], *rounds[k]),
        ]
        for c in small[k]:
            c.start()

    def small_end(k):
        for c in small[k]:
            c.wait_recv()
        row_now[k + 1] = row_now[k] + row_got[k]
        tap_now[k + 1] = tap_now[k] + tap_got[k]

    n = pieces.total
    gain_grad_ref[...] = attn_part_ref[...]

    def gx_end(k):
        m, here = pieces.mine(k)
        grad, gain_part = rms_back(gx.total(k), x_ref[m, here, :].astype(F32), gain_ref[...])
        gain_grad_ref[...] += gain_part
        in_grad_ref[m, here, :] = mid_ref[m, here, :] + grad
        down.forward(k)

    def down_end(k):
        m, here = pieces.mine(k)
        output_ref[m, here, :] = (resid_ref[m, here, :] + down.total(k)).astype(BF16)

    def small_turn(k):
        if k == 0:
            row_now[0, heads + 2 : heads + 3, :] = gain_grad_ref[...]
        else:
            small_end(k - 1)
        if k < len(rounds):
            small_start(k)

    aside = [(1, lambda: each(n, gx.forward, down.start))]
    aside += [(n + 2 * k, functools.partial(gx_end, k)) for k in range(n)]
    for k in range(max(len(rounds) + 1, n)):
        if k <= len(rounds):
            aside.append((3 * n + 2 * k, functools.partial(small_turn, k)))
        if k < n:
            aside.append((3 * n + 2 * k + 1, functools.partial(down_end, k)))
    each(n, gx.start)
    for t in range(total.ticks()):
        for chunk in total.tick(t):
            whole = total.view(full_ref, chunk, 0, total.rows)
            total.view(total_ref, chunk, 0, total.rows)[...] = whole[...].astype(F32)
        while aside and aside[0][0] <= t:
            aside.pop(0)[1]()
    for _, act in aside:
        act()
    k = len(total.bits)
    rows_ref[0] = row_now[k]
    rows_ref[1] = row_now[len(rounds)]
    for member in range(members):
        filter_ref[member] = tap_now[k, 8 * member : 8 * member + CONV, :]
    for group in small.values():
        for c in group:
            c.wait_send()
    each(pieces.total, gx.sent, down.sent)
    total.finish()


def finish(gx_part, down_part, mixer_part, beta_part, taps_part, attn_part, dense_part, out_part, inputs, mid, resid, gain, shards):
    count, local, width = inputs.shape
    members, _, head_width = mixer_part.shape
    bits = (shards - 1).bit_length()
    rounds = bits + 2
    chunks = 2 * members * head_width // 128
    whole = pltpu.VMEM(mixer_part.shape, BF16)
    return pl.pallas_call(
        functools.partial(finish_body, shards),
        in_specs=vmem_specs(12),
        out_specs=vmem_specs(5),
        out_shape=[
            jax.ShapeDtypeStruct(inputs.shape, F32),
            jax.ShapeDtypeStruct(inputs.shape, BF16),
            jax.ShapeDtypeStruct(mixer_part.shape, F32),
            jax.ShapeDtypeStruct((2, 8, width), F32),
            jax.ShapeDtypeStruct(taps_part.shape, F32),
        ],
        scratch_shapes=scatter_scratch(count, local, width) * 2
        + [
            whole, whole, whole,
            pltpu.SemaphoreType.DMA((2 * bits, chunks)),
            pltpu.SemaphoreType.DMA((2 * bits, chunks)),
            pltpu.VMEM((rounds, 8, width), F32),
            pltpu.VMEM((rounds + 1, 8, width), F32),
            pltpu.VMEM((rounds, 24, head_width), F32),
            pltpu.VMEM((rounds + 1, 24, head_width), F32),
            pltpu.SemaphoreType.DMA((2, rounds)),
            pltpu.SemaphoreType.DMA((2, rounds)),
            pltpu.VMEM((1, width), F32),
        ],
        compiler_params=comm_params(3),
        cost_estimate=cost(70),
        name="finish",
    )(gx_part, down_part, mixer_part, beta_part, taps_part, attn_part, dense_part, out_part, inputs, mid, resid, gain)


def compose_body(shards, backward, trans_ref, state_ref, *refs):
    gather = None
    if backward:
        out_ref, stage_ref, got_ref, tx_ref, t_ref, s_ref, send, recv = refs
    else:
        top_ref, out_ref, all_ref, stage_ref, got_ref, tx_ref, t_ref, s_ref, send, recv, gs, gr = refs
        pieces = Pieces(top_ref.shape[0], top_ref.shape[1])
        gather = HeadGather(pieces, all_ref, True, 0, gs, gr)
        for k in range(pieces.total):
            m, here = pieces.mine(k)
            gather.place(k, pieces.head)[...] = top_ref[m, here, :]
    groups = trans_ref.shape[0]
    seq, head = lax.axis_index("seq"), lax.axis_index("head")
    place = shards - 1 - seq if backward else seq
    steps = [1 << k for k in range((shards - 1).bit_length())]

    def peer(distance):
        return lax.rem(seq + shards + distance, shards)

    sign = -1 if backward else 1
    pair = [(seq, pieces.far), (seq, pieces.near)] if gather else []
    greet([(peer(-sign * d), head) for d in steps] + pair, len(steps) + len(pair))

    def apply(trans, state):
        return mm(trans, state, 0, 0) if backward else mm(trans, state)

    def join(late, early):
        return mm(early, late) if backward else mm(late, early)

    for k, d in enumerate(steps):
        final = k == len(steps) - 1
        copies = []
        for part in range(1 if final else 2):
            if k == 0:
                src = state_ref if part == 0 else trans_ref
            else:
                src = stage_ref.at[k - 1, part]
            copies.append(
                remote(src, got_ref.at[k, part], send.at[k, part], recv.at[k, part], peer(sign * d), head)
            )
        for c in copies:
            c.start()
        if gather and k == 0:
            each(pieces.total, gather.own)
        if gather and k == min(1, len(steps) - 1):
            each(pieces.total, gather.forward)
        for c in copies:
            c.wait_recv()
        here = (place >= d).astype(F32)

        @pl.loop(0, groups)
        def _(g, k=k, final=final, here=here):
            state = got_ref[k, 0, g].astype(F32) * here
            if k == 0:
                out_ref[g] = state
            else:
                out_ref[g] += apply(tx_ref[g], state)
            if not final:
                trans = got_ref[k, 1, g].astype(F32) * here
                if k == 0:
                    old_t, old_s = trans_ref[g].astype(F32), state_ref[g].astype(F32)
                    tx_ref[g] = trans.astype(BF16)
                else:
                    old_t, old_s = t_ref[g], s_ref[g]
                    tx_ref[g] = join(tx_ref[g], trans).astype(BF16)
                new_s = old_s + apply(old_t, state)
                new_t = join(old_t, trans)
                s_ref[g] = new_s
                t_ref[g] = new_t
                stage_ref[k, 0, g] = new_s.astype(BF16)
                stage_ref[k, 1, g] = new_t.astype(BF16)

        for c in copies:
            c.wait_send()
    if gather:
        each(pieces.total, gather.arrived, gather.sent)


def compose(trans, state, shards, backward, top=None):
    count, heads = state.shape[:2]
    groups = count * heads
    flat = (groups, HEAD_DIM, HEAD_DIM)
    rounds = (shards - 1).bit_length()
    out_shape = [jax.ShapeDtypeStruct(flat, F32)]
    scratch = [
        pltpu.VMEM((max(rounds - 1, 1), 2) + flat, BF16),
        pltpu.VMEM((rounds, 2) + flat, BF16),
        pltpu.VMEM(flat, BF16),
        pltpu.VMEM(flat, F32),
        pltpu.VMEM(flat, F32),
        pltpu.SemaphoreType.DMA((rounds, 2)),
        pltpu.SemaphoreType.DMA((rounds, 2)),
    ]
    operands = [trans.reshape(flat), state.reshape(flat)]
    if not backward:
        local = top.shape[1]
        operands.append(top)
        n = count * local // PIECE
        out_shape.append(jax.ShapeDtypeStruct((n, PIECE * lax.axis_size("head"), top.shape[2]), BF16))
        scratch += gather_scratch(count, local)
    out = pl.pallas_call(
        functools.partial(compose_body, shards, backward),
        in_specs=vmem_specs(len(operands)),
        out_specs=vmem_specs(len(out_shape)),
        out_shape=out_shape,
        scratch_shapes=scratch,
        compiler_params=comm_params(5 if backward else 4),
        cost_estimate=cost(30),
        name="compose_back" if backward else "compose",
    )(*operands)
    return (out[0].reshape(state.shape), *out[1:])


def regroup(blocks, count):
    if blocks.shape[0] == count:
        return blocks
    _, members, hidden, _ = blocks.shape
    whole = blocks.transpose(1, 2, 0, 3).reshape(members, hidden, count, -1)
    return whole.transpose(2, 0, 1, 3)


def per_device(
    inputs, attn_gain, mixer_weights, beta_weight, filter_weights, out_gain, dense_gain, dense_weights,
    seq_offsets, seq_lengths, out_grad,
):
    count, local_rows, width = inputs.shape
    heads, shards = lax.axis_size("head"), lax.axis_size("seq")
    base = (lax.axis_index("seq") * local_rows * heads).astype(jnp.int32).reshape(1)
    taps = filter_weights
    beta_rows = beta_weight.T
    gain_row = out_gain.reshape(1, HEAD_DIM)
    attn_row = attn_gain.reshape(1, width)
    dense_row = dense_gain.reshape(1, width)
    dense_full = regroup(lax.all_gather(jnp.swapaxes(dense_weights, 1, 2), "seq", axis=0), width // 128)

    x_ext = norm_gather(inputs, attn_row, heads, shards)
    pq, pk, pv, rates, ps, oloc, phi, psi, score, inv, wr, up, trans, state = mix_fwd(
        seq_offsets, seq_lengths, base, x_ext, mixer_weights, beta_rows, taps
    )
    state_in, grad_top = compose(trans, state, shards, False, out_grad)
    start, mixed, head_out, attn_part = mix_out(state_in, ps, oloc, phi, psi, gain_row, mixer_weights)
    resid_mid, down_part, dense_part, grad_mid, grad_attn, dense_gain_part = dense_block(
        attn_part, inputs, out_grad, grad_top, dense_row, dense_full
    )
    dense_mine = lax.psum_scatter(regroup(dense_part, shards), "seq", scatter_dimension=0, tiled=True)
    dense_total = jnp.swapaxes(dense_mine[0], 1, 2).astype(F32)
    dout, out_gain_part, dstate = mix_back(grad_attn, mixer_weights, mixed, gain_row, ps, phi)
    dend = compose(trans, dstate, shards, True)[0]
    gq, gk, gv, tail, rim, grate, filter_part = mix_grad(
        seq_offsets, seq_lengths, base, (pq, pk, pv), rates, taps, dend, dout, start, ps, phi, score, inv, wr, up
    )
    rim_next = shifted(rim, "seq", -1)
    gx_part, mixer_part, beta_part = proj_back(
        (gq, gk, gv), tail, rim_next, grate, x_ext, mixer_weights, beta_rows, grad_attn, head_out
    )
    input_grad, output, mixer_total, rows_total, filter_total = finish(
        gx_part, down_part, mixer_part, beta_part, filter_part,
        jnp.zeros((1, width), F32), dense_gain_part, out_gain_part, inputs, grad_mid, resid_mid, attn_row, shards,
    )
    local_heads = beta_rows.shape[0]
    beta_total = rows_total[0, :local_heads].T
    dense_gain_total = rows_total[1, local_heads]
    out_gain_total = rows_total[1, local_heads + 1, :HEAD_DIM]
    attn_gain_total = rows_total[1, local_heads + 2]
    return (
        output, input_grad, attn_gain_total, mixer_total, beta_total, filter_total, out_gain_total,
        dense_gain_total, dense_total,
    )


def solution(mesh):
    rows = P(None, ("seq", "head"), None)
    return jax.shard_map(
        per_device,
        mesh=mesh,
        in_specs=(
            rows, P(), P(None, None, "head"), P(None, "head"), P(None, None, "head"), P(), P(),
            P(None, "seq", "head"), P(), P(), rows,
        ),
        out_specs=(
            rows, rows, P(), P(None, None, "head"), P(None, "head"), P(None, None, "head"), P(), P(),
            P(None, "seq", "head"),
        ),
        check_vma=False,
    )
```

```python
import functools

import jax
import jax.numpy as jnp
from jax import lax
from jax.experimental import pallas as pl
from jax.experimental.pallas import tpu as pltpu
from jax.sharding import PartitionSpec as P

HEAD_DIM = 128
CONV = 4
CHUNK = 128
HALO = 16
RIM = 8
PIECE = 64
EPS = 1e-06
F32 = jnp.float32
BF16 = jnp.bfloat16
VMEM_LIMIT = 56 * 1024 * 1024


def mm(a, b, ca=1, cb=0):
    return lax.dot_general(
        a.astype(BF16), b.astype(BF16), (((ca,), (cb,)), ((), ())), preferred_element_type=F32
    )


def split(a):
    high = a.astype(BF16)
    return high, (a - high.astype(F32)).astype(BF16)


def mm3(a, b, ca=1, cb=0):
    ah, al = split(a)
    bh, bl = split(b)
    return mm(ah, bh, ca, cb) + (mm(ah, bl, ca, cb) + mm(al, bh, ca, cb))


def sigmoid(v):
    return 1.0 / (1.0 + jnp.exp(-v))


def row_info(off_ref, len_ref, m, base, rows):
    t = base + lax.broadcasted_iota(jnp.int32, (rows, 1), 0)
    start = jnp.zeros_like(t)
    length = jnp.zeros_like(t)
    for i in range(off_ref.shape[1]):
        inside = t >= off_ref[m, i]
        start = jnp.where(inside, off_ref[m, i], start)
        length = jnp.where(inside, len_ref[m, i], length)
    rel = t - start
    return rel, (rel < length).astype(F32)


def chunk_masks(rel):
    n = rel.shape[0]
    i = lax.broadcasted_iota(jnp.int32, (n, n), 0)
    j = lax.broadcasted_iota(jnp.int32, (n, n), 1)
    same = rel >= i - j
    strict = jnp.logical_and(same, i > j)
    incl = jnp.logical_and(same, i >= j)
    col = lax.broadcasted_iota(jnp.int32, (n, 1), 0)
    sees = (rel > col).astype(F32)
    last = rel[n - 1 : n, :]
    stays = ((n - 1 - col) <= last).astype(F32)
    keep = (last > n - 1).astype(F32)
    return strict, incl, sees, stays, keep


def unit_lower_inverse(a_list):
    n = a_list[0].shape[0]
    i = lax.broadcasted_iota(jnp.int32, (n, n), 0)
    j = lax.broadcasted_iota(jnp.int32, (n, n), 1)
    eye = (i == j).astype(F32)
    size = 1
    inv_list = [eye for _ in a_list]
    while size < n:
        pair = jnp.logical_and(i // size == j // size + 1, (i // size) % 2 == 1)
        below = [jnp.where(pair, a, 0.0) for a in a_list]
        if size == 1:
            inv_list = [eye - b for b in below]
        else:
            half = [mm3(b, inv) for b, inv in zip(below, inv_list)]
            inv_list = [inv - mm3(inv, h) for inv, h in zip(inv_list, half)]
        size *= 2
    return inv_list


def lagged(ext, lag, rows):
    moved = pltpu.roll(ext, lag, 0) if lag else ext
    return moved[HALO : HALO + rows]


def lag_masks(rel):
    return [None] + [(rel >= lag).astype(F32) for lag in range(1, CONV)]


def filtered(ext, taps, masks, rows):
    total = None
    for lag in range(CONV):
        term = taps[lag : lag + 1, :] * lagged(ext, lag, rows)
        if masks[lag] is not None:
            term = term * masks[lag]
        total = term if total is None else total + term
    return total


MESH = pl.DeviceIdType.MESH


def flip(index, bit):
    return index + bit * (1 - 2 * (index // bit % 2))


def remote(src, dst, send, recv, seq, head):
    return pltpu.make_async_remote_copy(
        src_ref=src, dst_ref=dst, send_sem=send, recv_sem=recv, device_id=(seq, head), device_id_type=MESH
    )


def greet(devices, expected):
    barrier = pltpu.get_barrier_semaphore()
    for seq, head in devices:
        pl.semaphore_signal(barrier, inc=1, device_id=(seq, head), device_id_type=MESH)
    pl.semaphore_wait(barrier, expected)


class Pieces:
    def __init__(self, count, local):
        self.local = local
        self.per = local // PIECE
        self.total = count * self.per
        self.seq, self.head = lax.axis_index("seq"), lax.axis_index("head")
        self.far, self.near = flip(self.head, 2), flip(self.head, 1)

    def mine(self, k):
        return k // self.per, pl.ds(pl.multiple_of(k % self.per * PIECE, PIECE), PIECE)

    def block(self, ref, k, owner, tiled, first=0):
        if tiled:
            return ref.at[k, pl.ds(pl.multiple_of(owner * PIECE, PIECE), PIECE), :]
        start = first + owner * self.local + k % self.per * PIECE
        return ref.at[k // self.per, pl.ds(pl.multiple_of(start, 16), PIECE), :]


class HeadGather:
    def __init__(self, pieces, out_ref, tiled, first, send, recv):
        self.pieces, self.out, self.tiled, self.first = pieces, out_ref, tiled, first
        self.send, self.recv = send, recv

    def place(self, k, owner):
        return self.pieces.block(self.out, k, owner, self.tiled, self.first)

    def copy(self, kind, k):
        p = self.pieces
        owner = p.far if kind == 2 else p.head
        target = p.near if kind else p.far
        ref = self.place(k, owner)
        return remote(ref, ref, self.send.at[kind, k], self.recv.at[kind, k], p.seq, target)

    def own(self, k):
        self.copy(0, k).start()
        self.copy(1, k).start()

    def forward(self, k):
        self.copy(0, k).wait_recv()
        self.copy(2, k).start()

    def arrived(self, k):
        self.copy(1, k).wait_recv()
        self.copy(2, k).wait_recv()

    def sent(self, k):
        for kind in range(3):
            self.copy(kind, k).wait_send()


class HeadScatter:
    def __init__(self, pieces, part_ref, tiled, near_ref, stage_ref, far_ref, send, recv):
        self.pieces, self.part, self.tiled = pieces, part_ref, tiled
        self.nearby, self.stage, self.faraway = near_ref, stage_ref, far_ref
        self.send, self.recv = send, recv

    def block(self, k, owner):
        return self.pieces.block(self.part, k, owner, self.tiled)

    def copy(self, kind, k):
        p = self.pieces
        if kind == 2:
            return remote(
                self.stage.at[k], self.faraway.at[k], self.send.at[2, k], self.recv.at[2, k], p.seq, p.far
            )
        owner = p.near if kind else flip(p.near, 2)
        return remote(
            self.block(k, owner), self.nearby.at[kind, k], self.send.at[kind, k], self.recv.at[kind, k], p.seq, p.near
        )

    def start(self, k):
        self.copy(0, k).start()
        self.copy(1, k).start()

    def forward(self, k):
        self.copy(0, k).wait_recv()
        total = self.block(k, self.pieces.far)[...].astype(F32) + self.nearby[0, k].astype(F32)
        self.stage[k] = total.astype(BF16)
        self.copy(2, k).start()

    def total(self, k):
        self.copy(1, k).wait_recv()
        self.copy(2, k).wait_recv()
        near = self.block(k, self.pieces.head)[...].astype(F32) + self.nearby[1, k].astype(F32)
        return near + self.faraway[k].astype(F32)

    def sent(self, k):
        for kind in range(3):
            self.copy(kind, k).wait_send()


def each(count, *steps):
    for step in steps:
        pl.loop(0, count)(step)


def scatter_scratch(count, local, width):
    n = count * local // PIECE
    return [
        pltpu.VMEM((2, n, PIECE, width), BF16),
        pltpu.VMEM((n, PIECE, width), BF16),
        pltpu.VMEM((n, PIECE, width), BF16),
        pltpu.SemaphoreType.DMA((3, n)),
        pltpu.SemaphoreType.DMA((3, n)),
    ]


def gather_scratch(count, local):
    n = count * local // PIECE
    return [pltpu.SemaphoreType.DMA((3, n)), pltpu.SemaphoreType.DMA((3, n))]


class Compose:
    def __init__(self, shards, heads, trans_ref, state_ref, out_ref, back_x_ref, back_y_ref, scratch):
        self.shards, self.heads = shards, heads
        self.trans, self.state, self.out, self.back_x, self.back_y = trans_ref, state_ref, out_ref, back_x_ref, back_y_ref
        self.stage, self.got, self.got_back, self.tx, self.s, self.send, self.recv = scratch
        self.seq, self.head = lax.axis_index("seq"), lax.axis_index("head")
        self.steps = [1 << k for k in range((shards - 1).bit_length())]

    def peer(self, distance):
        return lax.rem(self.seq + self.shards + distance, self.shards)

    def peers(self):
        return [(self.peer(-d), self.head) for d in self.steps] + [(self.peer(d), self.head) for d in self.steps[:-1]]

    def copies(self, m, k):
        d = self.steps[k]
        here = pl.ds(m * self.heads, self.heads)
        final = k == len(self.steps) - 1
        out = []
        for part in range(1 if final else 3):
            if part == 2:
                src = self.trans if k == 0 else self.back_y.at[k - 1]
                dst = self.got_back.at[k]
            else:
                src = (self.state, self.trans)[part] if k == 0 else self.stage.at[k - 1, part]
                dst = self.got.at[k, part]
            to = self.peer(-d if part == 2 else d)
            sems = self.send.at[part, k, m], self.recv.at[part, k, m]
            out.append(remote(src.at[here], dst.at[here], *sems, to, self.head))
        return out

    def begin(self, m, k):
        for c in self.copies(m, k):
            c.start()

    def turn(self, m, k):
        n = len(self.steps)
        if k == 0:
            self.begin(m, 0)
            return
        for c in self.copies(m, k - 1):
            c.wait_recv()
        k -= 1
        final = k == n - 1
        here = (self.seq >= self.steps[k]).astype(F32)
        here_back = (self.seq + self.steps[k] < self.shards).astype(F32)
        groups = range(m * self.heads, (m + 1) * self.heads)
        pairs = {}
        for g in groups:
            state = self.got[k, 0, g].astype(F32) * here
            if final:
                self.out[g] = state if k == 0 else self.out[g] + mm(self.tx[g], state)
                continue
            pairs[g] = jnp.concatenate([self.got[k, 1, g].astype(F32) * here, state], axis=1).astype(BF16)
            old_t = self.trans[g] if k == 0 else self.stage[k - 1, 1, g]
            old_s = self.state[g].astype(F32) if k == 0 else self.s[g]
            both = mm(old_t, pairs[g])
            new_s = old_s + both[:, HEAD_DIM:]
            self.s[g] = new_s
            self.stage[k, 0, g] = new_s.astype(BF16)
            self.stage[k, 1, g] = both[:, :HEAD_DIM].astype(BF16)
            later = (self.got_back[k, g].astype(F32) * here_back).astype(BF16)
            self.back_x[k, g] = later if k == 0 else mm(later, self.back_x[k - 1, g]).astype(BF16)
            self.back_y[k, g] = mm(later, self.trans[g] if k == 0 else self.back_y[k - 1, g]).astype(BF16)
        if final:
            return
        self.begin(m, k + 1)
        for g in groups:
            if k == 0:
                self.out[g] = pairs[g][:, HEAD_DIM:].astype(F32)
                self.tx[g] = pairs[g][:, :HEAD_DIM]
            else:
                both = mm(self.tx[g], pairs[g])
                self.out[g] += both[:, HEAD_DIM:]
                self.tx[g] = both[:, :HEAD_DIM].astype(BF16)

    def sent(self, count):
        for m in range(count):
            for k in range(len(self.steps)):
                for c in self.copies(m, k):
                    c.wait_send()

    def script(self, m):
        return [functools.partial(self.turn, m, k) for k in range(len(self.steps) + 1)]


def compose_scratch(shards, count, flat):
    rounds = (shards - 1).bit_length()
    more = max(rounds - 1, 1)
    return [
        pltpu.VMEM((more, 2) + flat, BF16),
        pltpu.VMEM((rounds, 2) + flat, BF16),
        pltpu.VMEM((more,) + flat, BF16),
        pltpu.VMEM(flat, BF16),
        pltpu.VMEM(flat, F32),
        pltpu.SemaphoreType.DMA((3, rounds, count)),
        pltpu.SemaphoreType.DMA((3, rounds, count)),
    ]


class ComposeBack:
    def __init__(self, shards, heads, trans_ref, state_ref, back_x_ref, back_y_ref, out_ref, scratch):
        self.shards, self.heads = shards, heads
        self.trans, self.state, self.back_x, self.back_y, self.out = trans_ref, state_ref, back_x_ref, back_y_ref, out_ref
        self.stage, self.got, self.s, self.send, self.recv = scratch
        self.seq, self.head = lax.axis_index("seq"), lax.axis_index("head")
        self.steps = [1 << k for k in range((shards - 1).bit_length())]

    def peer(self, distance):
        return lax.rem(self.seq + self.shards + distance, self.shards)

    def peers(self):
        return [(self.peer(d), self.head) for d in self.steps]

    def copy(self, m, k):
        here = pl.ds(m * self.heads, self.heads)
        src = self.state if k == 0 else self.stage.at[k - 1]
        dst = self.got.at[k]
        return remote(
            src.at[here], dst.at[here], self.send.at[k, m], self.recv.at[k, m], self.peer(-self.steps[k]), self.head
        )

    def begin(self, m, k):
        self.copy(m, k).start()

    def turn(self, m, k):
        n = len(self.steps)
        if k == 0:
            self.begin(m, 0)
            return
        k -= 1
        self.copy(m, k).wait_recv()
        here = (self.seq + self.steps[k] < self.shards).astype(F32)
        groups = range(m * self.heads, (m + 1) * self.heads)
        states = [(self.got[k, g].astype(F32) * here).astype(BF16) for g in groups]
        if k + 1 < n:
            for g, state in zip(groups, states):
                trans = self.trans[g] if k == 0 else self.back_y[k - 1, g]
                new_s = (self.state[g].astype(F32) if k == 0 else self.s[g]) + mm(trans, state, 0, 0)
                self.s[g] = new_s
                self.stage[k, g] = new_s.astype(BF16)
            self.begin(m, k + 1)
        for g, state in zip(groups, states):
            if k == 0:
                self.out[g] = state.astype(F32)
            else:
                self.out[g] += mm(self.back_x[k - 1, g], state, 0, 0)

    def sent(self, count):
        for m in range(count):
            for k in range(len(self.steps)):
                self.copy(m, k).wait_send()


def compose_back_scratch(shards, count, flat):
    rounds = (shards - 1).bit_length()
    return [
        pltpu.VMEM((max(rounds - 1, 1),) + flat, BF16),
        pltpu.VMEM((rounds,) + flat, BF16),
        pltpu.VMEM(flat, F32),
        pltpu.SemaphoreType.DMA((rounds, count)),
        pltpu.SemaphoreType.DMA((rounds, count)),
    ]


class LineGather:
    def __init__(self, shards, src_ref, place, send, recv, local):
        self.shards, self.src, self.place = shards, src_ref, place
        self.send, self.recv, self.local = send, recv, local
        self.seq, self.head = lax.axis_index("seq"), lax.axis_index("head")
        self.neighbour = flip(self.seq, 1)
        self.half = shards // 2

    def on_line(self, distance, base=None):
        base = self.seq if base is None else base
        return lax.rem(base + self.shards + 2 * distance, self.shards)

    def peers(self):
        return [(self.on_line(-d), self.head) for d in range(1, self.half)] + [(self.neighbour, self.head)]

    def along(self, member, d, block):
        sems = self.send.at[member, d], self.recv.at[member, d]
        return remote(self.src.at[member], self.place(member, block), *sems, self.on_line(d), self.head)

    def across(self, member, d, block):
        dst = self.place(member, block)
        sems = self.send.at[member, self.half + d], self.recv.at[member, self.half + d]
        return remote(dst if d else self.src.at[member], dst, *sems, self.neighbour, self.head)

    def mine(self, member):
        return pltpu.make_async_copy(self.src.at[member], self.place(member, self.seq), self.local.at[member])

    def start(self, member):
        self.mine(member).start()
        for d in range(1, self.half):
            self.along(member, d, self.seq).start()
        self.across(member, 0, self.seq).start()

    def forward(self, member):
        for d in range(1, self.half):
            block = self.on_line(-d)
            self.along(member, d, block).wait_recv()
            self.across(member, d, block).start()

    def arrived(self, member):
        self.mine(member).wait()
        for d in range(self.half):
            self.across(member, d, self.on_line(-d, self.neighbour)).wait_recv()

    def sent(self, member):
        for d in range(1, self.half):
            self.along(member, d, self.seq).wait_send()
        for d in range(self.half):
            self.across(member, d, self.on_line(-d)).wait_send()

    def finish(self, member):
        self.arrived(member)
        self.sent(member)


def mix_fwd_body(
    shards, count, heads, token_heads, extra, off_ref, len_ref, base_ref, w_ref, beta_ref, taps_ref, in_ref, gain_ref, top_ref, own_ref,
    pq_ref, pk_ref, pv_ref, rate_ref, ps_ref, oloc_ref, phi_ref, psi_ref, m_ref, inv_ref, wr_ref, up_ref,
    trans_ref, enter_ref, back_x_ref, back_y_ref, all_x_out, all_top_out, *refs,
):
    full_ref, refs = (refs[0], refs[1:]) if extra else (None, refs)
    all_x_ref, all_top_ref, out_sems, state_ref, x_send, x_recv, gather_send, gather_recv, halo_send, halo_recv, *refs = refs
    scratch, sems = refs[:7], refs[7:]
    mb = pl.program_id(0)
    head = pl.program_id(1)
    grid_step = mb * heads + head
    steps = count * heads
    local = in_ref.shape[1]
    pieces = Pieces(count, local)
    gather_x = HeadGather(pieces, all_x_ref, False, HALO, x_send, x_recv)
    gather = HeadGather(pieces, all_top_ref, True, 0, gather_send, gather_recv)
    rounds = Compose(shards, heads, trans_ref, state_ref, enter_ref, back_x_ref, back_y_ref, scratch)
    line = LineGather(shards, own_ref, lambda member, q: full_ref.at[q, member], *sems) if extra else None
    last = pieces.head == token_heads - 1

    def halo(target):
        src = all_x_ref.at[:, pl.ds(token_heads * local, HALO), :]
        dst = all_x_ref.at[:, pl.ds(0, HALO), :]
        return remote(src, dst, halo_send.at[target], halo_recv, lax.rem(pieces.seq + 1, shards), target)

    def some(act, first, stop):
        pl.loop(first, stop)(act)

    def write_out(i):
        src, dst = ((all_x_ref, all_x_out), (all_top_ref, all_top_out))[i]
        return pltpu.make_async_copy(src, dst, out_sems.at[i])

    @pl.when(grid_step == 0)
    def _():
        for k in range(pieces.total):
            m, here = pieces.mine(k)
            x = in_ref[m, here, :].astype(F32)
            gather_x.place(k, pieces.head)[...] = rms(x, gain_ref[...]).astype(BF16)
            gather.place(k, pieces.head)[...] = top_ref[m, here, :]
        before = lax.rem(pieces.seq + shards - 1, shards)
        peers = rounds.peers() + (line.peers() if extra else []) + [(pieces.seq, pieces.far), (pieces.seq, pieces.near)]
        greet(peers + [(before, token_heads - 1)], len(peers) + token_heads * last.astype(jnp.int32))
        some(gather_x.own, 0, pieces.per)

        @pl.when(last)
        def _():
            for target in range(token_heads):
                halo(target).start()

        some(gather_x.own, pieces.per, pieces.total)
        if extra:
            for member in range(2):
                line.start(member)
        some(gather_x.forward, 0, pieces.per)
        some(gather_x.arrived, 0, pieces.per)
        halo(0).wait_recv()

    @pl.when(grid_step == min(1, steps - 1))
    def _():
        some(gather_x.forward, pieces.per, pieces.total)
        each(pieces.total, gather.own)

    @pl.when(grid_step == min(heads, steps - 1))
    def _():
        some(gather_x.arrived, pieces.per, pieces.total)
        write_out(0).start()

    if extra:
        for at, member in ((1, 0), (steps - 1, 1)):

            @pl.when(grid_step == at)
            def _(member=member):
                line.forward(member)

    left = []
    plan = {}
    for m in range(count):
        turns = rounds.script(m)
        if m + 1 < count:
            places = [((m + 1) * heads - 1, 1), ((m + 1) * heads, 1)]
            for place in places:
                if turns:
                    plan.setdefault(place, []).append(turns.pop(0))
        left.append(turns)

    def advance(point):
        for (at, where), turns in plan.items():
            if where == point:

                @pl.when(grid_step == at)
                def _(turns=turns):
                    for turn in turns:
                        turn()

    rows = all_x_ref.shape[1] - HALO
    rel, valid = row_info(off_ref, len_ref, mb, base_ref[0], rows)
    x = all_x_ref[mb]
    masks = lag_masks(rel)
    acts = []
    for member, out in enumerate((pq_ref, pk_ref, pv_ref)):
        proj = mm(x, w_ref[member]).astype(BF16)
        out[0] = proj
        filt = filtered(proj.astype(F32), taps_ref[member].astype(F32), masks, rows)
        acts.append(filt * sigmoid(filt))
    query, key, value = acts
    query = query * lax.rsqrt(jnp.sum(query * query, axis=-1, keepdims=True) + EPS)
    key = key * lax.rsqrt(jnp.sum(key * key, axis=-1, keepdims=True) + EPS)
    raw_all = mm(x, beta_ref[...], 1, 1)[HALO:]
    lane = lax.broadcasted_iota(jnp.int32, raw_all.shape, 1)
    raw = jnp.sum(jnp.where(lane == head, raw_all, 0.0), axis=-1, keepdims=True)
    rate_ref[0, 0] = raw
    rate = sigmoid(raw) * valid
    spans = [slice(c * CHUNK, (c + 1) * CHUNK) for c in range(rows // CHUNK)]
    all_masks = [chunk_masks(rel[s]) for s in spans]
    systems, scores = [], []
    for s, (strict, incl, _, _, _) in zip(spans, all_masks):
        both = mm(jnp.concatenate([query[s], key[s]], axis=0), key[s], 1, 1)
        scores.append(jnp.where(incl, both[:CHUNK], 0.0))
        systems.append(jnp.where(strict, rate[s] * both[CHUNK:], 0.0))
    advance(0)
    inverses = unit_lower_inverse(systems)
    i = lax.broadcasted_iota(jnp.int32, (HEAD_DIM, HEAD_DIM), 0)
    j = lax.broadcasted_iota(jnp.int32, (HEAD_DIM, HEAD_DIM), 1)
    eye = (i == j).astype(F32)
    phis, psis, ps, olocs = [], [], [], []
    for s, masks_c, inv, score in zip(spans, all_masks, inverses, scores):
        _, _, sees, stays, keep = masks_c
        right = rate[s] * jnp.concatenate([sees * key[s], value[s]], axis=1)
        solved = mm(inv, right)
        write, update = solved[:, :HEAD_DIM], solved[:, HEAD_DIM:]
        moved = mm(stays * key[s], solved, 0, 0)
        phi = keep * eye - moved[:, :HEAD_DIM]
        psi = moved[:, HEAD_DIM:]
        scored = mm(score, solved)
        p = sees * query[s] - scored[:, :HEAD_DIM]
        m_ref[0, 0, s] = score.astype(BF16)
        inv_ref[0, 0, s] = inv.astype(BF16)
        wr_ref[0, 0, s] = write.astype(BF16)
        up_ref[0, 0, s] = update
        ps_ref[0, 0, s] = p.astype(BF16)
        oloc_ref[0, 0, s] = scored[:, HEAD_DIM:]
        phi_ref[0, 0, s] = phi
        psi_ref[0, 0, s] = psi
        phis.append(phi)
        psis.append(psi)
    trans, state = phis[0], psis[0]
    for phi, psi in zip(phis[1:], psis[1:]):
        both = mm3(phi, jnp.concatenate([trans, state], axis=1))
        trans = both[:, :HEAD_DIM]
        state = both[:, HEAD_DIM:] + psi
    trans_ref[grid_step] = trans.astype(BF16)
    state_ref[grid_step] = state.astype(BF16)
    advance(1)

    @pl.when(grid_step == count * heads - 1)
    def _():
        each(pieces.total, gather.forward)
        while any(left):
            for turns in left:
                if turns:
                    turns.pop(0)()
        rounds.sent(count)
        each(pieces.total, gather.arrived)
        write_out(1).start()
        each(pieces.total, gather.sent, gather_x.sent)
        write_out(0).wait()
        write_out(1).wait()

        @pl.when(last)
        def _():
            for target in range(token_heads):
                halo(target).wait_send()

        if extra:
            for member in range(2):
                line.finish(member)


def cost(us):
    return pl.CostEstimate(flops=0, bytes_accessed=int(us * 3.0e6), transcendentals=0)


def any_spec():
    return pl.BlockSpec(memory_space=pl.ANY)


def smem_spec():
    return pl.BlockSpec(memory_space=pltpu.SMEM)


def params(count, collective=None):
    return pltpu.CompilerParams(
        dimension_semantics=("arbitrary",) * count,
        vmem_limit_bytes=VMEM_LIMIT,
        collective_id=collective,
        has_side_effects=collective is not None,
    )


def line_scratch(shards):
    return [pltpu.SemaphoreType.DMA((3, shards))] * 2 + [pltpu.SemaphoreType.DMA((3,))]


def mix_fwd(offsets, lengths, base, mixer_weights, beta_weight, taps, inputs, gain, top, dense_weights, shards, extra):
    count, local, width = inputs.shape
    token_heads = lax.axis_size("head")
    rows = local * token_heads
    ext_rows = rows + HALO
    heads = beta_weight.shape[0]
    per_head = pl.BlockSpec((1, 1, rows, HEAD_DIM), lambda m, h: (m, h, 0, 0))
    proj_spec = pl.BlockSpec((1, ext_rows, HEAD_DIM), lambda m, h: (m, 0, h))
    proj_shape = jax.ShapeDtypeStruct((count, ext_rows, heads * HEAD_DIM), BF16)

    def big(kind):
        return jax.ShapeDtypeStruct((count, heads, rows, HEAD_DIM), kind)

    flat = (count * heads, HEAD_DIM, HEAD_DIM)
    more = max((shards - 1).bit_length() - 1, 1)
    all_x = (count, ext_rows, width)
    all_top = (count * local // PIECE, PIECE * token_heads, width)
    shapes = [
        jax.ShapeDtypeStruct(flat, BF16),
        jax.ShapeDtypeStruct(flat, F32),
        jax.ShapeDtypeStruct((more,) + flat, BF16),
        jax.ShapeDtypeStruct((more,) + flat, BF16),
        jax.ShapeDtypeStruct(all_x, BF16),
        jax.ShapeDtypeStruct(all_top, BF16),
    ]
    more_shapes = [jax.ShapeDtypeStruct((shards, 2) + dense_weights.shape[1:], BF16)] if extra else []
    shapes += more_shapes
    line_sems = line_scratch(shards) if extra else []
    return pl.pallas_call(
        functools.partial(mix_fwd_body, shards, count, heads, token_heads, extra),
        grid=(count, heads),
        in_specs=[
            smem_spec(), smem_spec(), smem_spec(),
            pl.BlockSpec((3, width, HEAD_DIM), lambda m, h: (0, 0, h)),
            pl.BlockSpec(beta_weight.shape, lambda m, h: (0, 0)),
            pl.BlockSpec((3, CONV, HEAD_DIM), lambda m, h: (0, 0, h)),
        ]
        + vmem_specs(3)
        + [any_spec()],
        out_specs=[proj_spec] * 3
        + [pl.BlockSpec((1, 1, rows, 1), lambda m, h: (m, h, 0, 0))]
        + [per_head] * 8
        + vmem_specs(4)
        + [any_spec()] * (len(shapes) - 4),
        out_shape=[proj_shape] * 3
        + [jax.ShapeDtypeStruct((count, heads, rows, 1), F32)]
        + [big(BF16), big(F32), big(F32), big(F32), big(BF16), big(BF16), big(BF16), big(F32)]
        + shapes,
        scratch_shapes=[
            pltpu.VMEM(all_x, BF16), pltpu.VMEM(all_top, BF16), pltpu.SemaphoreType.DMA((2,)), pltpu.VMEM(flat, BF16)
        ]
        + gather_scratch(count, local) * 2
        + [pltpu.SemaphoreType.DMA((token_heads,)), pltpu.SemaphoreType.DMA]
        + compose_scratch(shards, count, flat)
        + line_sems,
        compiler_params=params(2, 4),
        cost_estimate=cost(45),
        name="mix_fwd",
    )(offsets, lengths, base, mixer_weights, beta_weight, taps, inputs, gain, top, dense_weights)


def mix_out_body(state_ref, ps_ref, oloc_ref, phi_ref, psi_ref, gain_ref, w_ref, start_ref, mixed_ref, head_ref, part_ref):
    heads = ps_ref.shape[1]
    rows = ps_ref.shape[2]
    gain = gain_ref[...]
    states = [state_ref[0, h] for h in range(heads)]
    for c in range(rows // CHUNK):
        s = slice(c * CHUNK, (c + 1) * CHUNK)
        for h in range(heads):
            state = states[h]
            start_ref[0, h, s] = state.astype(BF16)
            mixed = oloc_ref[0, h, s] + mm(ps_ref[0, h, s], state)
            mixed_ref[0, h, s] = mixed
            normed = mixed * lax.rsqrt(jnp.mean(mixed * mixed, axis=-1, keepdims=True) + EPS) * gain
            head_ref[0, s, h * HEAD_DIM : (h + 1) * HEAD_DIM] = normed.astype(BF16)
            states[h] = mm3(phi_ref[0, h, s], state) + psi_ref[0, h, s]
    part_ref[0] = mm(head_ref[0], w_ref[0], 1, 1).astype(BF16)


def mix_out(state_in, ps, oloc, phi, psi, out_gain, mixer_weights):
    count, heads, rows, _ = ps.shape
    width = mixer_weights.shape[1]
    head_width = mixer_weights.shape[2]
    per_mb = pl.BlockSpec((1, heads, rows, HEAD_DIM), lambda m: (m, 0, 0, 0))
    return pl.pallas_call(
        mix_out_body,
        grid=(count,),
        in_specs=[
            pl.BlockSpec((1, heads, HEAD_DIM, HEAD_DIM), lambda m: (m, 0, 0, 0)),
            per_mb, per_mb, per_mb, per_mb,
            pl.BlockSpec((1, HEAD_DIM), lambda m: (0, 0)),
            pl.BlockSpec((1, width, head_width), lambda m: (3, 0, 0)),
        ],
        out_specs=[
            per_mb, per_mb,
            pl.BlockSpec((1, rows, head_width), lambda m: (m, 0, 0)),
            pl.BlockSpec((1, rows, width), lambda m: (m, 0, 0)),
        ],
        out_shape=[
            jax.ShapeDtypeStruct(ps.shape, BF16),
            jax.ShapeDtypeStruct(ps.shape, F32),
            jax.ShapeDtypeStruct((count, rows, head_width), BF16),
            jax.ShapeDtypeStruct((count, rows, width), BF16),
        ],
        compiler_params=params(1),
        cost_estimate=cost(5),
        name="mix_out",
    )(state_in, ps, oloc, phi, psi, out_gain, mixer_weights)


def mix_grad_body(
    shards, count, heads,
    off_ref, len_ref, base_ref, pq_ref, pk_ref, pv_ref, rate_ref, taps_ref, start_ref,
    m_ref, inv_ref, wr_ref, up_ref,
    grad_ref, wo_ref, mixed_ref, gain_ref, all_ps_ref, all_phi_ref, trans_ref, back_x_ref, back_y_ref,
    gq_ref, gk_ref, gv_ref, tail_ref, rim_ref, grate_ref, gtaps_ref, gain_grad_ref,
    dstate_ref, dend_ref, all_dout_ref, *scratch,
):
    mb = pl.program_id(0)
    head = pl.program_id(1)
    grid_step = mb * heads + head
    rounds = ComposeBack(shards, heads, trans_ref, dstate_ref, back_x_ref, back_y_ref, dend_ref, scratch)
    n = len(rounds.steps)
    late = [1] if count > 1 else []

    def mix_back(m):
        gain = gain_ref[...]
        grad_head = mm(grad_ref[m], wo_ref[0])
        states = [None] * heads
        for h in range(heads):
            e = grad_head[:, h * HEAD_DIM : (h + 1) * HEAD_DIM]
            v = mixed_ref[m, h]
            r = lax.rsqrt(jnp.mean(v * v, axis=-1, keepdims=True) + EPS)
            weighted = e * gain
            dout = r * weighted - v * (r * r * r * jnp.mean(weighted * v, axis=-1, keepdims=True))
            gain_grad_ref[...] += jnp.sum(e * v * r, axis=0, keepdims=True)
            all_dout_ref[m * heads + h] = dout.astype(BF16)
        for c in reversed(range(all_ps_ref.shape[2] // CHUNK)):
            s = slice(c * CHUNK, (c + 1) * CHUNK)
            for h in range(heads):
                new = mm(all_ps_ref[m, h, s], all_dout_ref[m * heads + h, s], 0, 0)
                if states[h] is not None:
                    new += mm3(all_phi_ref[m, h, s], states[h], 0, 0)
                states[h] = new
        for h in range(heads):
            dstate_ref[m * heads + h] = states[h].astype(BF16)

    @pl.when(grid_step == 0)
    def _():
        gain_grad_ref[...] = jnp.zeros_like(gain_grad_ref)
        gtaps_ref[...] = jnp.zeros_like(gtaps_ref)
        greet(rounds.peers(), n)
        for m in range(count):
            mix_back(m)
            rounds.turn(m, 0)
        for k in range(1, n + 1):
            for m in range(count):
                if m not in late:
                    rounds.turn(m, k)
            for m in late:
                if k > 1:
                    rounds.turn(m, k - 1)

    rows = rate_ref.shape[2]
    rel, valid = row_info(off_ref, len_ref, mb, base_ref[0], rows)
    masks = lag_masks(rel)
    projs, filts, sigs, acts = [], [], [], []
    for member, ref in enumerate((pq_ref, pk_ref, pv_ref)):
        proj = ref[0].astype(F32)
        filt = filtered(proj, taps_ref[member].astype(F32), masks, rows)
        sg = sigmoid(filt)
        projs.append(proj)
        filts.append(filt)
        sigs.append(sg)
        acts.append(filt * sg)
    rq = lax.rsqrt(jnp.sum(acts[0] * acts[0], axis=-1, keepdims=True) + EPS)
    rk = lax.rsqrt(jnp.sum(acts[1] * acts[1], axis=-1, keepdims=True) + EPS)
    query = acts[0] * rq
    key = acts[1] * rk
    value = acts[2]
    sig_rate = sigmoid(rate_ref[0, 0])
    rate = sig_rate * valid
    spans = [slice(c * CHUNK, (c + 1) * CHUNK) for c in range(rows // CHUNK)]
    dstates = [None] * len(spans)
    dstate = dend_ref[grid_step]
    for c in reversed(range(len(spans))):
        s = spans[c]
        dstates[c] = dstate
        if c:
            dstate = mm3(all_phi_ref[mb, head, s], dstate, 0, 0) + mm(all_ps_ref[mb, head, s], all_dout_ref[grid_step, s], 0, 0)
    dqs, dks, dvs, drates = [], [], [], []
    for c, s in enumerate(spans):
        strict, incl, sees, stays, _ = chunk_masks(rel[s])
        q, k, v, b = query[s], key[s], value[s], rate[s]
        dout = all_dout_ref[grid_step, s]
        start = start_ref[0, 0, s]
        fresh = up_ref[0, 0, s] - mm(wr_ref[0, 0, s], start)
        dfresh = mm(m_ref[0, 0, s], dout, 0, 0) + mm(stays * k, dstates[c])
        e = mm(inv_ref[0, 0, s], dfresh, 0, 0)
        left = jnp.concatenate([dout, e.astype(BF16)], axis=0)
        right = jnp.concatenate([fresh.astype(BF16), start], axis=0)
        outer = mm(left, right, 1, 1)
        dscore = jnp.where(incl, outer[:CHUNK, :CHUNK], 0.0)
        dsystem = jnp.where(strict, -outer[CHUNK:, :CHUNK], 0.0)
        grads = jnp.concatenate([dscore, dsystem], axis=0).astype(BF16)
        byk = mm(grads, k)
        z = byk[CHUNK:] - sees * outer[CHUNK:, CHUNK:]
        dqs.append(sees * outer[:CHUNK, CHUNK:] + byk[:CHUNK])
        dk = mm(grads, jnp.concatenate([q, b * k], axis=0), 0, 0)
        dks.append(dk + stays * mm(fresh, dstates[c], 1, 1) + b * z)
        dvs.append(b * e)
        drates.append(jnp.sum(e * v + k * z, axis=-1, keepdims=True))
    dq = jnp.concatenate(dqs, axis=0)
    dk = jnp.concatenate(dks, axis=0)
    dv = jnp.concatenate(dvs, axis=0)
    drate = jnp.concatenate(drates, axis=0)
    grate_ref[0, 0] = drate * valid * sig_rate * (1.0 - sig_rate)
    dacts = [
        rq * dq - acts[0] * (rq * rq * rq * jnp.sum(dq * acts[0], axis=-1, keepdims=True)),
        rk * dk - acts[1] * (rk * rk * rk * jnp.sum(dk * acts[1], axis=-1, keepdims=True)),
        dv,
    ]
    for member, out in enumerate((gq_ref, gk_ref, gv_ref)):
        sg = sigs[member]
        dfilt = dacts[member] * (sg * (1.0 + filts[member] * (1.0 - sg)))
        taps = taps_ref[member].astype(F32)
        total = None
        pieces = []
        for lag in range(CONV):
            masked = dfilt if lag == 0 else dfilt * masks[lag]
            pieces.append(jnp.sum(masked * lagged(projs[member], lag, rows), axis=0, keepdims=True))
            scaled = masked * taps[lag : lag + 1, :]
            ext = jnp.concatenate([jnp.zeros((RIM, HEAD_DIM), F32), scaled], axis=0)
            if lag:
                ext = pltpu.roll(ext, rows + RIM - lag, 0)
            total = ext if total is None else total + ext
        here = total[RIM:]
        out[0] = here.astype(BF16)
        tail_ref[0, member] = here[rows - RIM :]
        rim_ref[0, member] = total[:RIM]
        lanes = pl.ds(pl.multiple_of(head * HEAD_DIM, HEAD_DIM), HEAD_DIM)
        gtaps_ref[member, :, lanes] += jnp.concatenate(pieces, axis=0)

    @pl.when(grid_step == 0)
    def _():
        for m in late:
            rounds.turn(m, n)

    @pl.when(grid_step == count * heads - 1)
    def _():
        rounds.sent(count)


def mix_grad(
    offsets, lengths, base, proj3, rates, taps, start, m, inv, wr, up,
    grad_attn, mixer_weights, mixed, out_gain, ps, phi, trans, back_x, back_y, shards,
):
    count, heads, rows, _ = ps.shape
    ext_rows = rows + HALO
    width = mixer_weights.shape[1]
    head_width = mixer_weights.shape[2]
    flat = (count * heads, HEAD_DIM, HEAD_DIM)
    per_head = pl.BlockSpec((1, 1, rows, HEAD_DIM), lambda m, h: (m, h, 0, 0))
    proj_spec = pl.BlockSpec((1, ext_rows, HEAD_DIM), lambda m, h: (m, 0, h))
    out_spec = pl.BlockSpec((1, rows, HEAD_DIM), lambda m, h: (m, 0, h))
    rate_spec = pl.BlockSpec((1, 1, rows, 1), lambda m, h: (m, h, 0, 0))
    small = pl.BlockSpec((1, 3, RIM, HEAD_DIM), lambda m, h: (m, 0, 0, h))
    small_shape = jax.ShapeDtypeStruct((count, 3, RIM, head_width), F32)
    return pl.pallas_call(
        functools.partial(mix_grad_body, shards, count, heads),
        grid=(count, heads),
        in_specs=[
            smem_spec(), smem_spec(), smem_spec(),
            proj_spec, proj_spec, proj_spec, rate_spec,
            pl.BlockSpec((3, CONV, HEAD_DIM), lambda m, h: (0, 0, h)),
        ]
        + [per_head] * 5
        + vmem_specs(1)
        + [pl.BlockSpec((1, width, head_width), lambda m, h: (3, 0, 0))]
        + vmem_specs(7),
        out_specs=[out_spec] * 3 + [small, small, rate_spec] + vmem_specs(2),
        out_shape=[jax.ShapeDtypeStruct((count, rows, head_width), BF16)] * 3
        + [
            small_shape, small_shape,
            jax.ShapeDtypeStruct(rates.shape, F32),
            jax.ShapeDtypeStruct(taps.shape, F32),
            jax.ShapeDtypeStruct((1, HEAD_DIM), F32),
        ],
        scratch_shapes=[
            pltpu.VMEM(flat, BF16),
            pltpu.VMEM(flat, F32),
            pltpu.VMEM((count * heads, rows, HEAD_DIM), BF16),
        ]
        + compose_back_scratch(shards, count, flat),
        compiler_params=params(2, 5),
        cost_estimate=cost(45),
        name="mix_grad",
    )(
        offsets, lengths, base, *proj3, rates, taps, start, m, inv, wr, up,
        grad_attn, mixer_weights, mixed, out_gain, ps, phi, trans, back_x, back_y,
    )


def rms(values, gain):
    return values * lax.rsqrt(jnp.mean(values * values, axis=-1, keepdims=True) + EPS) * gain


def rms_back(grad, values, gain):
    inv = lax.rsqrt(jnp.mean(values * values, axis=-1, keepdims=True) + EPS)
    weighted = grad * gain
    grad_in = inv * weighted - values * inv**3 * jnp.mean(weighted * values, axis=-1, keepdims=True)
    return grad_in, jnp.sum(grad * values * inv, axis=0, keepdims=True)

def vmem_specs(count):
    return [pl.BlockSpec(memory_space=pltpu.VMEM)] * count


def comm_params(collective):
    return pltpu.CompilerParams(
        collective_id=collective, has_side_effects=True, vmem_limit_bytes=VMEM_LIMIT
    )


def dense_block_body(
    shards, extra, part_ref, x_ref, top_ref, all_top_ref, gain_ref, w_ref, own_ref,
    resid_ref, down_ref, grad_ref, mid_ref, out_ref, gain_grad_ref,
    wt_ref, wsem, acc_ref, in_ref, gin_ref, gate_ref, up_ref, *scratch,
):
    count, local, width = x_ref.shape
    groups = w_ref.shape[0]
    cut = width // groups
    ready = 2 if extra else 3
    pieces = Pieces(count, local)
    line = None
    if extra:
        line = LineGather(
            shards, own_ref, lambda i, q: wt_ref.at[i, :, pl.ds(pl.multiple_of(q * cut, cut), cut)], *scratch[14:]
        )
    first = HeadScatter(pieces, part_ref, False, *scratch[:5])
    spread = HeadGather(pieces, in_ref, True, 0, *scratch[5:7])
    second = HeadScatter(pieces, gin_ref, True, *scratch[7:12])
    back = HeadGather(pieces, out_ref, False, 0, *scratch[12:14])

    def weights(p):
        return pltpu.make_async_copy(w_ref.at[p, 0:ready], wt_ref.at[0:ready, :, pl.ds(p * cut, cut)], wsem.at[p])

    peers = line.peers() if extra else []
    for p in range(groups):
        weights(p).start()
    greet([(pieces.seq, pieces.far), (pieces.seq, pieces.near)] + peers, 2 + len(peers))
    n = pieces.total
    each(n, first.start)
    if extra:
        line.start(2)
    each(n, first.forward)
    gain_grad_ref[...] = jnp.zeros_like(gain_grad_ref)

    @pl.loop(0, n)
    def _(k):
        m, here = pieces.mine(k)
        resid = x_ref[m, here, :].astype(F32) + first.total(k)
        resid_ref[m, here, :] = resid
        spread.place(k, pieces.head)[...] = rms(resid, gain_ref[...]).astype(BF16)
        spread.own(k)

    for p in range(groups):
        weights(p).wait()

    def turn_back(k):
        m, here = pieces.mine(k)
        grad, gain_part = rms_back(second.total(k), resid_ref[m, here, :], gain_ref[...])
        mid = top_ref[m, here, :].astype(F32) + grad
        gain_grad_ref[...] += gain_part
        mid_ref[m, here, :] = mid
        back.place(k, pieces.head)[...] = mid.astype(BF16)
        back.own(k)

    spread.forward(0)
    if extra:
        line.forward(2)

    @pl.loop(0, n)
    def _(k):
        spread.arrived(k)
        x = in_ref[k]
        gate_ref[k] = mm(x, wt_ref[0], 1, 1)
        up_ref[k] = mm(x, wt_ref[1], 1, 1)

        @pl.when(k + 1 < n)
        def _():
            spread.forward(k + 1)

    if extra:
        line.arrived(2)

    @pl.loop(0, n)
    def _(k):
        x = in_ref[k]
        gate = gate_ref[k]
        up = up_ref[k]
        grad_hidden = mm(all_top_ref[k], wt_ref[2], 1, 1)
        sg = sigmoid(gate)
        silu = gate * sg
        hidden = (silu * up).astype(BF16)
        grad_gate = (grad_hidden * up * (sg * (1.0 + gate * (1.0 - sg)))).astype(BF16)
        grad_up = (grad_hidden * silu).astype(BF16)
        gin_ref[k] = (mm(grad_gate, wt_ref[0]) + mm(grad_up, wt_ref[1])).astype(BF16)
        second.start(k)
        down_ref[k] = mm(hidden, wt_ref[2]).astype(BF16)
        second.forward(k)
        adds = (mm(grad_gate, x, 0, 0), mm(grad_up, x, 0, 0), mm(hidden, all_top_ref[k], 0, 0))

        @pl.when(k == 0)
        def _():
            for i, add in enumerate(adds):
                acc_ref[i] = add

        @pl.when(jnp.logical_and(k > 0, k + 1 < n))
        def _():
            for i, add in enumerate(adds):
                acc_ref[i] += add

        @pl.when(k + 1 == n)
        def _():
            for i, add in enumerate(adds):
                total = (acc_ref[i] + add).astype(BF16)
                for p in range(groups):
                    grad_ref[p, i] = total[:, p * cut : (p + 1) * cut]

        @pl.when(k > 0)
        def _():
            turn_back(k - 1)

        @pl.when(k > 1)
        def _():
            back.forward(k - 2)

    turn_back(n - 1)
    back.forward(n - 2)
    back.forward(n - 1)
    each(n, back.arrived, back.sent, second.sent, spread.sent, first.sent)
    if extra:
        line.sent(2)


def dense_block(part, inputs, top, all_top, gain, weights, own, shards, extra):
    count, local, width = inputs.shape
    groups, _, hidden, cut = weights.shape
    n = count * local // PIECE
    tile = all_top.shape[1]
    rows = part.shape[1]
    return pl.pallas_call(
        functools.partial(dense_block_body, shards, extra),
        in_specs=vmem_specs(5) + [any_spec()] * 2,
        out_specs=vmem_specs(6),
        out_shape=[
            jax.ShapeDtypeStruct(inputs.shape, F32),
            jax.ShapeDtypeStruct((n, tile, width), BF16),
            jax.ShapeDtypeStruct((groups, 3, hidden, cut), BF16),
            jax.ShapeDtypeStruct(inputs.shape, F32),
            jax.ShapeDtypeStruct((count, rows, width), BF16),
            jax.ShapeDtypeStruct((1, width), F32),
        ],
        scratch_shapes=[
            pltpu.VMEM((3, hidden, width), BF16),
            pltpu.SemaphoreType.DMA((groups,)),
            pltpu.VMEM((3, hidden, width), F32),
            pltpu.VMEM((n, tile, width), BF16),
            pltpu.VMEM((n, tile, width), BF16),
            pltpu.VMEM((n, tile, hidden), F32),
            pltpu.VMEM((n, tile, hidden), F32),
        ]
        + (scatter_scratch(count, local, width) + gather_scratch(count, local)) * 2
        + (line_scratch(shards) if extra else []),
        compiler_params=comm_params(1),
        cost_estimate=cost(55),
        name="dense_block",
    )(part, inputs, top, all_top, gain, weights, own)


class SeqSum:
    def __init__(self, shards, part_ref, work_ref, got_ref, full_ref, send, recv):
        self.part, self.work, self.got, self.full = part_ref, work_ref, got_ref, full_ref
        self.send, self.recv = send, recv
        self.seq, self.head = lax.axis_index("seq"), lax.axis_index("head")
        self.bits = [1 << k for k in range((shards - 1).bit_length())]
        self.members, self.rows = part_ref.shape[0], part_ref.shape[1] // 2
        self.half = 128
        self.chunks = 2 * self.members * (part_ref.shape[2] // self.half)
        self.steps = 2 * len(self.bits)
        self.order = [self.members - 1, *range(self.members - 1)]
        self.copies = {}
        self.kept, self.gone = [0], []
        size = self.rows
        for bit in self.bits:
            size //= 2
            mine = self.seq // bit % 2
            self.gone.append(self.kept[-1] + size * (1 - mine))
            self.kept.append(self.kept[-1] + size * mine)

    def view(self, ref, chunk, first, size):
        per = self.chunks // self.members
        first = pl.multiple_of(chunk % 2 * self.rows + first, 8)
        return ref.at[self.order[chunk // per], pl.ds(first, size), pl.ds(chunk % per // 2 * self.half, self.half)]

    def begin(self, chunk, step):
        size = self.rows >> (step + 1)
        src = self.view(self.part if step == 0 else self.work, chunk, self.gone[step], size)
        offset = self.rows - 2 * size
        dst = self.view(self.got, chunk, offset, size)
        c = remote(src, dst, self.send.at[step, chunk], self.recv.at[step, chunk], flip(self.seq, self.bits[step]), self.head)
        c.start()
        self.copies[step, chunk] = c

    def fold(self, chunk, step):
        size = self.rows >> (step + 1)
        self.copies[step, chunk].wait_recv()
        got = self.view(self.got, chunk, self.rows - 2 * size, size)
        kept = self.view(self.part if step == 0 else self.work, chunk, self.kept[step + 1], size)
        total = (kept[...].astype(F32) + got[...].astype(F32)).astype(BF16)
        last = step == len(self.bits) - 1
        self.view(self.full if last else self.work, chunk, self.kept[step + 1], size)[...] = total

    def spread(self, chunk, step):
        back = len(self.bits) - 1 - step
        size = self.rows >> (back + 1)
        ref = self.view(self.full, chunk, self.kept[back + 1], size)
        at = len(self.bits) + step
        c = remote(ref, ref, self.send.at[at, chunk], self.recv.at[at, chunk], flip(self.seq, self.bits[back]), self.head)
        c.start()
        self.copies[at, chunk] = c

    def stage(self, chunk, step):
        n = len(self.bits)
        if step > n:
            self.copies[step - 1, chunk].wait_recv()
        elif step > 0:
            self.fold(chunk, step - 1)
        if step < n:
            self.begin(chunk, step)
        elif step < 2 * n:
            self.spread(chunk, step - n)

    def tick(self, t):
        done = []
        for chunk in range(self.chunks):
            step, odd = divmod(t - chunk, 2)
            if not odd and 0 <= step <= self.steps:
                self.stage(chunk, step)
                if step == self.steps:
                    done.append(chunk)
        return done

    def ticks(self):
        return self.chunks + 2 * self.steps

    def finish(self):
        for c in self.copies.values():
            c.wait_send()


def finish_body(
    shards, gq_ref, gk_ref, gv_ref, tail_ref, rim_ref, grate_ref, all_x_ref, w_ref, beta_ref, gattn_ref, head_ref,
    down_ref, taps_ref, dense_part_ref, out_part_ref, x_ref, mid_ref, resid_ref, gain_ref,
    in_grad_ref, output_ref, total_ref, rows_ref, filter_ref,
    gx_ref, mixer_ref, g_ref, rim_got, rim_send, rim_recv, *scratch,
):
    gx_scratch, down_scratch = scratch[:5], scratch[5:10]
    work_ref, got_ref, full_ref, ms, mr, row_got, row_now, tap_got, tap_now, rs, rr, gain_grad_ref = scratch[10:]
    count, local, width = x_ref.shape
    heads = beta_ref.shape[0]
    members = taps_ref.shape[0]
    rows = gq_ref.shape[1]
    pieces = Pieces(count, local)
    gx = HeadScatter(pieces, gx_ref, False, *gx_scratch)
    down = HeadScatter(pieces, down_ref, True, *down_scratch)
    total = SeqSum(shards, mixer_ref, work_ref, got_ref, full_ref, ms, mr)
    seq, head = pieces.seq, pieces.head

    row_now[0] = jnp.zeros(row_now.shape[1:], F32)
    tap_now[0] = jnp.zeros(tap_now.shape[1:], F32)
    row_now[0, heads : heads + 1, :] = dense_part_ref[...]
    row_now[0, heads + 1 : heads + 2, 0:HEAD_DIM] = out_part_ref[...]
    for k in range(members):
        tap_now[0, 8 * k : 8 * k + CONV, :] = taps_ref[k]
    rounds = [(flip(seq, bit), head) for bit in total.bits] + [(seq, flip(head, 2)), (seq, flip(head, 1))]
    before = lax.rem(seq + shards - 1, shards)
    after = lax.rem(seq + 1, shards)
    greet(rounds + [(after, head)], len(rounds) + 1)
    rim = remote(rim_ref, rim_got, rim_send, rim_recv, before, head)
    rim.start()
    small = {}

    def grates(m):
        lane = lax.broadcasted_iota(jnp.int32, (rows, heads), 1)
        out = jnp.zeros((rows, heads), F32)
        for h in range(heads):
            out = jnp.where(lane == h, grate_ref[m, h], out)
        return out

    def weight_grad(member):
        total = None
        for m in range(count):
            left, right = (gattn_ref[m], head_ref[m]) if member == members else (all_x_ref[m, HALO:, :], g_ref[member, m])
            add = mm(left, right, 0, 0)
            total = add if total is None else total + add
        mixer_ref[member] = total.astype(BF16)

    def join_rims():
        rim.wait_recv()
        for member, ref in enumerate((gq_ref, gk_ref, gv_ref)):
            for m in range(count):
                g_ref[member, m, 0 : rows - 2 * RIM, :] = ref[m, 0 : rows - 2 * RIM, :]
                last = (tail_ref[m, member] + rim_got[m, member]).astype(BF16)
                g_ref[member, m, rows - 2 * RIM :, :] = jnp.concatenate([ref[m, rows - 2 * RIM : rows - RIM, :], last], axis=0)

    def row_grad(m):
        total = mm(grates(m), beta_ref[...])
        for member in range(members):
            total += mm(g_ref[member, m], w_ref[member], 1, 1)
        gx_ref[m] = total.astype(BF16)
        for k in range(m * pieces.per, (m + 1) * pieces.per):
            gx.start(k)

    def beta_grad():
        total = None
        for m in range(count):
            add = mm(grates(m), all_x_ref[m, HALO:, :], 0, 0)
            total = add if total is None else total + add
        row_now[0, 0:heads, :] = total

    def small_start(k):
        small[k] = [
            remote(row_now.at[k], row_got.at[k], rs.at[0, k], rr.at[0, k], *rounds[k]),
            remote(tap_now.at[k], tap_got.at[k], rs.at[1, k], rr.at[1, k], *rounds[k]),
        ]
        for c in small[k]:
            c.start()

    def small_end(k):
        for c in small[k]:
            c.wait_recv()
        row_now[k + 1] = row_now[k] + row_got[k]
        tap_now[k + 1] = tap_now[k] + tap_got[k]

    n = pieces.total
    gain_grad_ref[...] = jnp.zeros_like(gain_grad_ref)

    def gx_end(k):
        m, here = pieces.mine(k)
        grad, gain_part = rms_back(gx.total(k), x_ref[m, here, :].astype(F32), gain_ref[...])
        gain_grad_ref[...] += gain_part
        in_grad_ref[m, here, :] = mid_ref[m, here, :] + grad
        down.forward(k)

    def down_end(k):
        m, here = pieces.mine(k)
        output_ref[m, here, :] = (resid_ref[m, here, :] + down.total(k)).astype(BF16)

    def small_turn(k):
        if k == 0:
            row_now[0, heads + 2 : heads + 3, :] = gain_grad_ref[...]
        else:
            small_end(k - 1)
        if k < len(rounds):
            small_start(k)

    def weight_ready(chunk):
        per = total.chunks // total.members
        if chunk < total.chunks and chunk % per == 0:
            weight_grad(total.order[chunk // per])

    aside = [(1, join_rims), (1, functools.partial(row_grad, 0))]
    aside += [(2, functools.partial(row_grad, m)) for m in range(1, count)]
    aside += [(3, lambda: each(n, gx.forward, down.start)), (4, beta_grad)]
    aside += [(n + 2 + 2 * k, functools.partial(gx_end, k)) for k in range(n)]
    first = 3 * n + 2
    for k in range(max(len(rounds) + 1, n)):
        if k <= len(rounds):
            aside.append((first + 2 * k, functools.partial(small_turn, k)))
        if k < n:
            aside.append((first + 2 * k + 1, functools.partial(down_end, k)))
    weight_ready(0)
    for t in range(total.ticks()):
        for chunk in total.tick(t):
            whole = total.view(full_ref, chunk, 0, total.rows)
            total.view(total_ref, chunk, 0, total.rows)[...] = whole[...].astype(F32)
        while aside and aside[0][0] <= t:
            aside.pop(0)[1]()
        weight_ready(t + 1)
    for _, act in aside:
        act()
    k = len(total.bits)
    rows_ref[0] = row_now[k]
    rows_ref[1] = row_now[len(rounds)]
    for member in range(members):
        filter_ref[member] = tap_now[k, 8 * member : 8 * member + CONV, :]
    for group in small.values():
        for c in group:
            c.wait_send()
    each(pieces.total, gx.sent, down.sent)
    total.finish()
    rim.wait_send()


def finish(
    g3, tail, rim, grate, all_x, mixer_weights, beta_rows, grad_attn, head_out,
    down_part, taps_part, dense_part, out_part, inputs, mid, resid, gain, shards,
):
    count, local, width = inputs.shape
    members, _, head_width = mixer_weights.shape
    rows = g3[0].shape[1]
    bits = (shards - 1).bit_length()
    rounds = bits + 2
    chunks = 2 * members * head_width // 128
    whole = pltpu.VMEM(mixer_weights.shape, BF16)
    return pl.pallas_call(
        functools.partial(finish_body, shards),
        in_specs=vmem_specs(19),
        out_specs=vmem_specs(5),
        out_shape=[
            jax.ShapeDtypeStruct(inputs.shape, F32),
            jax.ShapeDtypeStruct(inputs.shape, BF16),
            jax.ShapeDtypeStruct(mixer_weights.shape, F32),
            jax.ShapeDtypeStruct((2, 8, width), F32),
            jax.ShapeDtypeStruct(taps_part.shape, F32),
        ],
        scratch_shapes=[
            pltpu.VMEM((count, rows, width), BF16),
            whole,
            pltpu.VMEM((3, count, rows, head_width), BF16),
            pltpu.VMEM(rim.shape, F32),
            pltpu.SemaphoreType.DMA,
            pltpu.SemaphoreType.DMA,
        ]
        + scatter_scratch(count, local, width) * 2
        + [
            whole, whole, whole,
            pltpu.SemaphoreType.DMA((2 * bits, chunks)),
            pltpu.SemaphoreType.DMA((2 * bits, chunks)),
            pltpu.VMEM((rounds, 8, width), F32),
            pltpu.VMEM((rounds + 1, 8, width), F32),
            pltpu.VMEM((rounds, 24, head_width), F32),
            pltpu.VMEM((rounds + 1, 24, head_width), F32),
            pltpu.SemaphoreType.DMA((2, rounds)),
            pltpu.SemaphoreType.DMA((2, rounds)),
            pltpu.VMEM((1, width), F32),
        ],
        compiler_params=comm_params(3),
        cost_estimate=cost(75),
        name="finish",
    )(
        *g3, tail, rim, grate, all_x, mixer_weights, beta_rows, grad_attn, head_out,
        down_part, taps_part, dense_part, out_part, inputs, mid, resid, gain,
    )


def regroup(blocks, count):
    if blocks.shape[0] == count:
        return blocks
    _, members, hidden, _ = blocks.shape
    whole = blocks.transpose(1, 2, 0, 3).reshape(members, hidden, count, -1)
    return whole.transpose(2, 0, 1, 3)


def per_device(
    inputs, attn_gain, mixer_weights, beta_weight, filter_weights, out_gain, dense_gain, dense_weights,
    seq_offsets, seq_lengths, out_grad,
):
    count, local_rows, width = inputs.shape
    heads, shards = lax.axis_size("head"), lax.axis_size("seq")
    base = (lax.axis_index("seq") * local_rows * heads).astype(jnp.int32).reshape(1)
    taps = filter_weights
    beta_rows = beta_weight.T
    gain_row = out_gain.reshape(1, HEAD_DIM)
    attn_row = attn_gain.reshape(1, width)
    dense_row = dense_gain.reshape(1, width)
    weights_t = jnp.swapaxes(dense_weights, 1, 2)
    extra = width == 128 * shards
    pq, pk, pv, rates, ps, oloc, phi, psi, score, inv, wr, up, trans, enter, back_x, back_y, x_ext, grad_top, *full = mix_fwd(
        seq_offsets, seq_lengths, base, mixer_weights, beta_rows, taps, inputs, attn_row, out_grad, weights_t, shards, extra
    )
    dense_full = full[0] if extra else regroup(lax.all_gather(weights_t, "seq", axis=0), width // 128)
    state_in = enter.reshape((count, -1) + enter.shape[1:])
    start, mixed, head_out, attn_part = mix_out(state_in, ps, oloc, phi, psi, gain_row, mixer_weights)
    resid_mid, down_part, dense_part, grad_mid, grad_attn, dense_gain_part = dense_block(
        attn_part, inputs, out_grad, grad_top, dense_row, dense_full, weights_t, shards, extra
    )
    dense_mine = lax.psum_scatter(regroup(dense_part, shards), "seq", scatter_dimension=0, tiled=True)
    dense_total = jnp.swapaxes(dense_mine[0], 1, 2).astype(F32)
    gq, gk, gv, tail, rim, grate, filter_part, out_gain_part = mix_grad(
        seq_offsets, seq_lengths, base, (pq, pk, pv), rates, taps, start, score, inv, wr, up,
        grad_attn, mixer_weights, mixed, gain_row, ps, phi, trans, back_x, back_y, shards,
    )
    input_grad, output, mixer_total, rows_total, filter_total = finish(
        (gq, gk, gv), tail, rim, grate, x_ext, mixer_weights, beta_rows, grad_attn, head_out,
        down_part, filter_part, dense_gain_part, out_gain_part, inputs, grad_mid, resid_mid, attn_row, shards,
    )
    local_heads = beta_rows.shape[0]
    beta_total = rows_total[0, :local_heads].T
    dense_gain_total = rows_total[1, local_heads]
    out_gain_total = rows_total[1, local_heads + 1, :HEAD_DIM]
    attn_gain_total = rows_total[1, local_heads + 2]
    return (
        output, input_grad, attn_gain_total, mixer_total, beta_total, filter_total, out_gain_total,
        dense_gain_total, dense_total,
    )


def solution(mesh):
    rows = P(None, ("seq", "head"), None)
    return jax.shard_map(
        per_device,
        mesh=mesh,
        in_specs=(
            rows, P(), P(None, None, "head"), P(None, "head"), P(None, None, "head"), P(), P(),
            P(None, "seq", "head"), P(), P(), rows,
        ),
        out_specs=(
            rows, rows, P(), P(None, None, "head"), P(None, "head"), P(None, None, "head"), P(), P(),
            P(None, "seq", "head"),
        ),
        check_vma=False,
    )
```

```python
import functools

import jax
import jax.numpy as jnp
from jax import lax
from jax.experimental import pallas as pl
from jax.experimental.pallas import tpu as pltpu
from jax.sharding import PartitionSpec as P

HEAD_DIM = 128
CONV = 4
CHUNK = 128
HALO = 16
RIM = 8
PIECE = 64
EPS = 1e-06
F32 = jnp.float32
BF16 = jnp.bfloat16
VMEM_LIMIT = 56 * 1024 * 1024


def mm(a, b, ca=1, cb=0):
    return lax.dot_general(
        a.astype(BF16), b.astype(BF16), (((ca,), (cb,)), ((), ())), preferred_element_type=F32
    )


def split(a):
    high = a.astype(BF16)
    return high, (a - high.astype(F32)).astype(BF16)


def mm3(a, b, ca=1, cb=0):
    ah, al = split(a)
    bh, bl = split(b)
    return mm(ah, bh, ca, cb) + (mm(ah, bl, ca, cb) + mm(al, bh, ca, cb))


def sigmoid(v):
    return 1.0 / (1.0 + jnp.exp(-v))


def row_info(off_ref, len_ref, m, base, rows):
    t = base + lax.broadcasted_iota(jnp.int32, (rows, 1), 0)
    start = jnp.zeros_like(t)
    length = jnp.zeros_like(t)
    for i in range(off_ref.shape[1]):
        inside = t >= off_ref[m, i]
        start = jnp.where(inside, off_ref[m, i], start)
        length = jnp.where(inside, len_ref[m, i], length)
    rel = t - start
    return rel, (rel < length).astype(F32)


def chunk_masks(rel):
    n = rel.shape[0]
    i = lax.broadcasted_iota(jnp.int32, (n, n), 0)
    j = lax.broadcasted_iota(jnp.int32, (n, n), 1)
    same = rel >= i - j
    strict = jnp.logical_and(same, i > j)
    incl = jnp.logical_and(same, i >= j)
    col = lax.broadcasted_iota(jnp.int32, (n, 1), 0)
    sees = (rel > col).astype(F32)
    last = rel[n - 1 : n, :]
    stays = ((n - 1 - col) <= last).astype(F32)
    keep = (last > n - 1).astype(F32)
    return strict, incl, sees, stays, keep


def unit_lower_inverse(a_list):
    n = a_list[0].shape[0]
    i = lax.broadcasted_iota(jnp.int32, (n, n), 0)
    j = lax.broadcasted_iota(jnp.int32, (n, n), 1)
    eye = (i == j).astype(F32)
    size = 1
    inv_list = [eye for _ in a_list]
    while size < n:
        pair = jnp.logical_and(i // size == j // size + 1, (i // size) % 2 == 1)
        below = [jnp.where(pair, a, 0.0) for a in a_list]
        if size == 1:
            inv_list = [eye - b for b in below]
        else:
            half = [mm3(b, inv) for b, inv in zip(below, inv_list)]
            inv_list = [inv - mm3(inv, h) for inv, h in zip(inv_list, half)]
        size *= 2
    return inv_list


def lagged(ext, lag, rows):
    moved = pltpu.roll(ext, lag, 0) if lag else ext
    return moved[HALO : HALO + rows]


def lag_masks(rel):
    return [None] + [(rel >= lag).astype(F32) for lag in range(1, CONV)]


def filtered(ext, taps, masks, rows):
    total = None
    for lag in range(CONV):
        term = taps[lag : lag + 1, :] * lagged(ext, lag, rows)
        if masks[lag] is not None:
            term = term * masks[lag]
        total = term if total is None else total + term
    return total


MESH = pl.DeviceIdType.MESH


def flip(index, bit):
    return index + bit * (1 - 2 * (index // bit % 2))


def remote(src, dst, send, recv, seq, head):
    return pltpu.make_async_remote_copy(
        src_ref=src, dst_ref=dst, send_sem=send, recv_sem=recv, device_id=(seq, head), device_id_type=MESH
    )


def greet(devices, expected):
    barrier = pltpu.get_barrier_semaphore()
    for seq, head in devices:
        pl.semaphore_signal(barrier, inc=1, device_id=(seq, head), device_id_type=MESH)
    pl.semaphore_wait(barrier, expected)


class Pieces:
    def __init__(self, count, local):
        self.local = local
        self.per = local // PIECE
        self.total = count * self.per
        self.seq, self.head = lax.axis_index("seq"), lax.axis_index("head")
        self.far, self.near = flip(self.head, 2), flip(self.head, 1)

    def mine(self, k):
        return k // self.per, pl.ds(pl.multiple_of(k % self.per * PIECE, PIECE), PIECE)

    def block(self, ref, k, owner, tiled, first=0):
        if tiled:
            return ref.at[k, pl.ds(pl.multiple_of(owner * PIECE, PIECE), PIECE), :]
        start = first + owner * self.local + k % self.per * PIECE
        return ref.at[k // self.per, pl.ds(pl.multiple_of(start, 16), PIECE), :]


class HeadGather:
    def __init__(self, pieces, out_ref, tiled, first, send, recv):
        self.pieces, self.out, self.tiled, self.first = pieces, out_ref, tiled, first
        self.send, self.recv = send, recv

    def place(self, k, owner):
        return self.pieces.block(self.out, k, owner, self.tiled, self.first)

    def copy(self, kind, k):
        p = self.pieces
        owner = p.far if kind == 2 else p.head
        target = p.near if kind else p.far
        ref = self.place(k, owner)
        return remote(ref, ref, self.send.at[kind, k], self.recv.at[kind, k], p.seq, target)

    def own(self, k):
        self.copy(0, k).start()
        self.copy(1, k).start()

    def forward(self, k):
        self.copy(0, k).wait_recv()
        self.copy(2, k).start()

    def arrived(self, k):
        self.copy(1, k).wait_recv()
        self.copy(2, k).wait_recv()

    def sent(self, k):
        for kind in range(3):
            self.copy(kind, k).wait_send()


class HeadScatter:
    def __init__(self, pieces, part_ref, tiled, near_ref, stage_ref, far_ref, send, recv):
        self.pieces, self.part, self.tiled = pieces, part_ref, tiled
        self.nearby, self.stage, self.faraway = near_ref, stage_ref, far_ref
        self.send, self.recv = send, recv

    def block(self, k, owner):
        return self.pieces.block(self.part, k, owner, self.tiled)

    def copy(self, kind, k):
        p = self.pieces
        if kind == 2:
            return remote(
                self.stage.at[k], self.faraway.at[k], self.send.at[2, k], self.recv.at[2, k], p.seq, p.far
            )
        owner = p.near if kind else flip(p.near, 2)
        return remote(
            self.block(k, owner), self.nearby.at[kind, k], self.send.at[kind, k], self.recv.at[kind, k], p.seq, p.near
        )

    def start(self, k):
        self.copy(0, k).start()
        self.copy(1, k).start()

    def forward(self, k):
        self.copy(0, k).wait_recv()
        total = self.block(k, self.pieces.far)[...].astype(F32) + self.nearby[0, k].astype(F32)
        self.stage[k] = total.astype(BF16)
        self.copy(2, k).start()

    def total(self, k):
        self.copy(1, k).wait_recv()
        self.copy(2, k).wait_recv()
        near = self.block(k, self.pieces.head)[...].astype(F32) + self.nearby[1, k].astype(F32)
        return near + self.faraway[k].astype(F32)

    def sent(self, k):
        for kind in range(3):
            self.copy(kind, k).wait_send()


def each(count, *steps):
    for step in steps:
        pl.loop(0, count)(step)


def scatter_scratch(count, local, width):
    n = count * local // PIECE
    return [
        pltpu.VMEM((2, n, PIECE, width), BF16),
        pltpu.VMEM((n, PIECE, width), BF16),
        pltpu.VMEM((n, PIECE, width), BF16),
        pltpu.SemaphoreType.DMA((3, n)),
        pltpu.SemaphoreType.DMA((3, n)),
    ]


def gather_scratch(count, local):
    n = count * local // PIECE
    return [pltpu.SemaphoreType.DMA((3, n)), pltpu.SemaphoreType.DMA((3, n))]


class Compose:
    def __init__(self, shards, heads, trans_ref, state_ref, out_ref, back_x_ref, back_y_ref, scratch):
        self.shards, self.heads = shards, heads
        self.trans, self.state, self.out, self.back_x, self.back_y = trans_ref, state_ref, out_ref, back_x_ref, back_y_ref
        self.stage, self.got, self.got_back, self.tx, self.s, self.send, self.recv = scratch
        self.seq, self.head = lax.axis_index("seq"), lax.axis_index("head")
        self.steps = [1 << k for k in range((shards - 1).bit_length())]

    def peer(self, distance):
        return lax.rem(self.seq + self.shards + distance, self.shards)

    def peers(self):
        return [(self.peer(-d), self.head) for d in self.steps] + [(self.peer(d), self.head) for d in self.steps[:-1]]

    def copies(self, m, k):
        d = self.steps[k]
        here = pl.ds(m * self.heads, self.heads)
        final = k == len(self.steps) - 1
        out = []
        for part in range(1 if final else 3):
            if part == 2:
                src = self.trans if k == 0 else self.back_y.at[k - 1]
                dst = self.got_back.at[k]
            else:
                src = (self.state, self.trans)[part] if k == 0 else self.stage.at[k - 1, part]
                dst = self.got.at[k, part]
            to = self.peer(-d if part == 2 else d)
            sems = self.send.at[part, k, m], self.recv.at[part, k, m]
            out.append(remote(src.at[here], dst.at[here], *sems, to, self.head))
        return out

    def begin(self, m, k):
        for c in self.copies(m, k):
            c.start()

    def turn(self, m, k):
        n = len(self.steps)
        if k == 0:
            self.begin(m, 0)
            return
        for c in self.copies(m, k - 1):
            c.wait_recv()
        k -= 1
        final = k == n - 1
        here = (self.seq >= self.steps[k]).astype(F32)
        here_back = (self.seq + self.steps[k] < self.shards).astype(F32)
        groups = range(m * self.heads, (m + 1) * self.heads)
        pairs = {}
        for g in groups:
            state = self.got[k, 0, g].astype(F32) * here
            if final:
                self.out[g] = state if k == 0 else self.out[g] + mm(self.tx[g], state)
                continue
            pairs[g] = jnp.concatenate([self.got[k, 1, g].astype(F32) * here, state], axis=1).astype(BF16)
            old_t = self.trans[g] if k == 0 else self.stage[k - 1, 1, g]
            old_s = self.state[g].astype(F32) if k == 0 else self.s[g]
            both = mm(old_t, pairs[g])
            new_s = old_s + both[:, HEAD_DIM:]
            self.s[g] = new_s
            self.stage[k, 0, g] = new_s.astype(BF16)
            self.stage[k, 1, g] = both[:, :HEAD_DIM].astype(BF16)
            later = (self.got_back[k, g].astype(F32) * here_back).astype(BF16)
            self.back_x[k, g] = later if k == 0 else mm(later, self.back_x[k - 1, g]).astype(BF16)
            self.back_y[k, g] = mm(later, self.trans[g] if k == 0 else self.back_y[k - 1, g]).astype(BF16)
        if final:
            return
        self.begin(m, k + 1)
        for g in groups:
            if k == 0:
                self.out[g] = pairs[g][:, HEAD_DIM:].astype(F32)
                self.tx[g] = pairs[g][:, :HEAD_DIM]
            else:
                both = mm(self.tx[g], pairs[g])
                self.out[g] += both[:, HEAD_DIM:]
                self.tx[g] = both[:, :HEAD_DIM].astype(BF16)

    def sent(self, count):
        for m in range(count):
            for k in range(len(self.steps)):
                for c in self.copies(m, k):
                    c.wait_send()

    def script(self, m):
        return [functools.partial(self.turn, m, k) for k in range(len(self.steps) + 1)]


def compose_scratch(shards, count, flat):
    rounds = (shards - 1).bit_length()
    more = max(rounds - 1, 1)
    return [
        pltpu.VMEM((more, 2) + flat, BF16),
        pltpu.VMEM((rounds, 2) + flat, BF16),
        pltpu.VMEM((more,) + flat, BF16),
        pltpu.VMEM(flat, BF16),
        pltpu.VMEM(flat, F32),
        pltpu.SemaphoreType.DMA((3, rounds, count)),
        pltpu.SemaphoreType.DMA((3, rounds, count)),
    ]


class ComposeBack:
    def __init__(self, shards, heads, trans_ref, state_ref, back_x_ref, back_y_ref, out_ref, scratch):
        self.shards, self.heads = shards, heads
        self.trans, self.state, self.back_x, self.back_y, self.out = trans_ref, state_ref, back_x_ref, back_y_ref, out_ref
        self.stage, self.got, self.s, self.send, self.recv = scratch
        self.seq, self.head = lax.axis_index("seq"), lax.axis_index("head")
        self.steps = [1 << k for k in range((shards - 1).bit_length())]

    def peer(self, distance):
        return lax.rem(self.seq + self.shards + distance, self.shards)

    def peers(self):
        return [(self.peer(d), self.head) for d in self.steps]

    def copy(self, m, k):
        here = pl.ds(m * self.heads, self.heads)
        src = self.state if k == 0 else self.stage.at[k - 1]
        dst = self.got.at[k]
        return remote(
            src.at[here], dst.at[here], self.send.at[k, m], self.recv.at[k, m], self.peer(-self.steps[k]), self.head
        )

    def begin(self, m, k):
        self.copy(m, k).start()

    def turn(self, m, k):
        n = len(self.steps)
        if k == 0:
            self.begin(m, 0)
            return
        k -= 1
        self.copy(m, k).wait_recv()
        here = (self.seq + self.steps[k] < self.shards).astype(F32)
        groups = range(m * self.heads, (m + 1) * self.heads)
        states = [(self.got[k, g].astype(F32) * here).astype(BF16) for g in groups]
        if k + 1 < n:
            for g, state in zip(groups, states):
                trans = self.trans[g] if k == 0 else self.back_y[k - 1, g]
                new_s = (self.state[g].astype(F32) if k == 0 else self.s[g]) + mm(trans, state, 0, 0)
                self.s[g] = new_s
                self.stage[k, g] = new_s.astype(BF16)
            self.begin(m, k + 1)
        for g, state in zip(groups, states):
            if k == 0:
                self.out[g] = state.astype(F32)
            else:
                self.out[g] += mm(self.back_x[k - 1, g], state, 0, 0)

    def sent(self, count):
        for m in range(count):
            for k in range(len(self.steps)):
                self.copy(m, k).wait_send()


def compose_back_scratch(shards, count, flat):
    rounds = (shards - 1).bit_length()
    return [
        pltpu.VMEM((max(rounds - 1, 1),) + flat, BF16),
        pltpu.VMEM((rounds,) + flat, BF16),
        pltpu.VMEM(flat, F32),
        pltpu.SemaphoreType.DMA((rounds, count)),
        pltpu.SemaphoreType.DMA((rounds, count)),
    ]


class LineGather:
    def __init__(self, shards, src_ref, place, send, recv, local):
        self.shards, self.src, self.place = shards, src_ref, place
        self.send, self.recv, self.local = send, recv, local
        self.seq, self.head = lax.axis_index("seq"), lax.axis_index("head")
        self.neighbour = flip(self.seq, 1)
        self.half = shards // 2

    def on_line(self, distance, base=None):
        base = self.seq if base is None else base
        return lax.rem(base + self.shards + 2 * distance, self.shards)

    def peers(self):
        return [(self.on_line(-d), self.head) for d in range(1, self.half)] + [(self.neighbour, self.head)]

    def along(self, member, d, block):
        sems = self.send.at[member, d], self.recv.at[member, d]
        return remote(self.src.at[member], self.place(member, block), *sems, self.on_line(d), self.head)

    def across(self, member, d, block):
        dst = self.place(member, block)
        sems = self.send.at[member, self.half + d], self.recv.at[member, self.half + d]
        return remote(dst if d else self.src.at[member], dst, *sems, self.neighbour, self.head)

    def mine(self, member):
        return pltpu.make_async_copy(self.src.at[member], self.place(member, self.seq), self.local.at[member])

    def start(self, member):
        self.mine(member).start()
        for d in range(1, self.half):
            self.along(member, d, self.seq).start()
        self.across(member, 0, self.seq).start()

    def forward(self, member):
        for d in range(1, self.half):
            block = self.on_line(-d)
            self.along(member, d, block).wait_recv()
            self.across(member, d, block).start()

    def arrived(self, member):
        self.mine(member).wait()
        for d in range(self.half):
            self.across(member, d, self.on_line(-d, self.neighbour)).wait_recv()

    def sent(self, member):
        for d in range(1, self.half):
            self.along(member, d, self.seq).wait_send()
        for d in range(self.half):
            self.across(member, d, self.on_line(-d)).wait_send()

    def finish(self, member):
        self.arrived(member)
        self.sent(member)


def mix_fwd_body(
    shards, count, heads, token_heads, extra, off_ref, len_ref, base_ref, w_ref, beta_ref, taps_ref, in_ref, gain_ref, top_ref, own_ref,
    pq_ref, pk_ref, pv_ref, rate_ref, ps_ref, oloc_ref, phi_ref, psi_ref, m_ref, inv_ref, wr_ref, up_ref,
    trans_ref, enter_ref, back_x_ref, back_y_ref, all_x_out, all_top_out, *refs,
):
    full_ref, refs = (refs[0], refs[1:]) if extra else (None, refs)
    all_x_ref, all_top_ref, out_sems, state_ref, x_send, x_recv, gather_send, gather_recv, halo_send, halo_recv, *refs = refs
    scratch, sems = refs[:7], refs[7:]
    mb = pl.program_id(0)
    head = pl.program_id(1)
    grid_step = mb * heads + head
    steps = count * heads
    local = in_ref.shape[1]
    pieces = Pieces(count, local)
    gather_x = HeadGather(pieces, all_x_ref, False, HALO, x_send, x_recv)
    gather = HeadGather(pieces, all_top_ref, True, 0, gather_send, gather_recv)
    rounds = Compose(shards, heads, trans_ref, state_ref, enter_ref, back_x_ref, back_y_ref, scratch)
    line = LineGather(shards, own_ref, lambda member, q: full_ref.at[q, member], *sems) if extra else None
    last = pieces.head == token_heads - 1

    def halo(target):
        src = all_x_ref.at[:, pl.ds(token_heads * local, HALO), :]
        dst = all_x_ref.at[:, pl.ds(0, HALO), :]
        return remote(src, dst, halo_send.at[target], halo_recv, lax.rem(pieces.seq + 1, shards), target)

    def some(act, first, stop):
        pl.loop(first, stop)(act)

    def write_out(i):
        src, dst = ((all_x_ref, all_x_out), (all_top_ref, all_top_out))[i]
        return pltpu.make_async_copy(src, dst, out_sems.at[i])

    @pl.when(grid_step == 0)
    def _():
        for k in range(pieces.total):
            m, here = pieces.mine(k)
            x = in_ref[m, here, :].astype(F32)
            gather_x.place(k, pieces.head)[...] = rms(x, gain_ref[...]).astype(BF16)
            gather.place(k, pieces.head)[...] = top_ref[m, here, :]
        before = lax.rem(pieces.seq + shards - 1, shards)
        peers = rounds.peers() + (line.peers() if extra else []) + [(pieces.seq, pieces.far), (pieces.seq, pieces.near)]
        greet(peers + [(before, token_heads - 1)], len(peers) + token_heads * last.astype(jnp.int32))
        some(gather_x.own, 0, pieces.per)

        @pl.when(last)
        def _():
            for target in range(token_heads):
                halo(target).start()

        some(gather_x.own, pieces.per, pieces.total)
        if extra:
            for member in range(2):
                line.start(member)
        some(gather_x.forward, 0, pieces.per)
        some(gather_x.arrived, 0, pieces.per)
        halo(0).wait_recv()

    @pl.when(grid_step == min(1, steps - 1))
    def _():
        some(gather_x.forward, pieces.per, pieces.total)
        each(pieces.total, gather.own)

    @pl.when(grid_step == min(heads, steps - 1))
    def _():
        some(gather_x.arrived, pieces.per, pieces.total)
        write_out(0).start()

    if extra:
        for at, member in ((1, 0), (steps - 1, 1)):

            @pl.when(grid_step == at)
            def _(member=member):
                line.forward(member)

    left = []
    plan = {}
    for m in range(count):
        turns = rounds.script(m)
        if m + 1 < count:
            places = [((m + 1) * heads - 1, 1), ((m + 1) * heads, 1)]
            for place in places:
                if turns:
                    plan.setdefault(place, []).append(turns.pop(0))
        left.append(turns)

    def advance(point):
        for (at, where), turns in plan.items():
            if where == point:

                @pl.when(grid_step == at)
                def _(turns=turns):
                    for turn in turns:
                        turn()

    rows = all_x_ref.shape[1] - HALO
    rel, valid = row_info(off_ref, len_ref, mb, base_ref[0], rows)
    x = all_x_ref[mb]
    masks = lag_masks(rel)
    acts = []
    for member, out in enumerate((pq_ref, pk_ref, pv_ref)):
        proj = mm(x, w_ref[member]).astype(BF16)
        out[0] = proj
        filt = filtered(proj.astype(F32), taps_ref[member].astype(F32), masks, rows)
        acts.append(filt * sigmoid(filt))
    query, key, value = acts
    query = query * lax.rsqrt(jnp.sum(query * query, axis=-1, keepdims=True) + EPS)
    key = key * lax.rsqrt(jnp.sum(key * key, axis=-1, keepdims=True) + EPS)
    raw_all = mm(x, beta_ref[...], 1, 1)[HALO:]
    lane = lax.broadcasted_iota(jnp.int32, raw_all.shape, 1)
    raw = jnp.sum(jnp.where(lane == head, raw_all, 0.0), axis=-1, keepdims=True)
    rate_ref[0, 0] = raw
    rate = sigmoid(raw) * valid
    spans = [slice(c * CHUNK, (c + 1) * CHUNK) for c in range(rows // CHUNK)]
    all_masks = [chunk_masks(rel[s]) for s in spans]
    systems, scores = [], []
    for s, (strict, incl, _, _, _) in zip(spans, all_masks):
        both = mm(jnp.concatenate([query[s], key[s]], axis=0), key[s], 1, 1)
        scores.append(jnp.where(incl, both[:CHUNK], 0.0))
        systems.append(jnp.where(strict, rate[s] * both[CHUNK:], 0.0))
    advance(0)
    inverses = unit_lower_inverse(systems)
    i = lax.broadcasted_iota(jnp.int32, (HEAD_DIM, HEAD_DIM), 0)
    j = lax.broadcasted_iota(jnp.int32, (HEAD_DIM, HEAD_DIM), 1)
    eye = (i == j).astype(F32)
    phis, psis, ps, olocs = [], [], [], []
    for s, masks_c, inv, score in zip(spans, all_masks, inverses, scores):
        _, _, sees, stays, keep = masks_c
        right = rate[s] * jnp.concatenate([sees * key[s], value[s]], axis=1)
        solved = mm(inv, right)
        write, update = solved[:, :HEAD_DIM], solved[:, HEAD_DIM:]
        moved = mm(stays * key[s], solved, 0, 0)
        phi = keep * eye - moved[:, :HEAD_DIM]
        psi = moved[:, HEAD_DIM:]
        scored = mm(score, solved)
        p = sees * query[s] - scored[:, :HEAD_DIM]
        m_ref[0, 0, s] = score.astype(BF16)
        inv_ref[0, 0, s] = inv.astype(BF16)
        wr_ref[0, 0, s] = write.astype(BF16)
        up_ref[0, 0, s] = update
        ps_ref[0, 0, s] = p.astype(BF16)
        oloc_ref[0, 0, s] = scored[:, HEAD_DIM:]
        phi_ref[0, 0, s] = phi
        psi_ref[0, 0, s] = psi
        phis.append(phi)
        psis.append(psi)
    trans, state = phis[0], psis[0]
    for phi, psi in zip(phis[1:], psis[1:]):
        both = mm3(phi, jnp.concatenate([trans, state], axis=1))
        trans = both[:, :HEAD_DIM]
        state = both[:, HEAD_DIM:] + psi
    trans_ref[grid_step] = trans.astype(BF16)
    state_ref[grid_step] = state.astype(BF16)
    advance(1)

    @pl.when(grid_step == count * heads - 1)
    def _():
        each(pieces.total, gather.forward)
        while any(left):
            for turns in left:
                if turns:
                    turns.pop(0)()
        rounds.sent(count)
        each(pieces.total, gather.arrived)
        write_out(1).start()
        each(pieces.total, gather.sent, gather_x.sent)
        write_out(0).wait()
        write_out(1).wait()

        @pl.when(last)
        def _():
            for target in range(token_heads):
                halo(target).wait_send()

        if extra:
            for member in range(2):
                line.finish(member)


def cost(us):
    return pl.CostEstimate(flops=0, bytes_accessed=int(us * 3.0e6), transcendentals=0)


def any_spec():
    return pl.BlockSpec(memory_space=pl.ANY)


def smem_spec():
    return pl.BlockSpec(memory_space=pltpu.SMEM)


def params(count, collective=None):
    return pltpu.CompilerParams(
        dimension_semantics=("arbitrary",) * count,
        vmem_limit_bytes=VMEM_LIMIT,
        collective_id=collective,
        has_side_effects=collective is not None,
    )


def line_scratch(shards):
    return [pltpu.SemaphoreType.DMA((3, shards))] * 2 + [pltpu.SemaphoreType.DMA((3,))]


def mix_fwd(offsets, lengths, base, mixer_weights, beta_weight, taps, inputs, gain, top, dense_weights, shards, extra):
    count, local, width = inputs.shape
    token_heads = lax.axis_size("head")
    rows = local * token_heads
    ext_rows = rows + HALO
    heads = beta_weight.shape[0]
    per_head = pl.BlockSpec((1, 1, rows, HEAD_DIM), lambda m, h: (m, h, 0, 0))
    proj_spec = pl.BlockSpec((1, ext_rows, HEAD_DIM), lambda m, h: (m, 0, h))
    proj_shape = jax.ShapeDtypeStruct((count, ext_rows, heads * HEAD_DIM), BF16)

    def big(kind):
        return jax.ShapeDtypeStruct((count, heads, rows, HEAD_DIM), kind)

    flat = (count * heads, HEAD_DIM, HEAD_DIM)
    more = max((shards - 1).bit_length() - 1, 1)
    all_x = (count, ext_rows, width)
    all_top = (count * local // PIECE, PIECE * token_heads, width)
    shapes = [
        jax.ShapeDtypeStruct(flat, BF16),
        jax.ShapeDtypeStruct(flat, F32),
        jax.ShapeDtypeStruct((more,) + flat, BF16),
        jax.ShapeDtypeStruct((more,) + flat, BF16),
        jax.ShapeDtypeStruct(all_x, BF16),
        jax.ShapeDtypeStruct(all_top, BF16),
    ]
    more_shapes = [jax.ShapeDtypeStruct((shards, 2) + dense_weights.shape[1:], BF16)] if extra else []
    shapes += more_shapes
    line_sems = line_scratch(shards) if extra else []
    return pl.pallas_call(
        functools.partial(mix_fwd_body, shards, count, heads, token_heads, extra),
        grid=(count, heads),
        in_specs=[
            smem_spec(), smem_spec(), smem_spec(),
            pl.BlockSpec((3, width, HEAD_DIM), lambda m, h: (0, 0, h)),
            pl.BlockSpec(beta_weight.shape, lambda m, h: (0, 0)),
            pl.BlockSpec((3, CONV, HEAD_DIM), lambda m, h: (0, 0, h)),
        ]
        + vmem_specs(3)
        + [any_spec()],
        out_specs=[proj_spec] * 3
        + [pl.BlockSpec((1, 1, rows, 1), lambda m, h: (m, h, 0, 0))]
        + [per_head] * 8
        + vmem_specs(4)
        + [any_spec()] * (len(shapes) - 4),
        out_shape=[proj_shape] * 3
        + [jax.ShapeDtypeStruct((count, heads, rows, 1), F32)]
        + [big(BF16), big(F32), big(F32), big(F32), big(BF16), big(BF16), big(BF16), big(F32)]
        + shapes,
        scratch_shapes=[
            pltpu.VMEM(all_x, BF16), pltpu.VMEM(all_top, BF16), pltpu.SemaphoreType.DMA((2,)), pltpu.VMEM(flat, BF16)
        ]
        + gather_scratch(count, local) * 2
        + [pltpu.SemaphoreType.DMA((token_heads,)), pltpu.SemaphoreType.DMA]
        + compose_scratch(shards, count, flat)
        + line_sems,
        compiler_params=params(2, 4),
        cost_estimate=cost(45),
        name="mix_fwd",
    )(offsets, lengths, base, mixer_weights, beta_weight, taps, inputs, gain, top, dense_weights)


def mix_out_body(state_ref, ps_ref, oloc_ref, phi_ref, psi_ref, gain_ref, w_ref, start_ref, mixed_ref, head_ref, part_ref):
    heads = ps_ref.shape[1]
    rows = ps_ref.shape[2]
    gain = gain_ref[...]
    states = [state_ref[0, h] for h in range(heads)]
    for c in range(rows // CHUNK):
        s = slice(c * CHUNK, (c + 1) * CHUNK)
        for h in range(heads):
            state = states[h]
            start_ref[0, h, s] = state.astype(BF16)
            mixed = oloc_ref[0, h, s] + mm(ps_ref[0, h, s], state)
            mixed_ref[0, h, s] = mixed
            normed = mixed * lax.rsqrt(jnp.mean(mixed * mixed, axis=-1, keepdims=True) + EPS) * gain
            head_ref[0, s, h * HEAD_DIM : (h + 1) * HEAD_DIM] = normed.astype(BF16)
            states[h] = mm3(phi_ref[0, h, s], state) + psi_ref[0, h, s]
    part_ref[0] = mm(head_ref[0], w_ref[0], 1, 1).astype(BF16)


def mix_out(state_in, ps, oloc, phi, psi, out_gain, mixer_weights):
    count, heads, rows, _ = ps.shape
    width = mixer_weights.shape[1]
    head_width = mixer_weights.shape[2]
    per_mb = pl.BlockSpec((1, heads, rows, HEAD_DIM), lambda m: (m, 0, 0, 0))
    return pl.pallas_call(
        mix_out_body,
        grid=(count,),
        in_specs=[
            pl.BlockSpec((1, heads, HEAD_DIM, HEAD_DIM), lambda m: (m, 0, 0, 0)),
            per_mb, per_mb, per_mb, per_mb,
            pl.BlockSpec((1, HEAD_DIM), lambda m: (0, 0)),
            pl.BlockSpec((1, width, head_width), lambda m: (3, 0, 0)),
        ],
        out_specs=[
            per_mb, per_mb,
            pl.BlockSpec((1, rows, head_width), lambda m: (m, 0, 0)),
            pl.BlockSpec((1, rows, width), lambda m: (m, 0, 0)),
        ],
        out_shape=[
            jax.ShapeDtypeStruct(ps.shape, BF16),
            jax.ShapeDtypeStruct(ps.shape, F32),
            jax.ShapeDtypeStruct((count, rows, head_width), BF16),
            jax.ShapeDtypeStruct((count, rows, width), BF16),
        ],
        compiler_params=params(1),
        cost_estimate=cost(5),
        name="mix_out",
    )(state_in, ps, oloc, phi, psi, out_gain, mixer_weights)


def mix_grad_body(
    shards, count, heads,
    off_ref, len_ref, base_ref, pq_ref, pk_ref, pv_ref, rate_ref, taps_ref, start_ref,
    m_ref, inv_ref, wr_ref, up_ref,
    grad_ref, wo_ref, mixed_ref, gain_ref, all_ps_ref, all_phi_ref, trans_ref, back_x_ref, back_y_ref,
    gq_ref, gk_ref, gv_ref, tail_ref, rim_ref, grate_ref, gtaps_ref, gain_grad_ref,
    dstate_ref, dend_ref, all_dout_ref, *scratch,
):
    mb = pl.program_id(0)
    head = pl.program_id(1)
    grid_step = mb * heads + head
    rounds = ComposeBack(shards, heads, trans_ref, dstate_ref, back_x_ref, back_y_ref, dend_ref, scratch)
    n = len(rounds.steps)
    late = [1] if count > 1 else []

    def mix_back(m):
        gain = gain_ref[...]
        grad_head = mm(grad_ref[m], wo_ref[0])
        states = [None] * heads
        for h in range(heads):
            e = grad_head[:, h * HEAD_DIM : (h + 1) * HEAD_DIM]
            v = mixed_ref[m, h]
            r = lax.rsqrt(jnp.mean(v * v, axis=-1, keepdims=True) + EPS)
            weighted = e * gain
            dout = r * weighted - v * (r * r * r * jnp.mean(weighted * v, axis=-1, keepdims=True))
            gain_grad_ref[...] += jnp.sum(e * v * r, axis=0, keepdims=True)
            all_dout_ref[m * heads + h] = dout.astype(BF16)
        for c in reversed(range(all_ps_ref.shape[2] // CHUNK)):
            s = slice(c * CHUNK, (c + 1) * CHUNK)
            for h in range(heads):
                new = mm(all_ps_ref[m, h, s], all_dout_ref[m * heads + h, s], 0, 0)
                if states[h] is not None:
                    new += mm3(all_phi_ref[m, h, s], states[h], 0, 0)
                states[h] = new
        for h in range(heads):
            dstate_ref[m * heads + h] = states[h].astype(BF16)

    @pl.when(grid_step == 0)
    def _():
        gain_grad_ref[...] = jnp.zeros_like(gain_grad_ref)
        gtaps_ref[...] = jnp.zeros_like(gtaps_ref)
        greet(rounds.peers(), n)
        for m in range(count):
            mix_back(m)
            rounds.turn(m, 0)
        for k in range(1, n + 1):
            for m in range(count):
                if m not in late:
                    rounds.turn(m, k)
            for m in late:
                if k > 1:
                    rounds.turn(m, k - 1)

    rows = rate_ref.shape[2]
    rel, valid = row_info(off_ref, len_ref, mb, base_ref[0], rows)
    masks = lag_masks(rel)
    projs, filts, sigs, acts = [], [], [], []
    for member, ref in enumerate((pq_ref, pk_ref, pv_ref)):
        proj = ref[0].astype(F32)
        filt = filtered(proj, taps_ref[member].astype(F32), masks, rows)
        sg = sigmoid(filt)
        projs.append(proj)
        filts.append(filt)
        sigs.append(sg)
        acts.append(filt * sg)
    rq = lax.rsqrt(jnp.sum(acts[0] * acts[0], axis=-1, keepdims=True) + EPS)
    rk = lax.rsqrt(jnp.sum(acts[1] * acts[1], axis=-1, keepdims=True) + EPS)
    query = acts[0] * rq
    key = acts[1] * rk
    value = acts[2]
    sig_rate = sigmoid(rate_ref[0, 0])
    rate = sig_rate * valid
    spans = [slice(c * CHUNK, (c + 1) * CHUNK) for c in range(rows // CHUNK)]
    dstates = [None] * len(spans)
    dstate = dend_ref[grid_step]
    for c in reversed(range(len(spans))):
        s = spans[c]
        dstates[c] = dstate
        if c:
            dstate = mm3(all_phi_ref[mb, head, s], dstate, 0, 0) + mm(all_ps_ref[mb, head, s], all_dout_ref[grid_step, s], 0, 0)
    dqs, dks, dvs, drates = [], [], [], []
    for c, s in enumerate(spans):
        strict, incl, sees, stays, _ = chunk_masks(rel[s])
        q, k, v, b = query[s], key[s], value[s], rate[s]
        dout = all_dout_ref[grid_step, s]
        start = start_ref[0, 0, s]
        fresh = up_ref[0, 0, s] - mm(wr_ref[0, 0, s], start)
        dfresh = mm(m_ref[0, 0, s], dout, 0, 0) + mm(stays * k, dstates[c])
        e = mm(inv_ref[0, 0, s], dfresh, 0, 0)
        left = jnp.concatenate([dout, e.astype(BF16)], axis=0)
        right = jnp.concatenate([fresh.astype(BF16), start], axis=0)
        outer = mm(left, right, 1, 1)
        dscore = jnp.where(incl, outer[:CHUNK, :CHUNK], 0.0)
        dsystem = jnp.where(strict, -outer[CHUNK:, :CHUNK], 0.0)
        grads = jnp.concatenate([dscore, dsystem], axis=0).astype(BF16)
        byk = mm(grads, k)
        z = byk[CHUNK:] - sees * outer[CHUNK:, CHUNK:]
        dqs.append(sees * outer[:CHUNK, CHUNK:] + byk[:CHUNK])
        dk = mm(grads, jnp.concatenate([q, b * k], axis=0), 0, 0)
        dks.append(dk + stays * mm(fresh, dstates[c], 1, 1) + b * z)
        dvs.append(b * e)
        drates.append(jnp.sum(e * v + k * z, axis=-1, keepdims=True))
    dq = jnp.concatenate(dqs, axis=0)
    dk = jnp.concatenate(dks, axis=0)
    dv = jnp.concatenate(dvs, axis=0)
    drate = jnp.concatenate(drates, axis=0)
    grate_ref[0, 0] = drate * valid * sig_rate * (1.0 - sig_rate)
    dacts = [
        rq * dq - acts[0] * (rq * rq * rq * jnp.sum(dq * acts[0], axis=-1, keepdims=True)),
        rk * dk - acts[1] * (rk * rk * rk * jnp.sum(dk * acts[1], axis=-1, keepdims=True)),
        dv,
    ]
    for member, out in enumerate((gq_ref, gk_ref, gv_ref)):
        sg = sigs[member]
        dfilt = dacts[member] * (sg * (1.0 + filts[member] * (1.0 - sg)))
        taps = taps_ref[member].astype(F32)
        total = None
        pieces = []
        for lag in range(CONV):
            masked = dfilt if lag == 0 else dfilt * masks[lag]
            pieces.append(jnp.sum(masked * lagged(projs[member], lag, rows), axis=0, keepdims=True))
            scaled = masked * taps[lag : lag + 1, :]
            ext = jnp.concatenate([jnp.zeros((RIM, HEAD_DIM), F32), scaled], axis=0)
            if lag:
                ext = pltpu.roll(ext, rows + RIM - lag, 0)
            total = ext if total is None else total + ext
        here = total[RIM:]
        out[0] = here.astype(BF16)
        tail_ref[0, member] = here[rows - RIM :]
        rim_ref[0, member] = total[:RIM]
        lanes = pl.ds(pl.multiple_of(head * HEAD_DIM, HEAD_DIM), HEAD_DIM)
        gtaps_ref[member, :, lanes] += jnp.concatenate(pieces, axis=0)

    @pl.when(grid_step == 0)
    def _():
        for m in late:
            rounds.turn(m, n)

    @pl.when(grid_step == count * heads - 1)
    def _():
        rounds.sent(count)


def mix_grad(
    offsets, lengths, base, proj3, rates, taps, start, m, inv, wr, up,
    grad_attn, mixer_weights, mixed, out_gain, ps, phi, trans, back_x, back_y, shards,
):
    count, heads, rows, _ = ps.shape
    ext_rows = rows + HALO
    width = mixer_weights.shape[1]
    head_width = mixer_weights.shape[2]
    flat = (count * heads, HEAD_DIM, HEAD_DIM)
    per_head = pl.BlockSpec((1, 1, rows, HEAD_DIM), lambda m, h: (m, h, 0, 0))
    proj_spec = pl.BlockSpec((1, ext_rows, HEAD_DIM), lambda m, h: (m, 0, h))
    out_spec = pl.BlockSpec((1, rows, HEAD_DIM), lambda m, h: (m, 0, h))
    rate_spec = pl.BlockSpec((1, 1, rows, 1), lambda m, h: (m, h, 0, 0))
    small = pl.BlockSpec((1, 3, RIM, HEAD_DIM), lambda m, h: (m, 0, 0, h))
    small_shape = jax.ShapeDtypeStruct((count, 3, RIM, head_width), F32)
    return pl.pallas_call(
        functools.partial(mix_grad_body, shards, count, heads),
        grid=(count, heads),
        in_specs=[
            smem_spec(), smem_spec(), smem_spec(),
            proj_spec, proj_spec, proj_spec, rate_spec,
            pl.BlockSpec((3, CONV, HEAD_DIM), lambda m, h: (0, 0, h)),
        ]
        + [per_head] * 5
        + vmem_specs(1)
        + [pl.BlockSpec((1, width, head_width), lambda m, h: (3, 0, 0))]
        + vmem_specs(7),
        out_specs=[out_spec] * 3 + [small, small, rate_spec] + vmem_specs(2),
        out_shape=[jax.ShapeDtypeStruct((count, rows, head_width), BF16)] * 3
        + [
            small_shape, small_shape,
            jax.ShapeDtypeStruct(rates.shape, F32),
            jax.ShapeDtypeStruct(taps.shape, F32),
            jax.ShapeDtypeStruct((1, HEAD_DIM), F32),
        ],
        scratch_shapes=[
            pltpu.VMEM(flat, BF16),
            pltpu.VMEM(flat, F32),
            pltpu.VMEM((count * heads, rows, HEAD_DIM), BF16),
        ]
        + compose_back_scratch(shards, count, flat),
        compiler_params=params(2, 5),
        cost_estimate=cost(45),
        name="mix_grad",
    )(
        offsets, lengths, base, *proj3, rates, taps, start, m, inv, wr, up,
        grad_attn, mixer_weights, mixed, out_gain, ps, phi, trans, back_x, back_y,
    )


def rms(values, gain):
    return values * lax.rsqrt(jnp.mean(values * values, axis=-1, keepdims=True) + EPS) * gain


def rms_back(grad, values, gain):
    inv = lax.rsqrt(jnp.mean(values * values, axis=-1, keepdims=True) + EPS)
    weighted = grad * gain
    grad_in = inv * weighted - values * inv**3 * jnp.mean(weighted * values, axis=-1, keepdims=True)
    return grad_in, jnp.sum(grad * values * inv, axis=0, keepdims=True)

def vmem_specs(count):
    return [pl.BlockSpec(memory_space=pltpu.VMEM)] * count


def comm_params(collective):
    return pltpu.CompilerParams(
        collective_id=collective, has_side_effects=True, vmem_limit_bytes=VMEM_LIMIT
    )


def dense_block_body(
    shards, extra, part_ref, x_ref, top_ref, all_top_ref, gain_ref, w_ref, own_ref,
    resid_ref, down_ref, grad_ref, mid_ref, out_ref, gain_grad_ref,
    wt_ref, wsem, acc_ref, in_ref, gin_ref, gate_ref, up_ref, *scratch,
):
    count, local, width = x_ref.shape
    groups = w_ref.shape[0]
    cut = width // groups
    ready = 2 if extra else 3
    pieces = Pieces(count, local)
    line = None
    if extra:
        line = LineGather(
            shards, own_ref, lambda i, q: wt_ref.at[i, :, pl.ds(pl.multiple_of(q * cut, cut), cut)], *scratch[14:]
        )
    first = HeadScatter(pieces, part_ref, False, *scratch[:5])
    spread = HeadGather(pieces, in_ref, True, 0, *scratch[5:7])
    second = HeadScatter(pieces, gin_ref, True, *scratch[7:12])
    back = HeadGather(pieces, out_ref, False, 0, *scratch[12:14])

    def weights(p):
        return pltpu.make_async_copy(w_ref.at[p, 0:ready], wt_ref.at[0:ready, :, pl.ds(p * cut, cut)], wsem.at[p])

    peers = line.peers() if extra else []
    for p in range(groups):
        weights(p).start()
    greet([(pieces.seq, pieces.far), (pieces.seq, pieces.near)] + peers, 2 + len(peers))
    n = pieces.total
    each(n, first.start)
    if extra:
        line.start(2)
    each(n, first.forward)
    gain_grad_ref[...] = jnp.zeros_like(gain_grad_ref)

    @pl.loop(0, n)
    def _(k):
        m, here = pieces.mine(k)
        resid = x_ref[m, here, :].astype(F32) + first.total(k)
        resid_ref[m, here, :] = resid
        spread.place(k, pieces.head)[...] = rms(resid, gain_ref[...]).astype(BF16)
        spread.own(k)

    for p in range(groups):
        weights(p).wait()

    def turn_back(k):
        m, here = pieces.mine(k)
        grad, gain_part = rms_back(second.total(k), resid_ref[m, here, :], gain_ref[...])
        mid = top_ref[m, here, :].astype(F32) + grad
        gain_grad_ref[...] += gain_part
        mid_ref[m, here, :] = mid
        back.place(k, pieces.head)[...] = mid.astype(BF16)
        back.own(k)

    spread.forward(0)
    if extra:
        line.forward(2)

    @pl.loop(0, n)
    def _(k):
        spread.arrived(k)
        x = in_ref[k]
        gate_ref[k] = mm(x, wt_ref[0], 1, 1)
        up_ref[k] = mm(x, wt_ref[1], 1, 1)

        @pl.when(k + 1 < n)
        def _():
            spread.forward(k + 1)

    if extra:
        line.arrived(2)

    @pl.loop(0, n)
    def _(k):
        x = in_ref[k]
        gate = gate_ref[k]
        up = up_ref[k]
        grad_hidden = mm(all_top_ref[k], wt_ref[2], 1, 1)
        sg = sigmoid(gate)
        silu = gate * sg
        hidden = (silu * up).astype(BF16)
        grad_gate = (grad_hidden * up * (sg * (1.0 + gate * (1.0 - sg)))).astype(BF16)
        grad_up = (grad_hidden * silu).astype(BF16)
        gin_ref[k] = (mm(grad_gate, wt_ref[0]) + mm(grad_up, wt_ref[1])).astype(BF16)
        second.start(k)
        down_ref[k] = mm(hidden, wt_ref[2]).astype(BF16)
        second.forward(k)
        adds = (mm(grad_gate, x, 0, 0), mm(grad_up, x, 0, 0), mm(hidden, all_top_ref[k], 0, 0))

        @pl.when(k == 0)
        def _():
            for i, add in enumerate(adds):
                acc_ref[i] = add

        @pl.when(jnp.logical_and(k > 0, k + 1 < n))
        def _():
            for i, add in enumerate(adds):
                acc_ref[i] += add

        @pl.when(k + 1 == n)
        def _():
            for i, add in enumerate(adds):
                total = (acc_ref[i] + add).astype(BF16)
                for p in range(groups):
                    grad_ref[p, i] = total[:, p * cut : (p + 1) * cut]

        @pl.when(k > 0)
        def _():
            turn_back(k - 1)

        @pl.when(k > 1)
        def _():
            back.forward(k - 2)

    turn_back(n - 1)
    back.forward(n - 2)
    back.forward(n - 1)
    each(n, back.arrived, back.sent, second.sent, spread.sent, first.sent)
    if extra:
        line.sent(2)


def dense_block(part, inputs, top, all_top, gain, weights, own, shards, extra):
    count, local, width = inputs.shape
    groups, _, hidden, cut = weights.shape
    n = count * local // PIECE
    tile = all_top.shape[1]
    rows = part.shape[1]
    return pl.pallas_call(
        functools.partial(dense_block_body, shards, extra),
        in_specs=vmem_specs(5) + [any_spec()] * 2,
        out_specs=vmem_specs(6),
        out_shape=[
            jax.ShapeDtypeStruct(inputs.shape, F32),
            jax.ShapeDtypeStruct((n, tile, width), BF16),
            jax.ShapeDtypeStruct((groups, 3, hidden, cut), BF16),
            jax.ShapeDtypeStruct(inputs.shape, F32),
            jax.ShapeDtypeStruct((count, rows, width), BF16),
            jax.ShapeDtypeStruct((1, width), F32),
        ],
        scratch_shapes=[
            pltpu.VMEM((3, hidden, width), BF16),
            pltpu.SemaphoreType.DMA((groups,)),
            pltpu.VMEM((3, hidden, width), F32),
            pltpu.VMEM((n, tile, width), BF16),
            pltpu.VMEM((n, tile, width), BF16),
            pltpu.VMEM((n, tile, hidden), F32),
            pltpu.VMEM((n, tile, hidden), F32),
        ]
        + (scatter_scratch(count, local, width) + gather_scratch(count, local)) * 2
        + (line_scratch(shards) if extra else []),
        compiler_params=comm_params(1),
        cost_estimate=cost(55),
        name="dense_block",
    )(part, inputs, top, all_top, gain, weights, own)


class SeqSum:
    def __init__(self, shards, part_ref, work_ref, got_ref, full_ref, send, recv):
        self.part, self.work, self.got, self.full = part_ref, work_ref, got_ref, full_ref
        self.send, self.recv = send, recv
        self.seq, self.head = lax.axis_index("seq"), lax.axis_index("head")
        self.bits = [1 << k for k in range((shards - 1).bit_length())]
        self.members, self.rows = part_ref.shape[0], part_ref.shape[1] // 2
        self.half = 128
        self.chunks = 2 * self.members * (part_ref.shape[2] // self.half)
        self.steps = 2 * len(self.bits)
        self.order = [self.members - 1, *range(self.members - 1)]
        self.copies = {}
        self.kept, self.gone = [0], []
        size = self.rows
        for bit in self.bits:
            size //= 2
            mine = self.seq // bit % 2
            self.gone.append(self.kept[-1] + size * (1 - mine))
            self.kept.append(self.kept[-1] + size * mine)

    def view(self, ref, chunk, first, size):
        per = self.chunks // self.members
        first = pl.multiple_of(chunk % 2 * self.rows + first, 8)
        return ref.at[self.order[chunk // per], pl.ds(first, size), pl.ds(chunk % per // 2 * self.half, self.half)]

    def begin(self, chunk, step):
        size = self.rows >> (step + 1)
        src = self.view(self.part if step == 0 else self.work, chunk, self.gone[step], size)
        offset = self.rows - 2 * size
        dst = self.view(self.got, chunk, offset, size)
        c = remote(src, dst, self.send.at[step, chunk], self.recv.at[step, chunk], flip(self.seq, self.bits[step]), self.head)
        c.start()
        self.copies[step, chunk] = c

    def fold(self, chunk, step):
        size = self.rows >> (step + 1)
        self.copies[step, chunk].wait_recv()
        got = self.view(self.got, chunk, self.rows - 2 * size, size)
        kept = self.view(self.part if step == 0 else self.work, chunk, self.kept[step + 1], size)
        total = (kept[...].astype(F32) + got[...].astype(F32)).astype(BF16)
        last = step == len(self.bits) - 1
        self.view(self.full if last else self.work, chunk, self.kept[step + 1], size)[...] = total

    def spread(self, chunk, step):
        back = len(self.bits) - 1 - step
        size = self.rows >> (back + 1)
        ref = self.view(self.full, chunk, self.kept[back + 1], size)
        at = len(self.bits) + step
        c = remote(ref, ref, self.send.at[at, chunk], self.recv.at[at, chunk], flip(self.seq, self.bits[back]), self.head)
        c.start()
        self.copies[at, chunk] = c

    def stage(self, chunk, step):
        n = len(self.bits)
        if step > n:
            self.copies[step - 1, chunk].wait_recv()
        elif step > 0:
            self.fold(chunk, step - 1)
        if step < n:
            self.begin(chunk, step)
        elif step < 2 * n:
            self.spread(chunk, step - n)

    def tick(self, t):
        done = []
        for chunk in range(self.chunks):
            step, odd = divmod(t - chunk, 2)
            if not odd and 0 <= step <= self.steps:
                self.stage(chunk, step)
                if step == self.steps:
                    done.append(chunk)
        return done

    def ticks(self):
        return self.chunks + 2 * self.steps

    def finish(self):
        for c in self.copies.values():
            c.wait_send()


def finish_body(
    shards, gq_ref, gk_ref, gv_ref, tail_ref, rim_ref, grate_ref, all_x_ref, w_ref, beta_ref, gattn_ref, head_ref,
    down_ref, taps_ref, dense_part_ref, out_part_ref, x_ref, mid_ref, resid_ref, gain_ref,
    in_grad_ref, output_ref, total_ref, rows_ref, filter_ref,
    gx_ref, mixer_ref, g_ref, rim_got, rim_send, rim_recv, *scratch,
):
    gx_scratch, down_scratch = scratch[:5], scratch[5:10]
    work_ref, got_ref, full_ref, ms, mr, row_got, row_now, tap_got, tap_now, rs, rr, gain_grad_ref = scratch[10:]
    count, local, width = x_ref.shape
    heads = beta_ref.shape[0]
    members = taps_ref.shape[0]
    rows = gq_ref.shape[1]
    pieces = Pieces(count, local)
    gx = HeadScatter(pieces, gx_ref, False, *gx_scratch)
    down = HeadScatter(pieces, down_ref, True, *down_scratch)
    total = SeqSum(shards, mixer_ref, work_ref, got_ref, full_ref, ms, mr)
    seq, head = pieces.seq, pieces.head

    row_now[0] = jnp.zeros(row_now.shape[1:], F32)
    tap_now[0] = jnp.zeros(tap_now.shape[1:], F32)
    row_now[0, heads : heads + 1, :] = dense_part_ref[...]
    row_now[0, heads + 1 : heads + 2, 0:HEAD_DIM] = out_part_ref[...]
    for k in range(members):
        tap_now[0, 8 * k : 8 * k + CONV, :] = taps_ref[k]
    rounds = [(flip(seq, bit), head) for bit in total.bits] + [(seq, flip(head, 2)), (seq, flip(head, 1))]
    before = lax.rem(seq + shards - 1, shards)
    after = lax.rem(seq + 1, shards)
    greet(rounds + [(after, head)], len(rounds) + 1)
    rim = remote(rim_ref, rim_got, rim_send, rim_recv, before, head)
    rim.start()
    small = {}

    def grates(m):
        lane = lax.broadcasted_iota(jnp.int32, (rows, heads), 1)
        out = jnp.zeros((rows, heads), F32)
        for h in range(heads):
            out = jnp.where(lane == h, grate_ref[m, h], out)
        return out

    def weight_grad(member):
        total = None
        for m in range(count):
            left, right = (gattn_ref[m], head_ref[m]) if member == members else (all_x_ref[m, HALO:, :], g_ref[member, m])
            add = mm(left, right, 0, 0)
            total = add if total is None else total + add
        mixer_ref[member] = total.astype(BF16)

    def join_rims():
        rim.wait_recv()
        for member, ref in enumerate((gq_ref, gk_ref, gv_ref)):
            for m in range(count):
                g_ref[member, m, 0 : rows - 2 * RIM, :] = ref[m, 0 : rows - 2 * RIM, :]
                last = (tail_ref[m, member] + rim_got[m, member]).astype(BF16)
                g_ref[member, m, rows - 2 * RIM :, :] = jnp.concatenate([ref[m, rows - 2 * RIM : rows - RIM, :], last], axis=0)

    def row_grad(m):
        total = mm(grates(m), beta_ref[...])
        for member in range(members):
            total += mm(g_ref[member, m], w_ref[member], 1, 1)
        gx_ref[m] = total.astype(BF16)
        for k in range(m * pieces.per, (m + 1) * pieces.per):
            gx.start(k)

    def beta_grad():
        total = None
        for m in range(count):
            add = mm(grates(m), all_x_ref[m, HALO:, :], 0, 0)
            total = add if total is None else total + add
        row_now[0, 0:heads, :] = total

    def small_start(k):
        small[k] = [
            remote(row_now.at[k], row_got.at[k], rs.at[0, k], rr.at[0, k], *rounds[k]),
            remote(tap_now.at[k], tap_got.at[k], rs.at[1, k], rr.at[1, k], *rounds[k]),
        ]
        for c in small[k]:
            c.start()

    def small_end(k):
        for c in small[k]:
            c.wait_recv()
        row_now[k + 1] = row_now[k] + row_got[k]
        tap_now[k + 1] = tap_now[k] + tap_got[k]

    n = pieces.total
    gain_grad_ref[...] = jnp.zeros_like(gain_grad_ref)

    def gx_end(k):
        m, here = pieces.mine(k)
        grad, gain_part = rms_back(gx.total(k), x_ref[m, here, :].astype(F32), gain_ref[...])
        gain_grad_ref[...] += gain_part
        in_grad_ref[m, here, :] = mid_ref[m, here, :] + grad
        down.forward(k)

    def down_end(k):
        m, here = pieces.mine(k)
        output_ref[m, here, :] = (resid_ref[m, here, :] + down.total(k)).astype(BF16)

    def small_turn(k):
        if k == 0:
            row_now[0, heads + 2 : heads + 3, :] = gain_grad_ref[...]
        else:
            small_end(k - 1)
        if k < len(rounds):
            small_start(k)

    def weight_ready(chunk):
        per = total.chunks // total.members
        if chunk < total.chunks and chunk % per == 0:
            weight_grad(total.order[chunk // per])

    aside = [(1, join_rims), (1, functools.partial(row_grad, 0))]
    aside += [(2, functools.partial(row_grad, m)) for m in range(1, count)]
    aside += [(3, lambda: each(n, gx.forward, down.start)), (4, beta_grad)]
    aside += [(n + 2 + 2 * k, functools.partial(gx_end, k)) for k in range(n)]
    first = 3 * n + 2
    for k in range(max(len(rounds) + 1, n)):
        if k <= len(rounds):
            aside.append((first + 2 * k, functools.partial(small_turn, k)))
        if k < n:
            aside.append((first + 2 * k + 1, functools.partial(down_end, k)))
    weight_ready(0)
    for t in range(total.ticks()):
        for chunk in total.tick(t):
            whole = total.view(full_ref, chunk, 0, total.rows)
            total.view(total_ref, chunk, 0, total.rows)[...] = whole[...].astype(F32)
        while aside and aside[0][0] <= t:
            aside.pop(0)[1]()
        weight_ready(t + 1)
    for _, act in aside:
        act()
    k = len(total.bits)
    rows_ref[0] = row_now[k]
    rows_ref[1] = row_now[len(rounds)]
    for member in range(members):
        filter_ref[member] = tap_now[k, 8 * member : 8 * member + CONV, :]
    for group in small.values():
        for c in group:
            c.wait_send()
    each(pieces.total, gx.sent, down.sent)
    total.finish()
    rim.wait_send()


def finish(
    g3, tail, rim, grate, all_x, mixer_weights, beta_rows, grad_attn, head_out,
    down_part, taps_part, dense_part, out_part, inputs, mid, resid, gain, shards,
):
    count, local, width = inputs.shape
    members, _, head_width = mixer_weights.shape
    rows = g3[0].shape[1]
    bits = (shards - 1).bit_length()
    rounds = bits + 2
    chunks = 2 * members * head_width // 128
    whole = pltpu.VMEM(mixer_weights.shape, BF16)
    return pl.pallas_call(
        functools.partial(finish_body, shards),
        in_specs=vmem_specs(19),
        out_specs=vmem_specs(5),
        out_shape=[
            jax.ShapeDtypeStruct(inputs.shape, F32),
            jax.ShapeDtypeStruct(inputs.shape, BF16),
            jax.ShapeDtypeStruct(mixer_weights.shape, F32),
            jax.ShapeDtypeStruct((2, 8, width), F32),
            jax.ShapeDtypeStruct(taps_part.shape, F32),
        ],
        scratch_shapes=[
            pltpu.VMEM((count, rows, width), BF16),
            whole,
            pltpu.VMEM((3, count, rows, head_width), BF16),
            pltpu.VMEM(rim.shape, F32),
            pltpu.SemaphoreType.DMA,
            pltpu.SemaphoreType.DMA,
        ]
        + scatter_scratch(count, local, width) * 2
        + [
            whole, whole, whole,
            pltpu.SemaphoreType.DMA((2 * bits, chunks)),
            pltpu.SemaphoreType.DMA((2 * bits, chunks)),
            pltpu.VMEM((rounds, 8, width), F32),
            pltpu.VMEM((rounds + 1, 8, width), F32),
            pltpu.VMEM((rounds, 24, head_width), F32),
            pltpu.VMEM((rounds + 1, 24, head_width), F32),
            pltpu.SemaphoreType.DMA((2, rounds)),
            pltpu.SemaphoreType.DMA((2, rounds)),
            pltpu.VMEM((1, width), F32),
        ],
        compiler_params=comm_params(3),
        cost_estimate=cost(75),
        name="finish",
    )(
        *g3, tail, rim, grate, all_x, mixer_weights, beta_rows, grad_attn, head_out,
        down_part, taps_part, dense_part, out_part, inputs, mid, resid, gain,
    )


def regroup(blocks, count):
    if blocks.shape[0] == count:
        return blocks
    _, members, hidden, _ = blocks.shape
    whole = blocks.transpose(1, 2, 0, 3).reshape(members, hidden, count, -1)
    return whole.transpose(2, 0, 1, 3)


def per_device(
    inputs, attn_gain, mixer_weights, beta_weight, filter_weights, out_gain, dense_gain, dense_weights,
    seq_offsets, seq_lengths, out_grad,
):
    count, local_rows, width = inputs.shape
    heads, shards = lax.axis_size("head"), lax.axis_size("seq")
    base = (lax.axis_index("seq") * local_rows * heads).astype(jnp.int32).reshape(1)
    taps = filter_weights
    beta_rows = beta_weight.T
    gain_row = out_gain.reshape(1, HEAD_DIM)
    attn_row = attn_gain.reshape(1, width)
    dense_row = dense_gain.reshape(1, width)
    weights_t = jnp.swapaxes(dense_weights, 1, 2)
    extra = width == 128 * shards
    pq, pk, pv, rates, ps, oloc, phi, psi, score, inv, wr, up, trans, enter, back_x, back_y, x_ext, grad_top = mix_fwd(
        seq_offsets, seq_lengths, base, mixer_weights, beta_rows, taps, inputs, attn_row, out_grad, weights_t, shards, False
    )
    ready = 2 if extra else 3
    dense_full = regroup(lax.all_gather(weights_t[:ready], "seq", axis=0), width // 128)
    state_in = enter.reshape((count, -1) + enter.shape[1:])
    start, mixed, head_out, attn_part = mix_out(state_in, ps, oloc, phi, psi, gain_row, mixer_weights)
    resid_mid, down_part, dense_part, grad_mid, grad_attn, dense_gain_part = dense_block(
        attn_part, inputs, out_grad, grad_top, dense_row, dense_full, weights_t, shards, extra
    )
    dense_mine = lax.psum_scatter(regroup(dense_part, shards), "seq", scatter_dimension=0, tiled=True)
    dense_total = jnp.swapaxes(dense_mine[0], 1, 2).astype(F32)
    gq, gk, gv, tail, rim, grate, filter_part, out_gain_part = mix_grad(
        seq_offsets, seq_lengths, base, (pq, pk, pv), rates, taps, start, score, inv, wr, up,
        grad_attn, mixer_weights, mixed, gain_row, ps, phi, trans, back_x, back_y, shards,
    )
    input_grad, output, mixer_total, rows_total, filter_total = finish(
        (gq, gk, gv), tail, rim, grate, x_ext, mixer_weights, beta_rows, grad_attn, head_out,
        down_part, filter_part, dense_gain_part, out_gain_part, inputs, grad_mid, resid_mid, attn_row, shards,
    )
    local_heads = beta_rows.shape[0]
    beta_total = rows_total[0, :local_heads].T
    dense_gain_total = rows_total[1, local_heads]
    out_gain_total = rows_total[1, local_heads + 1, :HEAD_DIM]
    attn_gain_total = rows_total[1, local_heads + 2]
    return (
        output, input_grad, attn_gain_total, mixer_total, beta_total, filter_total, out_gain_total,
        dense_gain_total, dense_total,
    )


def solution(mesh):
    rows = P(None, ("seq", "head"), None)
    return jax.shard_map(
        per_device,
        mesh=mesh,
        in_specs=(
            rows, P(), P(None, None, "head"), P(None, "head"), P(None, None, "head"), P(), P(),
            P(None, "seq", "head"), P(), P(), rows,
        ),
        out_specs=(
            rows, rows, P(), P(None, None, "head"), P(None, "head"), P(None, None, "head"), P(), P(),
            P(None, "seq", "head"),
        ),
        check_vma=False,
    )
```

```python
import functools

import jax
import jax.numpy as jnp
from jax import lax
from jax.experimental import pallas as pl
from jax.experimental.pallas import tpu as pltpu
from jax.sharding import PartitionSpec as P

HEAD_DIM = 128
CONV = 4
CHUNK = 128
HALO = 16
RIM = 8
PIECE = 64
EPS = 1e-06
F32 = jnp.float32
BF16 = jnp.bfloat16
VMEM_LIMIT = 56 * 1024 * 1024


def mm(a, b, ca=1, cb=0):
    return lax.dot_general(
        a.astype(BF16), b.astype(BF16), (((ca,), (cb,)), ((), ())), preferred_element_type=F32
    )


def split(a):
    high = a.astype(BF16)
    return high, (a - high.astype(F32)).astype(BF16)


def mm3(a, b, ca=1, cb=0):
    ah, al = split(a)
    bh, bl = split(b)
    return mm(ah, bh, ca, cb) + (mm(ah, bl, ca, cb) + mm(al, bh, ca, cb))


def sigmoid(v):
    return 1.0 / (1.0 + jnp.exp(-v))


def row_info(off_ref, len_ref, m, base, rows):
    t = base + lax.broadcasted_iota(jnp.int32, (rows, 1), 0)
    start = jnp.zeros_like(t)
    length = jnp.zeros_like(t)
    for i in range(off_ref.shape[1]):
        inside = t >= off_ref[m, i]
        start = jnp.where(inside, off_ref[m, i], start)
        length = jnp.where(inside, len_ref[m, i], length)
    rel = t - start
    return rel, (rel < length).astype(F32)


def chunk_masks(rel):
    n = rel.shape[0]
    i = lax.broadcasted_iota(jnp.int32, (n, n), 0)
    j = lax.broadcasted_iota(jnp.int32, (n, n), 1)
    same = rel >= i - j
    strict = jnp.logical_and(same, i > j)
    incl = jnp.logical_and(same, i >= j)
    col = lax.broadcasted_iota(jnp.int32, (n, 1), 0)
    sees = (rel > col).astype(F32)
    last = rel[n - 1 : n, :]
    stays = ((n - 1 - col) <= last).astype(F32)
    keep = (last > n - 1).astype(F32)
    return strict, incl, sees, stays, keep


def unit_lower_inverse(a_list):
    n = a_list[0].shape[0]
    i = lax.broadcasted_iota(jnp.int32, (n, n), 0)
    j = lax.broadcasted_iota(jnp.int32, (n, n), 1)
    eye = (i == j).astype(F32)
    size = 1
    inv_list = [eye for _ in a_list]
    while size < n:
        pair = jnp.logical_and(i // size == j // size + 1, (i // size) % 2 == 1)
        below = [jnp.where(pair, a, 0.0) for a in a_list]
        if size == 1:
            inv_list = [eye - b for b in below]
        else:
            half = [mm3(b, inv) for b, inv in zip(below, inv_list)]
            inv_list = [inv - mm3(inv, h) for inv, h in zip(inv_list, half)]
        size *= 2
    return inv_list


def lagged(ext, lag, rows):
    moved = pltpu.roll(ext, lag, 0) if lag else ext
    return moved[HALO : HALO + rows]


def lag_masks(rel):
    return [None] + [(rel >= lag).astype(F32) for lag in range(1, CONV)]


def filtered(ext, taps, masks, rows):
    total = None
    for lag in range(CONV):
        term = taps[lag : lag + 1, :] * lagged(ext, lag, rows)
        if masks[lag] is not None:
            term = term * masks[lag]
        total = term if total is None else total + term
    return total


MESH = pl.DeviceIdType.MESH


def flip(index, bit):
    return index + bit * (1 - 2 * (index // bit % 2))


def remote(src, dst, send, recv, seq, head):
    return pltpu.make_async_remote_copy(
        src_ref=src, dst_ref=dst, send_sem=send, recv_sem=recv, device_id=(seq, head), device_id_type=MESH
    )


def greet(devices, expected):
    barrier = pltpu.get_barrier_semaphore()
    for seq, head in devices:
        pl.semaphore_signal(barrier, inc=1, device_id=(seq, head), device_id_type=MESH)
    pl.semaphore_wait(barrier, expected)


class Pieces:
    def __init__(self, count, local):
        self.local = local
        self.per = local // PIECE
        self.total = count * self.per
        self.seq, self.head = lax.axis_index("seq"), lax.axis_index("head")
        self.far, self.near = flip(self.head, 2), flip(self.head, 1)

    def mine(self, k):
        return k // self.per, pl.ds(pl.multiple_of(k % self.per * PIECE, PIECE), PIECE)

    def block(self, ref, k, owner, tiled, first=0):
        if tiled:
            return ref.at[k, pl.ds(pl.multiple_of(owner * PIECE, PIECE), PIECE), :]
        start = first + owner * self.local + k % self.per * PIECE
        return ref.at[k // self.per, pl.ds(pl.multiple_of(start, 16), PIECE), :]


class HeadGather:
    def __init__(self, pieces, out_ref, tiled, first, send, recv):
        self.pieces, self.out, self.tiled, self.first = pieces, out_ref, tiled, first
        self.send, self.recv = send, recv

    def place(self, k, owner):
        return self.pieces.block(self.out, k, owner, self.tiled, self.first)

    def copy(self, kind, k):
        p = self.pieces
        owner = p.far if kind == 2 else p.head
        target = p.near if kind else p.far
        ref = self.place(k, owner)
        return remote(ref, ref, self.send.at[kind, k], self.recv.at[kind, k], p.seq, target)

    def own(self, k):
        self.copy(0, k).start()
        self.copy(1, k).start()

    def forward(self, k):
        self.copy(0, k).wait_recv()
        self.copy(2, k).start()

    def arrived(self, k):
        self.copy(1, k).wait_recv()
        self.copy(2, k).wait_recv()

    def sent(self, k):
        for kind in range(3):
            self.copy(kind, k).wait_send()


class HeadScatter:
    def __init__(self, pieces, part_ref, tiled, near_ref, stage_ref, far_ref, send, recv):
        self.pieces, self.part, self.tiled = pieces, part_ref, tiled
        self.nearby, self.stage, self.faraway = near_ref, stage_ref, far_ref
        self.send, self.recv = send, recv

    def block(self, k, owner):
        return self.pieces.block(self.part, k, owner, self.tiled)

    def copy(self, kind, k):
        p = self.pieces
        if kind == 2:
            return remote(
                self.stage.at[k], self.faraway.at[k], self.send.at[2, k], self.recv.at[2, k], p.seq, p.far
            )
        owner = p.near if kind else flip(p.near, 2)
        return remote(
            self.block(k, owner), self.nearby.at[kind, k], self.send.at[kind, k], self.recv.at[kind, k], p.seq, p.near
        )

    def start(self, k):
        self.copy(0, k).start()
        self.copy(1, k).start()

    def forward(self, k):
        self.copy(0, k).wait_recv()
        total = self.block(k, self.pieces.far)[...].astype(F32) + self.nearby[0, k].astype(F32)
        self.stage[k] = total.astype(BF16)
        self.copy(2, k).start()

    def total(self, k):
        self.copy(1, k).wait_recv()
        self.copy(2, k).wait_recv()
        near = self.block(k, self.pieces.head)[...].astype(F32) + self.nearby[1, k].astype(F32)
        return near + self.faraway[k].astype(F32)

    def sent(self, k):
        for kind in range(3):
            self.copy(kind, k).wait_send()


def each(count, *steps):
    for step in steps:
        pl.loop(0, count)(step)


def scatter_scratch(count, local, width):
    n = count * local // PIECE
    return [
        pltpu.VMEM((2, n, PIECE, width), BF16),
        pltpu.VMEM((n, PIECE, width), BF16),
        pltpu.VMEM((n, PIECE, width), BF16),
        pltpu.SemaphoreType.DMA((3, n)),
        pltpu.SemaphoreType.DMA((3, n)),
    ]


def gather_scratch(count, local):
    n = count * local // PIECE
    return [pltpu.SemaphoreType.DMA((3, n)), pltpu.SemaphoreType.DMA((3, n))]


class Compose:
    def __init__(self, shards, heads, trans_ref, state_ref, out_ref, back_x_ref, back_y_ref, scratch):
        self.shards, self.heads = shards, heads
        self.trans, self.state, self.out, self.back_x, self.back_y = trans_ref, state_ref, out_ref, back_x_ref, back_y_ref
        self.stage, self.got, self.got_back, self.tx, self.s, self.send, self.recv = scratch
        self.seq, self.head = lax.axis_index("seq"), lax.axis_index("head")
        self.steps = [1 << k for k in range((shards - 1).bit_length())]

    def peer(self, distance):
        return lax.rem(self.seq + self.shards + distance, self.shards)

    def peers(self):
        return [(self.peer(-d), self.head) for d in self.steps] + [(self.peer(d), self.head) for d in self.steps[:-1]]

    def copies(self, m, k):
        d = self.steps[k]
        here = pl.ds(m * self.heads, self.heads)
        final = k == len(self.steps) - 1
        out = []
        for part in range(1 if final else 3):
            if part == 2:
                src = self.trans if k == 0 else self.back_y.at[k - 1]
                dst = self.got_back.at[k]
            else:
                src = (self.state, self.trans)[part] if k == 0 else self.stage.at[k - 1, part]
                dst = self.got.at[k, part]
            to = self.peer(-d if part == 2 else d)
            sems = self.send.at[part, k, m], self.recv.at[part, k, m]
            out.append(remote(src.at[here], dst.at[here], *sems, to, self.head))
        return out

    def begin(self, m, k):
        for c in self.copies(m, k):
            c.start()

    def turn(self, m, k):
        n = len(self.steps)
        if k == 0:
            self.begin(m, 0)
            return
        for c in self.copies(m, k - 1):
            c.wait_recv()
        k -= 1
        final = k == n - 1
        here = (self.seq >= self.steps[k]).astype(F32)
        here_back = (self.seq + self.steps[k] < self.shards).astype(F32)
        groups = range(m * self.heads, (m + 1) * self.heads)
        pairs = {}
        for g in groups:
            state = self.got[k, 0, g].astype(F32) * here
            if final:
                self.out[g] = state if k == 0 else self.out[g] + mm(self.tx[g], state)
                continue
            pairs[g] = jnp.concatenate([self.got[k, 1, g].astype(F32) * here, state], axis=1).astype(BF16)
            old_t = self.trans[g] if k == 0 else self.stage[k - 1, 1, g]
            old_s = self.state[g].astype(F32) if k == 0 else self.s[g]
            both = mm(old_t, pairs[g])
            new_s = old_s + both[:, HEAD_DIM:]
            self.s[g] = new_s
            self.stage[k, 0, g] = new_s.astype(BF16)
            self.stage[k, 1, g] = both[:, :HEAD_DIM].astype(BF16)
            later = (self.got_back[k, g].astype(F32) * here_back).astype(BF16)
            self.back_x[k, g] = later if k == 0 else mm(later, self.back_x[k - 1, g]).astype(BF16)
            self.back_y[k, g] = mm(later, self.trans[g] if k == 0 else self.back_y[k - 1, g]).astype(BF16)
        if final:
            return
        self.begin(m, k + 1)
        for g in groups:
            if k == 0:
                self.out[g] = pairs[g][:, HEAD_DIM:].astype(F32)
                self.tx[g] = pairs[g][:, :HEAD_DIM]
            else:
                both = mm(self.tx[g], pairs[g])
                self.out[g] += both[:, HEAD_DIM:]
                self.tx[g] = both[:, :HEAD_DIM].astype(BF16)

    def sent(self, count):
        for m in range(count):
            for k in range(len(self.steps)):
                for c in self.copies(m, k):
                    c.wait_send()

    def script(self, m):
        return [functools.partial(self.turn, m, k) for k in range(len(self.steps) + 1)]


def compose_scratch(shards, count, flat):
    rounds = (shards - 1).bit_length()
    more = max(rounds - 1, 1)
    return [
        pltpu.VMEM((more, 2) + flat, BF16),
        pltpu.VMEM((rounds, 2) + flat, BF16),
        pltpu.VMEM((more,) + flat, BF16),
        pltpu.VMEM(flat, BF16),
        pltpu.VMEM(flat, F32),
        pltpu.SemaphoreType.DMA((3, rounds, count)),
        pltpu.SemaphoreType.DMA((3, rounds, count)),
    ]


class ComposeBack:
    def __init__(self, shards, heads, trans_ref, state_ref, back_x_ref, back_y_ref, out_ref, scratch):
        self.shards, self.heads = shards, heads
        self.trans, self.state, self.back_x, self.back_y, self.out = trans_ref, state_ref, back_x_ref, back_y_ref, out_ref
        self.stage, self.got, self.s, self.send, self.recv = scratch
        self.seq, self.head = lax.axis_index("seq"), lax.axis_index("head")
        self.steps = [1 << k for k in range((shards - 1).bit_length())]

    def peer(self, distance):
        return lax.rem(self.seq + self.shards + distance, self.shards)

    def peers(self):
        return [(self.peer(d), self.head) for d in self.steps]

    def copy(self, m, k):
        here = pl.ds(m * self.heads, self.heads)
        src = self.state if k == 0 else self.stage.at[k - 1]
        dst = self.got.at[k]
        return remote(
            src.at[here], dst.at[here], self.send.at[k, m], self.recv.at[k, m], self.peer(-self.steps[k]), self.head
        )

    def begin(self, m, k):
        self.copy(m, k).start()

    def turn(self, m, k):
        n = len(self.steps)
        if k == 0:
            self.begin(m, 0)
            return
        k -= 1
        self.copy(m, k).wait_recv()
        here = (self.seq + self.steps[k] < self.shards).astype(F32)
        groups = range(m * self.heads, (m + 1) * self.heads)
        states = [(self.got[k, g].astype(F32) * here).astype(BF16) for g in groups]
        if k + 1 < n:
            for g, state in zip(groups, states):
                trans = self.trans[g] if k == 0 else self.back_y[k - 1, g]
                new_s = (self.state[g].astype(F32) if k == 0 else self.s[g]) + mm(trans, state, 0, 0)
                self.s[g] = new_s
                self.stage[k, g] = new_s.astype(BF16)
            self.begin(m, k + 1)
        for g, state in zip(groups, states):
            if k == 0:
                self.out[g] = state.astype(F32)
            else:
                self.out[g] += mm(self.back_x[k - 1, g], state, 0, 0)

    def sent(self, count):
        for m in range(count):
            for k in range(len(self.steps)):
                self.copy(m, k).wait_send()


def compose_back_scratch(shards, count, flat):
    rounds = (shards - 1).bit_length()
    return [
        pltpu.VMEM((max(rounds - 1, 1),) + flat, BF16),
        pltpu.VMEM((rounds,) + flat, BF16),
        pltpu.VMEM(flat, F32),
        pltpu.SemaphoreType.DMA((rounds, count)),
        pltpu.SemaphoreType.DMA((rounds, count)),
    ]


class LineGather:
    def __init__(self, shards, src_ref, place, send, recv, local):
        self.shards, self.src, self.place = shards, src_ref, place
        self.send, self.recv, self.local = send, recv, local
        self.seq, self.head = lax.axis_index("seq"), lax.axis_index("head")
        self.neighbour = flip(self.seq, 1)
        self.half = shards // 2

    def on_line(self, distance, base=None):
        base = self.seq if base is None else base
        return lax.rem(base + self.shards + 2 * distance, self.shards)

    def peers(self):
        return [(self.on_line(-d), self.head) for d in range(1, self.half)] + [(self.neighbour, self.head)]

    def along(self, member, d, block):
        sems = self.send.at[member, d], self.recv.at[member, d]
        return remote(self.src.at[member], self.place(member, block), *sems, self.on_line(d), self.head)

    def across(self, member, d, block):
        dst = self.place(member, block)
        sems = self.send.at[member, self.half + d], self.recv.at[member, self.half + d]
        return remote(dst if d else self.src.at[member], dst, *sems, self.neighbour, self.head)

    def mine(self, member):
        return pltpu.make_async_copy(self.src.at[member], self.place(member, self.seq), self.local.at[member])

    def start(self, member):
        self.mine(member).start()
        for d in range(1, self.half):
            self.along(member, d, self.seq).start()
        self.across(member, 0, self.seq).start()

    def forward(self, member):
        for d in range(1, self.half):
            block = self.on_line(-d)
            self.along(member, d, block).wait_recv()
            self.across(member, d, block).start()

    def arrived(self, member):
        self.mine(member).wait()
        for d in range(self.half):
            self.across(member, d, self.on_line(-d, self.neighbour)).wait_recv()

    def sent(self, member):
        for d in range(1, self.half):
            self.along(member, d, self.seq).wait_send()
        for d in range(self.half):
            self.across(member, d, self.on_line(-d)).wait_send()

    def finish(self, member):
        self.arrived(member)
        self.sent(member)


def mix_fwd_body(
    shards, count, heads, token_heads, extra, off_ref, len_ref, base_ref, w_ref, beta_ref, taps_ref, in_ref, gain_ref, top_ref, own_ref,
    pq_ref, pk_ref, pv_ref, rate_ref, ps_ref, oloc_ref, phi_ref, psi_ref, m_ref, inv_ref, wr_ref, up_ref,
    trans_ref, enter_ref, back_x_ref, back_y_ref, all_x_out, all_top_out, *refs,
):
    full_ref, refs = (refs[0], refs[1:]) if extra else (None, refs)
    all_x_ref, all_top_ref, out_sems, state_ref, x_send, x_recv, gather_send, gather_recv, halo_send, halo_recv, *refs = refs
    scratch, sems = refs[:7], refs[7:]
    mb = pl.program_id(0)
    head = pl.program_id(1)
    grid_step = mb * heads + head
    steps = count * heads
    local = in_ref.shape[1]
    pieces = Pieces(count, local)
    gather_x = HeadGather(pieces, all_x_ref, False, HALO, x_send, x_recv)
    gather = HeadGather(pieces, all_top_ref, True, 0, gather_send, gather_recv)
    rounds = Compose(shards, heads, trans_ref, state_ref, enter_ref, back_x_ref, back_y_ref, scratch)
    line = LineGather(shards, own_ref, lambda member, q: full_ref.at[q, member], *sems) if extra else None
    last = pieces.head == token_heads - 1

    def halo(target):
        src = all_x_ref.at[:, pl.ds(token_heads * local, HALO), :]
        dst = all_x_ref.at[:, pl.ds(0, HALO), :]
        return remote(src, dst, halo_send.at[target], halo_recv, lax.rem(pieces.seq + 1, shards), target)

    def some(act, first, stop):
        pl.loop(first, stop)(act)

    def write_out(i):
        src, dst = ((all_x_ref, all_x_out), (all_top_ref, all_top_out))[i]
        return pltpu.make_async_copy(src, dst, out_sems.at[i])

    @pl.when(grid_step == 0)
    def _():
        for k in range(pieces.total):
            m, here = pieces.mine(k)
            x = in_ref[m, here, :].astype(F32)
            gather_x.place(k, pieces.head)[...] = rms(x, gain_ref[...]).astype(BF16)
            gather.place(k, pieces.head)[...] = top_ref[m, here, :]
        before = lax.rem(pieces.seq + shards - 1, shards)
        peers = rounds.peers() + (line.peers() if extra else []) + [(pieces.seq, pieces.far), (pieces.seq, pieces.near)]
        greet(peers + [(before, token_heads - 1)], len(peers) + token_heads * last.astype(jnp.int32))
        some(gather_x.own, 0, pieces.per)

        @pl.when(last)
        def _():
            for target in range(token_heads):
                halo(target).start()

        some(gather_x.own, pieces.per, pieces.total)
        if extra:
            for member in range(2):
                line.start(member)
        some(gather_x.forward, 0, pieces.per)
        some(gather_x.arrived, 0, pieces.per)
        halo(0).wait_recv()

    @pl.when(grid_step == min(1, steps - 1))
    def _():
        some(gather_x.forward, pieces.per, pieces.total)
        each(pieces.total, gather.own)

    @pl.when(grid_step == min(heads, steps - 1))
    def _():
        some(gather_x.arrived, pieces.per, pieces.total)
        write_out(0).start()

    if extra:
        for at, member in ((1, 0), (steps - 1, 1)):

            @pl.when(grid_step == at)
            def _(member=member):
                line.forward(member)

    left = []
    plan = {}
    for m in range(count):
        turns = rounds.script(m)
        if m + 1 < count:
            places = [((m + 1) * heads - 1, 1), ((m + 1) * heads, 1)]
            for place in places:
                if turns:
                    plan.setdefault(place, []).append(turns.pop(0))
        left.append(turns)

    def advance(point):
        for (at, where), turns in plan.items():
            if where == point:

                @pl.when(grid_step == at)
                def _(turns=turns):
                    for turn in turns:
                        turn()

    rows = all_x_ref.shape[1] - HALO
    rel, valid = row_info(off_ref, len_ref, mb, base_ref[0], rows)
    x = all_x_ref[mb]
    masks = lag_masks(rel)
    acts = []
    for member, out in enumerate((pq_ref, pk_ref, pv_ref)):
        proj = mm(x, w_ref[member]).astype(BF16)
        out[0] = proj
        filt = filtered(proj.astype(F32), taps_ref[member].astype(F32), masks, rows)
        acts.append(filt * sigmoid(filt))
    query, key, value = acts
    query = query * lax.rsqrt(jnp.sum(query * query, axis=-1, keepdims=True) + EPS)
    key = key * lax.rsqrt(jnp.sum(key * key, axis=-1, keepdims=True) + EPS)
    raw_all = mm(x, beta_ref[...], 1, 1)[HALO:]
    lane = lax.broadcasted_iota(jnp.int32, raw_all.shape, 1)
    raw = jnp.sum(jnp.where(lane == head, raw_all, 0.0), axis=-1, keepdims=True)
    rate_ref[0, 0] = raw
    rate = sigmoid(raw) * valid
    spans = [slice(c * CHUNK, (c + 1) * CHUNK) for c in range(rows // CHUNK)]
    all_masks = [chunk_masks(rel[s]) for s in spans]
    systems, scores = [], []
    for s, (strict, incl, _, _, _) in zip(spans, all_masks):
        both = mm(jnp.concatenate([query[s], key[s]], axis=0), key[s], 1, 1)
        scores.append(jnp.where(incl, both[:CHUNK], 0.0))
        systems.append(jnp.where(strict, rate[s] * both[CHUNK:], 0.0))
    advance(0)
    inverses = unit_lower_inverse(systems)
    i = lax.broadcasted_iota(jnp.int32, (HEAD_DIM, HEAD_DIM), 0)
    j = lax.broadcasted_iota(jnp.int32, (HEAD_DIM, HEAD_DIM), 1)
    eye = (i == j).astype(F32)
    phis, psis, ps, olocs = [], [], [], []
    for s, masks_c, inv, score in zip(spans, all_masks, inverses, scores):
        _, _, sees, stays, keep = masks_c
        right = rate[s] * jnp.concatenate([sees * key[s], value[s]], axis=1)
        solved = mm(inv, right)
        write, update = solved[:, :HEAD_DIM], solved[:, HEAD_DIM:]
        moved = mm(stays * key[s], solved, 0, 0)
        phi = keep * eye - moved[:, :HEAD_DIM]
        psi = moved[:, HEAD_DIM:]
        scored = mm(score, solved)
        p = sees * query[s] - scored[:, :HEAD_DIM]
        m_ref[0, 0, s] = score.astype(BF16)
        inv_ref[0, 0, s] = inv.astype(BF16)
        wr_ref[0, 0, s] = write.astype(BF16)
        up_ref[0, 0, s] = update
        ps_ref[0, 0, s] = p.astype(BF16)
        oloc_ref[0, 0, s] = scored[:, HEAD_DIM:]
        phi_ref[0, 0, s] = phi
        psi_ref[0, 0, s] = psi
        phis.append(phi)
        psis.append(psi)
    trans, state = phis[0], psis[0]
    for phi, psi in zip(phis[1:], psis[1:]):
        both = mm3(phi, jnp.concatenate([trans, state], axis=1))
        trans = both[:, :HEAD_DIM]
        state = both[:, HEAD_DIM:] + psi
    trans_ref[grid_step] = trans.astype(BF16)
    state_ref[grid_step] = state.astype(BF16)
    advance(1)

    @pl.when(grid_step == count * heads - 1)
    def _():
        each(pieces.total, gather.forward)
        while any(left):
            for turns in left:
                if turns:
                    turns.pop(0)()
        rounds.sent(count)
        each(pieces.total, gather.arrived)
        write_out(1).start()
        each(pieces.total, gather.sent, gather_x.sent)
        write_out(0).wait()
        write_out(1).wait()

        @pl.when(last)
        def _():
            for target in range(token_heads):
                halo(target).wait_send()

        if extra:
            for member in range(2):
                line.finish(member)


def cost(us):
    return pl.CostEstimate(flops=0, bytes_accessed=int(us * 3.0e6), transcendentals=0)


def any_spec():
    return pl.BlockSpec(memory_space=pl.ANY)


def smem_spec():
    return pl.BlockSpec(memory_space=pltpu.SMEM)


def params(count, collective=None):
    return pltpu.CompilerParams(
        dimension_semantics=("arbitrary",) * count,
        vmem_limit_bytes=VMEM_LIMIT,
        collective_id=collective,
        has_side_effects=collective is not None,
    )


def line_scratch(shards):
    return [pltpu.SemaphoreType.DMA((3, shards))] * 2 + [pltpu.SemaphoreType.DMA((3,))]


def mix_fwd(offsets, lengths, base, mixer_weights, beta_weight, taps, inputs, gain, top, dense_weights, shards, extra):
    count, local, width = inputs.shape
    token_heads = lax.axis_size("head")
    rows = local * token_heads
    ext_rows = rows + HALO
    heads = beta_weight.shape[0]
    per_head = pl.BlockSpec((1, 1, rows, HEAD_DIM), lambda m, h: (m, h, 0, 0))
    proj_spec = pl.BlockSpec((1, ext_rows, HEAD_DIM), lambda m, h: (m, 0, h))
    proj_shape = jax.ShapeDtypeStruct((count, ext_rows, heads * HEAD_DIM), BF16)

    def big(kind):
        return jax.ShapeDtypeStruct((count, heads, rows, HEAD_DIM), kind)

    flat = (count * heads, HEAD_DIM, HEAD_DIM)
    more = max((shards - 1).bit_length() - 1, 1)
    all_x = (count, ext_rows, width)
    all_top = (count * local // PIECE, PIECE * token_heads, width)
    shapes = [
        jax.ShapeDtypeStruct(flat, BF16),
        jax.ShapeDtypeStruct(flat, F32),
        jax.ShapeDtypeStruct((more,) + flat, BF16),
        jax.ShapeDtypeStruct((more,) + flat, BF16),
        jax.ShapeDtypeStruct(all_x, BF16),
        jax.ShapeDtypeStruct(all_top, BF16),
    ]
    more_shapes = [jax.ShapeDtypeStruct((shards, 2) + dense_weights.shape[1:], BF16)] if extra else []
    shapes += more_shapes
    line_sems = line_scratch(shards) if extra else []
    return pl.pallas_call(
        functools.partial(mix_fwd_body, shards, count, heads, token_heads, extra),
        grid=(count, heads),
        in_specs=[
            smem_spec(), smem_spec(), smem_spec(),
            pl.BlockSpec((3, width, HEAD_DIM), lambda m, h: (0, 0, h)),
            pl.BlockSpec(beta_weight.shape, lambda m, h: (0, 0)),
            pl.BlockSpec((3, CONV, HEAD_DIM), lambda m, h: (0, 0, h)),
        ]
        + vmem_specs(3)
        + [any_spec()],
        out_specs=[proj_spec] * 3
        + [pl.BlockSpec((1, 1, rows, 1), lambda m, h: (m, h, 0, 0))]
        + [per_head] * 8
        + vmem_specs(4)
        + [any_spec()] * (len(shapes) - 4),
        out_shape=[proj_shape] * 3
        + [jax.ShapeDtypeStruct((count, heads, rows, 1), F32)]
        + [big(BF16), big(F32), big(F32), big(F32), big(BF16), big(BF16), big(BF16), big(F32)]
        + shapes,
        scratch_shapes=[
            pltpu.VMEM(all_x, BF16), pltpu.VMEM(all_top, BF16), pltpu.SemaphoreType.DMA((2,)), pltpu.VMEM(flat, BF16)
        ]
        + gather_scratch(count, local) * 2
        + [pltpu.SemaphoreType.DMA((token_heads,)), pltpu.SemaphoreType.DMA]
        + compose_scratch(shards, count, flat)
        + line_sems,
        compiler_params=params(2, 4),
        cost_estimate=cost(45),
        name="mix_fwd",
    )(offsets, lengths, base, mixer_weights, beta_weight, taps, inputs, gain, top, dense_weights)


def mix_out_body(state_ref, ps_ref, oloc_ref, phi_ref, psi_ref, gain_ref, w_ref, start_ref, mixed_ref, head_ref, part_ref):
    heads = ps_ref.shape[1]
    rows = ps_ref.shape[2]
    gain = gain_ref[...]
    states = [state_ref[0, h] for h in range(heads)]
    for c in range(rows // CHUNK):
        s = slice(c * CHUNK, (c + 1) * CHUNK)
        for h in range(heads):
            state = states[h]
            start_ref[0, h, s] = state.astype(BF16)
            mixed = oloc_ref[0, h, s] + mm(ps_ref[0, h, s], state)
            mixed_ref[0, h, s] = mixed
            normed = mixed * lax.rsqrt(jnp.mean(mixed * mixed, axis=-1, keepdims=True) + EPS) * gain
            head_ref[0, s, h * HEAD_DIM : (h + 1) * HEAD_DIM] = normed.astype(BF16)
            states[h] = mm3(phi_ref[0, h, s], state) + psi_ref[0, h, s]
    part_ref[0] = mm(head_ref[0], w_ref[0], 1, 1).astype(BF16)


def mix_out(state_in, ps, oloc, phi, psi, out_gain, mixer_weights):
    count, heads, rows, _ = ps.shape
    width = mixer_weights.shape[1]
    head_width = mixer_weights.shape[2]
    per_mb = pl.BlockSpec((1, heads, rows, HEAD_DIM), lambda m: (m, 0, 0, 0))
    return pl.pallas_call(
        mix_out_body,
        grid=(count,),
        in_specs=[
            pl.BlockSpec((1, heads, HEAD_DIM, HEAD_DIM), lambda m: (m, 0, 0, 0)),
            per_mb, per_mb, per_mb, per_mb,
            pl.BlockSpec((1, HEAD_DIM), lambda m: (0, 0)),
            pl.BlockSpec((1, width, head_width), lambda m: (3, 0, 0)),
        ],
        out_specs=[
            per_mb, per_mb,
            pl.BlockSpec((1, rows, head_width), lambda m: (m, 0, 0)),
            pl.BlockSpec((1, rows, width), lambda m: (m, 0, 0)),
        ],
        out_shape=[
            jax.ShapeDtypeStruct(ps.shape, BF16),
            jax.ShapeDtypeStruct(ps.shape, F32),
            jax.ShapeDtypeStruct((count, rows, head_width), BF16),
            jax.ShapeDtypeStruct((count, rows, width), BF16),
        ],
        compiler_params=params(1),
        cost_estimate=cost(5),
        name="mix_out",
    )(state_in, ps, oloc, phi, psi, out_gain, mixer_weights)


def mix_grad_body(
    shards, count, heads,
    off_ref, len_ref, base_ref, pq_ref, pk_ref, pv_ref, rate_ref, taps_ref, start_ref,
    m_ref, inv_ref, wr_ref, up_ref,
    grad_ref, wo_ref, mixed_ref, gain_ref, all_ps_ref, all_phi_ref, trans_ref, back_x_ref, back_y_ref,
    gq_ref, gk_ref, gv_ref, tail_ref, rim_ref, grate_ref, gtaps_ref, gain_grad_ref,
    dstate_ref, dend_ref, all_dout_ref, *scratch,
):
    mb = pl.program_id(0)
    head = pl.program_id(1)
    grid_step = mb * heads + head
    rounds = ComposeBack(shards, heads, trans_ref, dstate_ref, back_x_ref, back_y_ref, dend_ref, scratch)
    n = len(rounds.steps)
    late = [1] if count > 1 else []

    def mix_back(m):
        gain = gain_ref[...]
        grad_head = mm(grad_ref[m], wo_ref[0])
        states = [None] * heads
        for h in range(heads):
            e = grad_head[:, h * HEAD_DIM : (h + 1) * HEAD_DIM]
            v = mixed_ref[m, h]
            r = lax.rsqrt(jnp.mean(v * v, axis=-1, keepdims=True) + EPS)
            weighted = e * gain
            dout = r * weighted - v * (r * r * r * jnp.mean(weighted * v, axis=-1, keepdims=True))
            gain_grad_ref[...] += jnp.sum(e * v * r, axis=0, keepdims=True)
            all_dout_ref[m * heads + h] = dout.astype(BF16)
        for c in reversed(range(all_ps_ref.shape[2] // CHUNK)):
            s = slice(c * CHUNK, (c + 1) * CHUNK)
            for h in range(heads):
                new = mm(all_ps_ref[m, h, s], all_dout_ref[m * heads + h, s], 0, 0)
                if states[h] is not None:
                    new += mm3(all_phi_ref[m, h, s], states[h], 0, 0)
                states[h] = new
        for h in range(heads):
            dstate_ref[m * heads + h] = states[h].astype(BF16)

    @pl.when(grid_step == 0)
    def _():
        gain_grad_ref[...] = jnp.zeros_like(gain_grad_ref)
        gtaps_ref[...] = jnp.zeros_like(gtaps_ref)
        greet(rounds.peers(), n)
        for m in range(count):
            mix_back(m)
            rounds.turn(m, 0)
        for k in range(1, n + 1):
            for m in range(count):
                if m not in late:
                    rounds.turn(m, k)
            for m in late:
                if k > 1:
                    rounds.turn(m, k - 1)

    rows = rate_ref.shape[2]
    rel, valid = row_info(off_ref, len_ref, mb, base_ref[0], rows)
    masks = lag_masks(rel)
    projs, filts, sigs, acts = [], [], [], []
    for member, ref in enumerate((pq_ref, pk_ref, pv_ref)):
        proj = ref[0].astype(F32)
        filt = filtered(proj, taps_ref[member].astype(F32), masks, rows)
        sg = sigmoid(filt)
        projs.append(proj)
        filts.append(filt)
        sigs.append(sg)
        acts.append(filt * sg)
    rq = lax.rsqrt(jnp.sum(acts[0] * acts[0], axis=-1, keepdims=True) + EPS)
    rk = lax.rsqrt(jnp.sum(acts[1] * acts[1], axis=-1, keepdims=True) + EPS)
    query = acts[0] * rq
    key = acts[1] * rk
    value = acts[2]
    sig_rate = sigmoid(rate_ref[0, 0])
    rate = sig_rate * valid
    spans = [slice(c * CHUNK, (c + 1) * CHUNK) for c in range(rows // CHUNK)]
    dstates = [None] * len(spans)
    dstate = dend_ref[grid_step]
    for c in reversed(range(len(spans))):
        s = spans[c]
        dstates[c] = dstate
        if c:
            dstate = mm3(all_phi_ref[mb, head, s], dstate, 0, 0) + mm(all_ps_ref[mb, head, s], all_dout_ref[grid_step, s], 0, 0)
    dqs, dks, dvs, drates = [], [], [], []
    for c, s in enumerate(spans):
        strict, incl, sees, stays, _ = chunk_masks(rel[s])
        q, k, v, b = query[s], key[s], value[s], rate[s]
        dout = all_dout_ref[grid_step, s]
        start = start_ref[0, 0, s]
        fresh = up_ref[0, 0, s] - mm(wr_ref[0, 0, s], start)
        dfresh = mm(m_ref[0, 0, s], dout, 0, 0) + mm(stays * k, dstates[c])
        e = mm(inv_ref[0, 0, s], dfresh, 0, 0)
        left = jnp.concatenate([dout, e.astype(BF16)], axis=0)
        right = jnp.concatenate([fresh.astype(BF16), start], axis=0)
        outer = mm(left, right, 1, 1)
        dscore = jnp.where(incl, outer[:CHUNK, :CHUNK], 0.0)
        dsystem = jnp.where(strict, -outer[CHUNK:, :CHUNK], 0.0)
        grads = jnp.concatenate([dscore, dsystem], axis=0).astype(BF16)
        byk = mm(grads, k)
        z = byk[CHUNK:] - sees * outer[CHUNK:, CHUNK:]
        dqs.append(sees * outer[:CHUNK, CHUNK:] + byk[:CHUNK])
        dk = mm(grads, jnp.concatenate([q, b * k], axis=0), 0, 0)
        dks.append(dk + stays * mm(fresh, dstates[c], 1, 1) + b * z)
        dvs.append(b * e)
        drates.append(jnp.sum(e * v + k * z, axis=-1, keepdims=True))
    dq = jnp.concatenate(dqs, axis=0)
    dk = jnp.concatenate(dks, axis=0)
    dv = jnp.concatenate(dvs, axis=0)
    drate = jnp.concatenate(drates, axis=0)
    grate_ref[0, 0] = drate * valid * sig_rate * (1.0 - sig_rate)
    dacts = [
        rq * dq - acts[0] * (rq * rq * rq * jnp.sum(dq * acts[0], axis=-1, keepdims=True)),
        rk * dk - acts[1] * (rk * rk * rk * jnp.sum(dk * acts[1], axis=-1, keepdims=True)),
        dv,
    ]
    for member, out in enumerate((gq_ref, gk_ref, gv_ref)):
        sg = sigs[member]
        dfilt = dacts[member] * (sg * (1.0 + filts[member] * (1.0 - sg)))
        taps = taps_ref[member].astype(F32)
        total = None
        pieces = []
        for lag in range(CONV):
            masked = dfilt if lag == 0 else dfilt * masks[lag]
            pieces.append(jnp.sum(masked * lagged(projs[member], lag, rows), axis=0, keepdims=True))
            scaled = masked * taps[lag : lag + 1, :]
            ext = jnp.concatenate([jnp.zeros((RIM, HEAD_DIM), F32), scaled], axis=0)
            if lag:
                ext = pltpu.roll(ext, rows + RIM - lag, 0)
            total = ext if total is None else total + ext
        here = total[RIM:]
        out[0] = here.astype(BF16)
        tail_ref[0, member] = here[rows - RIM :]
        rim_ref[0, member] = total[:RIM]
        lanes = pl.ds(pl.multiple_of(head * HEAD_DIM, HEAD_DIM), HEAD_DIM)
        gtaps_ref[member, :, lanes] += jnp.concatenate(pieces, axis=0)

    @pl.when(grid_step == 0)
    def _():
        for m in late:
            rounds.turn(m, n)

    @pl.when(grid_step == count * heads - 1)
    def _():
        rounds.sent(count)


def mix_grad(
    offsets, lengths, base, proj3, rates, taps, start, m, inv, wr, up,
    grad_attn, mixer_weights, mixed, out_gain, ps, phi, trans, back_x, back_y, shards,
):
    count, heads, rows, _ = ps.shape
    ext_rows = rows + HALO
    width = mixer_weights.shape[1]
    head_width = mixer_weights.shape[2]
    flat = (count * heads, HEAD_DIM, HEAD_DIM)
    per_head = pl.BlockSpec((1, 1, rows, HEAD_DIM), lambda m, h: (m, h, 0, 0))
    proj_spec = pl.BlockSpec((1, ext_rows, HEAD_DIM), lambda m, h: (m, 0, h))
    out_spec = pl.BlockSpec((1, rows, HEAD_DIM), lambda m, h: (m, 0, h))
    rate_spec = pl.BlockSpec((1, 1, rows, 1), lambda m, h: (m, h, 0, 0))
    small = pl.BlockSpec((1, 3, RIM, HEAD_DIM), lambda m, h: (m, 0, 0, h))
    small_shape = jax.ShapeDtypeStruct((count, 3, RIM, head_width), F32)
    return pl.pallas_call(
        functools.partial(mix_grad_body, shards, count, heads),
        grid=(count, heads),
        in_specs=[
            smem_spec(), smem_spec(), smem_spec(),
            proj_spec, proj_spec, proj_spec, rate_spec,
            pl.BlockSpec((3, CONV, HEAD_DIM), lambda m, h: (0, 0, h)),
        ]
        + [per_head] * 5
        + vmem_specs(1)
        + [pl.BlockSpec((1, width, head_width), lambda m, h: (3, 0, 0))]
        + vmem_specs(7),
        out_specs=[out_spec] * 3 + [small, small, rate_spec] + vmem_specs(2),
        out_shape=[jax.ShapeDtypeStruct((count, rows, head_width), BF16)] * 3
        + [
            small_shape, small_shape,
            jax.ShapeDtypeStruct(rates.shape, F32),
            jax.ShapeDtypeStruct(taps.shape, F32),
            jax.ShapeDtypeStruct((1, HEAD_DIM), F32),
        ],
        scratch_shapes=[
            pltpu.VMEM(flat, BF16),
            pltpu.VMEM(flat, F32),
            pltpu.VMEM((count * heads, rows, HEAD_DIM), BF16),
        ]
        + compose_back_scratch(shards, count, flat),
        compiler_params=params(2, 5),
        cost_estimate=cost(45),
        name="mix_grad",
    )(
        offsets, lengths, base, *proj3, rates, taps, start, m, inv, wr, up,
        grad_attn, mixer_weights, mixed, out_gain, ps, phi, trans, back_x, back_y,
    )


def rms(values, gain):
    return values * lax.rsqrt(jnp.mean(values * values, axis=-1, keepdims=True) + EPS) * gain


def rms_back(grad, values, gain):
    inv = lax.rsqrt(jnp.mean(values * values, axis=-1, keepdims=True) + EPS)
    weighted = grad * gain
    grad_in = inv * weighted - values * inv**3 * jnp.mean(weighted * values, axis=-1, keepdims=True)
    return grad_in, jnp.sum(grad * values * inv, axis=0, keepdims=True)

def vmem_specs(count):
    return [pl.BlockSpec(memory_space=pltpu.VMEM)] * count


def comm_params(collective):
    return pltpu.CompilerParams(
        collective_id=collective, has_side_effects=True, vmem_limit_bytes=VMEM_LIMIT
    )


def dense_block_body(
    shards, extra, part_ref, x_ref, top_ref, all_top_ref, gain_ref, w_ref, own_ref,
    resid_ref, down_ref, grad_ref, mid_ref, out_ref, gain_grad_ref,
    wt_ref, wsem, acc_ref, in_ref, gin_ref, *scratch,
):
    count, local, width = x_ref.shape
    groups = w_ref.shape[0]
    cut = width // groups
    ready = 2 if extra else 3
    pieces = Pieces(count, local)
    line = None
    if extra:
        line = LineGather(
            shards, own_ref, lambda i, q: wt_ref.at[i, :, pl.ds(pl.multiple_of(q * cut, cut), cut)], *scratch[14:]
        )
    first = HeadScatter(pieces, part_ref, False, *scratch[:5])
    spread = HeadGather(pieces, in_ref, True, 0, *scratch[5:7])
    second = HeadScatter(pieces, gin_ref, True, *scratch[7:12])
    back = HeadGather(pieces, out_ref, False, 0, *scratch[12:14])

    def weights(p):
        return pltpu.make_async_copy(w_ref.at[p, 0:ready], wt_ref.at[0:ready, :, pl.ds(p * cut, cut)], wsem.at[p])

    peers = line.peers() if extra else []
    for p in range(groups):
        weights(p).start()
    greet([(pieces.seq, pieces.far), (pieces.seq, pieces.near)] + peers, 2 + len(peers))
    n = pieces.total
    each(n, first.start)
    if extra:
        line.start(2)
    each(n, first.forward)
    gain_grad_ref[...] = jnp.zeros_like(gain_grad_ref)

    @pl.loop(0, n)
    def _(k):
        m, here = pieces.mine(k)
        resid = x_ref[m, here, :].astype(F32) + first.total(k)
        resid_ref[m, here, :] = resid
        spread.place(k, pieces.head)[...] = rms(resid, gain_ref[...]).astype(BF16)
        spread.own(k)

    for p in range(groups):
        weights(p).wait()

    def turn_back(k):
        m, here = pieces.mine(k)
        grad, gain_part = rms_back(second.total(k), resid_ref[m, here, :], gain_ref[...])
        mid = top_ref[m, here, :].astype(F32) + grad
        gain_grad_ref[...] += gain_part
        mid_ref[m, here, :] = mid
        back.place(k, pieces.head)[...] = mid.astype(BF16)
        back.own(k)

    spread.forward(0)
    if extra:
        line.forward(2)

    @pl.loop(0, n)
    def _(k):
        if not extra:
            grad_hidden = mm(all_top_ref[k], wt_ref[2], 1, 1)
        spread.arrived(k)
        x = in_ref[k]
        gate = mm(x, wt_ref[0], 1, 1)
        up = mm(x, wt_ref[1], 1, 1)
        if extra:

            @pl.when(k == 0)
            def _():
                line.arrived(2)

        if extra:
            grad_hidden = mm(all_top_ref[k], wt_ref[2], 1, 1)
        sg = sigmoid(gate)
        silu = gate * sg
        hidden = (silu * up).astype(BF16)
        grad_gate = (grad_hidden * up * (sg * (1.0 + gate * (1.0 - sg)))).astype(BF16)
        grad_up = (grad_hidden * silu).astype(BF16)
        gin_ref[k] = (mm(grad_gate, wt_ref[0]) + mm(grad_up, wt_ref[1])).astype(BF16)
        second.start(k)

        @pl.when(k + 1 < n)
        def _():
            spread.forward(k + 1)

        down_ref[k] = mm(hidden, wt_ref[2]).astype(BF16)
        second.forward(k)
        adds = (mm(grad_gate, x, 0, 0), mm(grad_up, x, 0, 0), mm(hidden, all_top_ref[k], 0, 0))

        @pl.when(k == 0)
        def _():
            for i, add in enumerate(adds):
                acc_ref[i] = add

        @pl.when(jnp.logical_and(k > 0, k + 1 < n))
        def _():
            for i, add in enumerate(adds):
                acc_ref[i] += add

        @pl.when(k + 1 == n)
        def _():
            for i, add in enumerate(adds):
                total = (acc_ref[i] + add).astype(BF16)
                for p in range(groups):
                    grad_ref[p, i] = total[:, p * cut : (p + 1) * cut]

        @pl.when(k > 0)
        def _():
            turn_back(k - 1)

        @pl.when(k > 1)
        def _():
            back.forward(k - 2)

    turn_back(n - 1)
    back.forward(n - 2)
    back.forward(n - 1)
    each(n, back.arrived, back.sent, second.sent, spread.sent, first.sent)
    if extra:
        line.sent(2)


def dense_block(part, inputs, top, all_top, gain, weights, own, shards, extra):
    count, local, width = inputs.shape
    groups, _, hidden, cut = weights.shape
    n = count * local // PIECE
    tile = all_top.shape[1]
    rows = part.shape[1]
    return pl.pallas_call(
        functools.partial(dense_block_body, shards, extra),
        in_specs=vmem_specs(5) + [any_spec()] * 2,
        out_specs=vmem_specs(6),
        out_shape=[
            jax.ShapeDtypeStruct(inputs.shape, F32),
            jax.ShapeDtypeStruct((n, tile, width), BF16),
            jax.ShapeDtypeStruct((groups, 3, hidden, cut), BF16),
            jax.ShapeDtypeStruct(inputs.shape, F32),
            jax.ShapeDtypeStruct((count, rows, width), BF16),
            jax.ShapeDtypeStruct((1, width), F32),
        ],
        scratch_shapes=[
            pltpu.VMEM((3, hidden, width), BF16),
            pltpu.SemaphoreType.DMA((groups,)),
            pltpu.VMEM((3, hidden, width), F32),
            pltpu.VMEM((n, tile, width), BF16),
            pltpu.VMEM((n, tile, width), BF16),
        ]
        + (scatter_scratch(count, local, width) + gather_scratch(count, local)) * 2
        + (line_scratch(shards) if extra else []),
        compiler_params=comm_params(1),
        cost_estimate=cost(55),
        name="dense_block",
    )(part, inputs, top, all_top, gain, weights, own)


class SeqSum:
    def __init__(self, shards, part_ref, work_ref, got_ref, full_ref, send, recv):
        self.part, self.work, self.got, self.full = part_ref, work_ref, got_ref, full_ref
        self.send, self.recv = send, recv
        self.seq, self.head = lax.axis_index("seq"), lax.axis_index("head")
        self.bits = [1 << k for k in range((shards - 1).bit_length())]
        self.members, self.rows = part_ref.shape[0], part_ref.shape[1] // 2
        self.half = 128
        self.chunks = 2 * self.members * (part_ref.shape[2] // self.half)
        self.steps = 2 * len(self.bits)
        self.order = [self.members - 1, *range(self.members - 1)]
        self.copies = {}
        self.kept, self.gone = [0], []
        size = self.rows
        for bit in self.bits:
            size //= 2
            mine = self.seq // bit % 2
            self.gone.append(self.kept[-1] + size * (1 - mine))
            self.kept.append(self.kept[-1] + size * mine)

    def view(self, ref, chunk, first, size):
        per = self.chunks // self.members
        first = pl.multiple_of(chunk % 2 * self.rows + first, 8)
        return ref.at[self.order[chunk // per], pl.ds(first, size), pl.ds(chunk % per // 2 * self.half, self.half)]

    def begin(self, chunk, step):
        size = self.rows >> (step + 1)
        src = self.view(self.part if step == 0 else self.work, chunk, self.gone[step], size)
        offset = self.rows - 2 * size
        dst = self.view(self.got, chunk, offset, size)
        c = remote(src, dst, self.send.at[step, chunk], self.recv.at[step, chunk], flip(self.seq, self.bits[step]), self.head)
        c.start()
        self.copies[step, chunk] = c

    def fold(self, chunk, step):
        size = self.rows >> (step + 1)
        self.copies[step, chunk].wait_recv()
        got = self.view(self.got, chunk, self.rows - 2 * size, size)
        kept = self.view(self.part if step == 0 else self.work, chunk, self.kept[step + 1], size)
        total = (kept[...].astype(F32) + got[...].astype(F32)).astype(BF16)
        last = step == len(self.bits) - 1
        self.view(self.full if last else self.work, chunk, self.kept[step + 1], size)[...] = total

    def spread(self, chunk, step):
        back = len(self.bits) - 1 - step
        size = self.rows >> (back + 1)
        ref = self.view(self.full, chunk, self.kept[back + 1], size)
        at = len(self.bits) + step
        c = remote(ref, ref, self.send.at[at, chunk], self.recv.at[at, chunk], flip(self.seq, self.bits[back]), self.head)
        c.start()
        self.copies[at, chunk] = c

    def stage(self, chunk, step):
        n = len(self.bits)
        if step > n:
            self.copies[step - 1, chunk].wait_recv()
        elif step > 0:
            self.fold(chunk, step - 1)
        if step < n:
            self.begin(chunk, step)
        elif step < 2 * n:
            self.spread(chunk, step - n)

    def tick(self, t):
        done = []
        for chunk in range(self.chunks):
            step, odd = divmod(t - chunk, 2)
            if not odd and 0 <= step <= self.steps:
                self.stage(chunk, step)
                if step == self.steps:
                    done.append(chunk)
        return done

    def ticks(self):
        return self.chunks + 2 * self.steps

    def finish(self):
        for c in self.copies.values():
            c.wait_send()


def finish_body(
    shards, gq_ref, gk_ref, gv_ref, tail_ref, rim_ref, grate_ref, all_x_ref, w_ref, beta_ref, gattn_ref, head_ref,
    down_ref, taps_ref, dense_part_ref, out_part_ref, x_ref, mid_ref, resid_ref, gain_ref,
    in_grad_ref, output_ref, total_ref, rows_ref, filter_ref,
    gx_ref, mixer_ref, g_ref, rim_got, rim_send, rim_recv, *scratch,
):
    gx_scratch, down_scratch = scratch[:5], scratch[5:10]
    work_ref, got_ref, full_ref, ms, mr, row_got, row_now, tap_got, tap_now, rs, rr, gain_grad_ref = scratch[10:]
    count, local, width = x_ref.shape
    heads = beta_ref.shape[0]
    members = taps_ref.shape[0]
    rows = gq_ref.shape[1]
    pieces = Pieces(count, local)
    gx = HeadScatter(pieces, gx_ref, False, *gx_scratch)
    down = HeadScatter(pieces, down_ref, True, *down_scratch)
    total = SeqSum(shards, mixer_ref, work_ref, got_ref, full_ref, ms, mr)
    seq, head = pieces.seq, pieces.head

    row_now[0] = jnp.zeros(row_now.shape[1:], F32)
    tap_now[0] = jnp.zeros(tap_now.shape[1:], F32)
    row_now[0, heads : heads + 1, :] = dense_part_ref[...]
    row_now[0, heads + 1 : heads + 2, 0:HEAD_DIM] = out_part_ref[...]
    for k in range(members):
        tap_now[0, 8 * k : 8 * k + CONV, :] = taps_ref[k]
    rounds = [(flip(seq, bit), head) for bit in total.bits] + [(seq, flip(head, 2)), (seq, flip(head, 1))]
    before = lax.rem(seq + shards - 1, shards)
    after = lax.rem(seq + 1, shards)
    greet(rounds + [(after, head)], len(rounds) + 1)
    rim = remote(rim_ref, rim_got, rim_send, rim_recv, before, head)
    rim.start()
    small = {}

    def grates(m):
        lane = lax.broadcasted_iota(jnp.int32, (rows, heads), 1)
        out = jnp.zeros((rows, heads), F32)
        for h in range(heads):
            out = jnp.where(lane == h, grate_ref[m, h], out)
        return out

    def weight_grad(member):
        total = None
        for m in range(count):
            left, right = (gattn_ref[m], head_ref[m]) if member == members else (all_x_ref[m, HALO:, :], g_ref[member, m])
            add = mm(left, right, 0, 0)
            total = add if total is None else total + add
        mixer_ref[member] = total.astype(BF16)

    def join_rims():
        rim.wait_recv()
        for member, ref in enumerate((gq_ref, gk_ref, gv_ref)):
            for m in range(count):
                g_ref[member, m, 0 : rows - 2 * RIM, :] = ref[m, 0 : rows - 2 * RIM, :]
                last = (tail_ref[m, member] + rim_got[m, member]).astype(BF16)
                g_ref[member, m, rows - 2 * RIM :, :] = jnp.concatenate([ref[m, rows - 2 * RIM : rows - RIM, :], last], axis=0)

    def row_grad(m):
        total = mm(grates(m), beta_ref[...])
        for member in range(members):
            total += mm(g_ref[member, m], w_ref[member], 1, 1)
        gx_ref[m] = total.astype(BF16)
        for k in range(m * pieces.per, (m + 1) * pieces.per):
            gx.start(k)

    def beta_grad():
        total = None
        for m in range(count):
            add = mm(grates(m), all_x_ref[m, HALO:, :], 0, 0)
            total = add if total is None else total + add
        row_now[0, 0:heads, :] = total

    def small_start(k):
        small[k] = [
            remote(row_now.at[k], row_got.at[k], rs.at[0, k], rr.at[0, k], *rounds[k]),
            remote(tap_now.at[k], tap_got.at[k], rs.at[1, k], rr.at[1, k], *rounds[k]),
        ]
        for c in small[k]:
            c.start()

    def small_end(k):
        for c in small[k]:
            c.wait_recv()
        row_now[k + 1] = row_now[k] + row_got[k]
        tap_now[k + 1] = tap_now[k] + tap_got[k]

    n = pieces.total
    gain_grad_ref[...] = jnp.zeros_like(gain_grad_ref)

    def gx_end(k):
        m, here = pieces.mine(k)
        grad, gain_part = rms_back(gx.total(k), x_ref[m, here, :].astype(F32), gain_ref[...])
        gain_grad_ref[...] += gain_part
        in_grad_ref[m, here, :] = mid_ref[m, here, :] + grad
        down.forward(k)

    def down_end(k):
        m, here = pieces.mine(k)
        output_ref[m, here, :] = (resid_ref[m, here, :] + down.total(k)).astype(BF16)

    def small_turn(k):
        if k == 0:
            row_now[0, heads + 2 : heads + 3, :] = gain_grad_ref[...]
        else:
            small_end(k - 1)
        if k < len(rounds):
            small_start(k)

    def weight_ready(chunk):
        per = total.chunks // total.members
        if chunk < total.chunks and chunk % per == 0:
            weight_grad(total.order[chunk // per])

    aside = [(1, join_rims), (1, functools.partial(row_grad, 0))]
    aside += [(2, functools.partial(row_grad, m)) for m in range(1, count)]
    aside += [(3, lambda: each(n, gx.forward, down.start)), (4, beta_grad)]
    aside += [(n + 2 + 2 * k, functools.partial(gx_end, k)) for k in range(n)]
    first = 3 * n + 2
    for k in range(max(len(rounds) + 1, n)):
        if k <= len(rounds):
            aside.append((first + 2 * k, functools.partial(small_turn, k)))
        if k < n:
            aside.append((first + 2 * k + 1, functools.partial(down_end, k)))
    weight_ready(0)
    for t in range(total.ticks()):
        for chunk in total.tick(t):
            whole = total.view(full_ref, chunk, 0, total.rows)
            total.view(total_ref, chunk, 0, total.rows)[...] = whole[...].astype(F32)
        while aside and aside[0][0] <= t:
            aside.pop(0)[1]()
        weight_ready(t + 1)
    for _, act in aside:
        act()
    k = len(total.bits)
    rows_ref[0] = row_now[k]
    rows_ref[1] = row_now[len(rounds)]
    for member in range(members):
        filter_ref[member] = tap_now[k, 8 * member : 8 * member + CONV, :]
    for group in small.values():
        for c in group:
            c.wait_send()
    each(pieces.total, gx.sent, down.sent)
    total.finish()
    rim.wait_send()


def finish(
    g3, tail, rim, grate, all_x, mixer_weights, beta_rows, grad_attn, head_out,
    down_part, taps_part, dense_part, out_part, inputs, mid, resid, gain, shards,
):
    count, local, width = inputs.shape
    members, _, head_width = mixer_weights.shape
    rows = g3[0].shape[1]
    bits = (shards - 1).bit_length()
    rounds = bits + 2
    chunks = 2 * members * head_width // 128
    whole = pltpu.VMEM(mixer_weights.shape, BF16)
    return pl.pallas_call(
        functools.partial(finish_body, shards),
        in_specs=vmem_specs(19),
        out_specs=vmem_specs(5),
        out_shape=[
            jax.ShapeDtypeStruct(inputs.shape, F32),
            jax.ShapeDtypeStruct(inputs.shape, BF16),
            jax.ShapeDtypeStruct(mixer_weights.shape, F32),
            jax.ShapeDtypeStruct((2, 8, width), F32),
            jax.ShapeDtypeStruct(taps_part.shape, F32),
        ],
        scratch_shapes=[
            pltpu.VMEM((count, rows, width), BF16),
            whole,
            pltpu.VMEM((3, count, rows, head_width), BF16),
            pltpu.VMEM(rim.shape, F32),
            pltpu.SemaphoreType.DMA,
            pltpu.SemaphoreType.DMA,
        ]
        + scatter_scratch(count, local, width) * 2
        + [
            whole, whole, whole,
            pltpu.SemaphoreType.DMA((2 * bits, chunks)),
            pltpu.SemaphoreType.DMA((2 * bits, chunks)),
            pltpu.VMEM((rounds, 8, width), F32),
            pltpu.VMEM((rounds + 1, 8, width), F32),
            pltpu.VMEM((rounds, 24, head_width), F32),
            pltpu.VMEM((rounds + 1, 24, head_width), F32),
            pltpu.SemaphoreType.DMA((2, rounds)),
            pltpu.SemaphoreType.DMA((2, rounds)),
            pltpu.VMEM((1, width), F32),
        ],
        compiler_params=comm_params(3),
        cost_estimate=cost(75),
        name="finish",
    )(
        *g3, tail, rim, grate, all_x, mixer_weights, beta_rows, grad_attn, head_out,
        down_part, taps_part, dense_part, out_part, inputs, mid, resid, gain,
    )


def regroup(blocks, count):
    if blocks.shape[0] == count:
        return blocks
    _, members, hidden, _ = blocks.shape
    whole = blocks.transpose(1, 2, 0, 3).reshape(members, hidden, count, -1)
    return whole.transpose(2, 0, 1, 3)


def per_device(
    inputs, attn_gain, mixer_weights, beta_weight, filter_weights, out_gain, dense_gain, dense_weights,
    seq_offsets, seq_lengths, out_grad,
):
    count, local_rows, width = inputs.shape
    heads, shards = lax.axis_size("head"), lax.axis_size("seq")
    base = (lax.axis_index("seq") * local_rows * heads).astype(jnp.int32).reshape(1)
    taps = filter_weights
    beta_rows = beta_weight.T
    gain_row = out_gain.reshape(1, HEAD_DIM)
    attn_row = attn_gain.reshape(1, width)
    dense_row = dense_gain.reshape(1, width)
    weights_t = jnp.swapaxes(dense_weights, 1, 2)
    extra = False
    pq, pk, pv, rates, ps, oloc, phi, psi, score, inv, wr, up, trans, enter, back_x, back_y, x_ext, grad_top, *full = mix_fwd(
        seq_offsets, seq_lengths, base, mixer_weights, beta_rows, taps, inputs, attn_row, out_grad, weights_t, shards, extra
    )
    dense_full = full[0] if extra else regroup(lax.all_gather(weights_t, "seq", axis=0), width // 128)
    state_in = enter.reshape((count, -1) + enter.shape[1:])
    start, mixed, head_out, attn_part = mix_out(state_in, ps, oloc, phi, psi, gain_row, mixer_weights)
    resid_mid, down_part, dense_part, grad_mid, grad_attn, dense_gain_part = dense_block(
        attn_part, inputs, out_grad, grad_top, dense_row, dense_full, weights_t, shards, extra
    )
    dense_mine = lax.psum_scatter(regroup(dense_part, shards), "seq", scatter_dimension=0, tiled=True)
    dense_total = jnp.swapaxes(dense_mine[0], 1, 2).astype(F32)
    gq, gk, gv, tail, rim, grate, filter_part, out_gain_part = mix_grad(
        seq_offsets, seq_lengths, base, (pq, pk, pv), rates, taps, start, score, inv, wr, up,
        grad_attn, mixer_weights, mixed, gain_row, ps, phi, trans, back_x, back_y, shards,
    )
    input_grad, output, mixer_total, rows_total, filter_total = finish(
        (gq, gk, gv), tail, rim, grate, x_ext, mixer_weights, beta_rows, grad_attn, head_out,
        down_part, filter_part, dense_gain_part, out_gain_part, inputs, grad_mid, resid_mid, attn_row, shards,
    )
    local_heads = beta_rows.shape[0]
    beta_total = rows_total[0, :local_heads].T
    dense_gain_total = rows_total[1, local_heads]
    out_gain_total = rows_total[1, local_heads + 1, :HEAD_DIM]
    attn_gain_total = rows_total[1, local_heads + 2]
    return (
        output, input_grad, attn_gain_total, mixer_total, beta_total, filter_total, out_gain_total,
        dense_gain_total, dense_total,
    )


def solution(mesh):
    rows = P(None, ("seq", "head"), None)
    return jax.shard_map(
        per_device,
        mesh=mesh,
        in_specs=(
            rows, P(), P(None, None, "head"), P(None, "head"), P(None, None, "head"), P(), P(),
            P(None, "seq", "head"), P(), P(), rows,
        ),
        out_specs=(
            rows, rows, P(), P(None, None, "head"), P(None, "head"), P(None, None, "head"), P(), P(),
            P(None, "seq", "head"),
        ),
        check_vma=False,
    )
```
